128 devices in a mesh: grp: 8 (over x, core), inner: 16 (over z, y).
Axes of the slice: x: 4, y: 4, z: 4, core: 2. Of those that a mesh axis runs over, the one named last changes fastest.
Arguments:
- moe_input: bfloat16 [16384, 2048], P(('grp', 'inner')), may hold values from -6 to 6
- out_grad: bfloat16 [16384, 2048], P(('grp', 'inner')), may hold values from -1.5 to 1.5
- context: bfloat16 [16384, 4096], P('grp', 'inner'), may hold values from -0.119628906 to 0.119628906
- gate_scale: float32 [128, 256], P(('grp', 'inner')), may hold values from 0.2 to 1
- selected: int32 [128, 256], replicated, may hold values from 0 to 16383, as said below
- w_gate: bfloat16 [128, 2048, 768], P(('grp', 'inner')), may hold values from -0.125 to 0.125
- w_up: bfloat16 [128, 2048, 768], P(('grp', 'inner')), may hold values from -0.125 to 0.125
- w_down: bfloat16 [128, 768, 2048], P(('grp', 'inner')), may hold values from -0.21875 to 0.21875
- w_out: bfloat16 [4096, 2048], P('inner'), may hold values from -0.09375 to 0.09375
Outputs:
- grad_gate: bfloat16 [128, 2048, 768], P(('grp', 'inner'))
- grad_up: bfloat16 [128, 2048, 768], P(('grp', 'inner'))
- grad_down: bfloat16 [128, 768, 2048], P(('grp', 'inner'))
- grad_context: bfloat16 [16384, 4096], P('grp', 'inner')
- grad_out: bfloat16 [4096, 2048], P('inner', 'grp')
The draws below stay inside these ranges and needn't reach their ends.
Inputs may be any that keep to these rules, and one draw needn't show every extreme that they name: `selected`: each expert's 256 token indices are distinct; at most 4 of them lie among the 128 tokens of one device (tokens d * 128 to (d + 1) * 128 - 1), and every expert takes exactly 4 from some device.
All inputs are finite; a program needn't handle non-finite values.
Results may differ from the reference program's by a relative error of at most 0.014.
Values may be sent and summed in bfloat16 or wider, within the bound.
No kernel may reach another device: no remote copies, remote signals or barrier semaphores. Data moves between devices by JAX's collectives and lax.ppermute only.
A program may use at most 128 MiB of HBM per device.

```python
import math
import jax
import jax.numpy as jnp
from jax import lax

D = 2048
FF = 768
TOK_DEV = 128
CAP = 256
EXPERTS = 128
TOKENS = 16384
QDIM = 4096
MOST = 4


def draw_selected(key, part):
    devices = TOKENS // TOK_DEV
    items = devices * MOST
    first, second, third, fourth = jax.random.split(key, 4)
    item_ids = jnp.arange(items, dtype=jnp.int32)
    source_of = item_ids // MOST
    scores = jax.random.randint(first, (EXPERTS, items), 0, 1048576, dtype=jnp.int32) * items + item_ids[None, :]
    forced = jax.random.randint(second, (EXPERTS, 1), 0, devices, dtype=jnp.int32)
    favour = jax.random.randint(fourth, (devices,), 0, 4, dtype=jnp.int32) * 134217728
    scores = scores + jnp.where(source_of[None, :] == forced, 1073741824, 0) + favour[source_of][None, :]
    unused, chosen = lax.top_k(scores, CAP)
    source = chosen // MOST
    within = chosen % MOST
    base = jax.random.randint(third, (EXPERTS, devices), 0, TOK_DEV, dtype=jnp.int32)
    stride = TOK_DEV // MOST
    start = jnp.take_along_axis(base, source, axis=1)
    offset = (start + within * stride) % TOK_DEV
    return (source * TOK_DEV + offset).astype(jnp.int32)


def shard_levels(own_key, dims, pieces, least, largest):
    gain, own = 1.0, jax.random.fold_in(own_key, 6)
    for dim, blocks in pieces:
        heights = jnp.exp(jax.random.uniform(jax.random.fold_in(own, dim), (blocks,), jnp.float32, least / len(pieces), largest / len(pieces)))
        gain = gain * jnp.repeat(heights, dims[dim] // blocks).reshape([-1 if axis == dim else 1 for axis in range(len(dims))])
    return gain


def bell_draw(key, extent, scale, most, shards=(), held_as=jnp.bfloat16):
    gain = shard_levels(key, extent, shards, -0.22, 0.18) if shards else 1.0
    array = jax.random.normal(key, extent, jnp.float32) * scale * gain
    return jnp.minimum(jnp.maximum(array, -most), most).astype(held_as)


def setup_inputs(seed: int = 0) -> dict:
    key_list = jax.random.split(jax.random.key(seed), 10)
    return {
        "moe_input": bell_draw(key_list[0], (TOKENS, D), 1.0, 6.0, ((0, 128),)),
        "out_grad": bell_draw(key_list[1], (TOKENS, D), 0.25, 1.5, ((0, 128),)),
        "context": bell_draw(key_list[2], (TOKENS, QDIM), 0.02, 0.119628906, ((0, 8), (1, 16))),
        "gate_scale": jnp.clip(jnp.exp(math.log(1.0) - 1.609438 * jax.random.uniform(key_list[3], (EXPERTS, CAP), jnp.float32) ** shard_levels(key_list[3], (EXPERTS, CAP), ((0, 128),), -0.2, 0.2)), 0.2, 1.0),
        "selected": draw_selected(jax.random.fold_in(key_list[9], 71), 0),
        "w_gate": bell_draw(key_list[5], (EXPERTS, D, FF), D ** -0.5, 0.125, ((0, 128),)),
        "w_up": bell_draw(key_list[6], (EXPERTS, D, FF), D ** -0.5, 0.125, ((0, 128),)),
        "w_down": bell_draw(key_list[7], (EXPERTS, FF, D), FF ** -0.5, 0.21875, ((0, 128),)),
        "w_out": bell_draw(key_list[8], (QDIM, D), QDIM ** -0.5, 0.09375, ((0, 16),)),
    }


def expert_backward(rows_in, rows_grad, scales, gate_w, up_w, down_w):
    gate_pre = jnp.dot(rows_in, gate_w, preferred_element_type=jnp.float32)
    up_pre = jnp.dot(rows_in, up_w, preferred_element_type=jnp.float32)
    sig = jax.nn.sigmoid(gate_pre)
    silu = gate_pre * sig
    hidden = (silu * up_pre).astype(jnp.bfloat16)
    scaled = (rows_grad.astype(jnp.float32) * scales[:, None]).astype(jnp.bfloat16)
    outer = (((0,), (0,)), ((), ()))
    inner_dims = (((1,), (1,)), ((), ()))
    grad_down = lax.dot_general(hidden, scaled, outer, preferred_element_type=jnp.float32).astype(jnp.bfloat16)
    back_hidden = lax.dot_general(scaled, down_w, inner_dims, preferred_element_type=jnp.float32)
    back_gate = (back_hidden * up_pre * sig * (1.0 + gate_pre * (1.0 - sig))).astype(jnp.bfloat16)
    back_up = (back_hidden * silu).astype(jnp.bfloat16)
    grad_gate = lax.dot_general(rows_in, back_gate, outer, preferred_element_type=jnp.float32).astype(jnp.bfloat16)
    grad_up = lax.dot_general(rows_in, back_up, outer, preferred_element_type=jnp.float32).astype(jnp.bfloat16)
    row_grad = lax.dot_general(back_gate, gate_w, inner_dims, preferred_element_type=jnp.float32)
    row_grad = row_grad + lax.dot_general(back_up, up_w, inner_dims, preferred_element_type=jnp.float32)
    return grad_gate, grad_up, grad_down, row_grad.astype(jnp.bfloat16)


def reference(moe_input, out_grad, context, gate_scale, selected, w_gate, w_up, w_down, w_out):
    def per_expert(packed):
        rows, scales, gate_w, up_w, down_w = packed
        return expert_backward(moe_input[rows], out_grad[rows], scales, gate_w, up_w, down_w)

    grad_gate, grad_up, grad_down, row_grad = lax.map(per_expert, (selected, gate_scale, w_gate, w_up, w_down))
    row_grad = lax.optimization_barrier(row_grad)
    moe_back = jax.ops.segment_sum(row_grad.reshape(-1, D).astype(jnp.float32), selected.reshape(-1).astype(jnp.int32), num_segments=TOKENS)
    total = (out_grad.astype(jnp.float32) + moe_back).astype(jnp.bfloat16)
    grad_context = lax.dot_general(total, w_out, (((1,), (1,)), ((), ())), preferred_element_type=jnp.float32).astype(jnp.bfloat16)
    grad_out = lax.dot_general(context, total, (((0,), (0,)), ((), ())), preferred_element_type=jnp.float32).astype(jnp.bfloat16)
    return grad_gate, grad_up, grad_down, grad_context, grad_out
```

```python
import jax
import jax.numpy as jnp
from jax import lax
from jax.experimental import pallas as pl
from jax.experimental.pallas import tpu as pltpu
from jax.sharding import PartitionSpec as P

F32 = jnp.float32
BF16 = jnp.bfloat16
ROWS = (((0,), (0,)), ((), ()))
LAST = (((1,), (1,)), ((), ()))
SIDE = 4


def dot(left, right, dims=(((1,), (0,)), ((), ()))):
    return lax.dot_general(left, right, dims, preferred_element_type=F32)


def ring_pairs(step, along_z):
    pairs = []
    for z in range(SIDE):
        for y in range(SIDE):
            to = ((z + step) % SIDE) * SIDE + y if along_z else z * SIDE + (y + step) % SIDE
            pairs.append((z * SIDE + y, to))
    return pairs


def ring_gather(block, along_z):
    return [lax.ppermute(block, "inner", ring_pairs(-step, along_z)) for step in (1, 2, 3)]


def join_kernel(*refs):
    for path in range(2):
        out = refs[8 + path]
        rows = out.shape[0] // SIDE
        for k in range(SIDE):
            out[k * rows : (k + 1) * rows, :] = refs[path * SIDE + k][...]


def join(first, second):
    rows, cols = first[0].shape
    out = jax.ShapeDtypeStruct((SIDE * rows, cols), BF16)
    moved = 4 * SIDE * rows * cols * 2
    return pl.pallas_call(
        join_kernel,
        out_shape=(out, out),
        cost_estimate=pl.CostEstimate(flops=0, bytes_accessed=moved, transcendentals=0),
    )(*first, *second)


def proj_kernel(table, context, *refs):
    arrays, out, ctx_a, ctx_b = refs[:8], refs[8], refs[9], refs[10]
    block = pl.program_id(0)
    rows = context.shape[0] // 16

    @pl.when(block == 0)
    def _():
        for major in range(SIDE):
            for minor in range(SIDE):
                at = (major * SIDE + minor) * rows
                src_a = pl.multiple_of(table[major * SIDE + minor] * rows, rows)
                src_b = pl.multiple_of(table[minor * SIDE + major] * rows, rows)
                ctx_a[at : at + rows, :] = context[pl.ds(src_a, rows), :]
                ctx_b[at : at + rows, :] = context[pl.ds(src_b, rows), :]

    def part(ctx, pieces):
        total = None
        depth = SIDE * rows
        for k in range(SIDE):
            term = dot(ctx[k * depth : (k + 1) * depth, :], pieces[k][...], ROWS)
            total = term if total is None else total + term
        out[0] = total.astype(BF16)

    @pl.when(block < 4)
    def _():
        part(ctx_a, arrays[:4])

    @pl.when(block >= 4)
    def _():
        part(ctx_b, arrays[4:])


def proj(table, context, arrays_a, arrays_b, groups):
    tokens, heads = context.shape
    depth, cols = arrays_a[0].shape
    wide = 2 * cols // groups
    a_spec = pl.BlockSpec((depth, wide), lambda g, t: (0, jnp.minimum(g, groups // 2 - 1)))
    b_spec = pl.BlockSpec((depth, wide), lambda g, t: (0, jnp.maximum(g - groups // 2, 0)))
    return pl.pallas_call(
        proj_kernel,
        out_shape=jax.ShapeDtypeStruct((groups, heads, wide), BF16),
        grid_spec=pltpu.PrefetchScalarGridSpec(
            num_scalar_prefetch=1,
            grid=(groups,),
            in_specs=[pl.BlockSpec((tokens, heads), lambda g, t: (0, 0))]
            + [a_spec] * 4
            + [b_spec] * 4,
            out_specs=pl.BlockSpec((1, heads, wide), lambda g, t: (g, 0, 0)),
            scratch_shapes=[pltpu.VMEM((tokens, heads), BF16)] * 2,
        ),
        cost_estimate=pl.CostEstimate(
            flops=4 * tokens * heads * cols, bytes_accessed=4 * tokens * cols, transcendentals=0
        ),
    )(table, context, *arrays_a, *arrays_b)


def ctx_kernel(table, w_out, *refs):
    arrays, out = refs[:8], refs[8]
    rows = arrays[0].shape[0] // SIDE
    cols = arrays[0].shape[1]
    for dz in range(SIDE):
        for dy in range(SIDE):
            left = arrays[dz][dy * rows : (dy + 1) * rows, :]
            right = arrays[SIDE + dy][dz * rows : (dz + 1) * rows, :]
            total = dot(left, w_out[:, :cols], LAST) + dot(right, w_out[:, cols:], LAST)
            at = pl.multiple_of(table[dz * SIDE + dy] * rows, rows)
            out[pl.ds(at, rows), :] = total.astype(BF16)


def ctx_grad(table, w_out, arrays_a, arrays_b):
    heads = w_out.shape[0]
    depth, cols = arrays_a[0].shape
    tokens = SIDE * depth
    vmem = pl.BlockSpec(memory_space=pltpu.VMEM)
    return pl.pallas_call(
        ctx_kernel,
        out_shape=jax.ShapeDtypeStruct((tokens, heads), BF16),
        in_specs=[pl.BlockSpec(memory_space=pltpu.SMEM)] + [vmem] * 9,
        out_specs=vmem,
        cost_estimate=pl.CostEstimate(
            flops=4 * tokens * heads * cols, bytes_accessed=4 * tokens * cols, transcendentals=0
        ),
    )(table, w_out, *arrays_a, *arrays_b)


def body(moe_input, out_grad, context, gate_scale, selected, w_gate, w_up, w_down, w_out):
    groups = lax.axis_size("grp")
    inner_count = lax.axis_size("inner")
    devices = groups * inner_count
    tok_rows, width = moe_input.shape
    capacity = selected.shape[1]
    most = 4
    half = width // 2
    inner = lax.axis_index("inner")
    device = lax.axis_index("grp") * inner_count + inner
    both = ("grp", "inner")

    owner = selected // tok_rows
    mine = owner == device
    ordinal = jnp.cumsum(mine.astype(jnp.int32), axis=1) - 1
    slot_ids = jnp.arange(most, dtype=jnp.int32)
    match_slot = mine[:, :, None] & (ordinal[:, :, None] == slot_ids[None, None, :])
    local_token = selected - device * tok_rows
    token_table = jnp.sum(jnp.where(match_slot, local_token[:, :, None] + 1, 0), axis=1) - 1
    table8 = jnp.concatenate(
        [token_table, jnp.where(token_table >= 0, token_table + tok_rows, -1)], 1
    ).reshape(-1)
    token_ids = jnp.arange(2 * tok_rows, dtype=jnp.int32)
    picker = (table8[:, None] == token_ids[None, :]).astype(BF16)
    both_rows = jnp.concatenate([moe_input, out_grad], 0)
    sent = dot(picker, both_rows).astype(BF16).reshape(devices, 2 * most, width)
    arrived = lax.all_to_all(sent, both, split_axis=0, concat_axis=0, tiled=True)
    arrived = arrived.reshape(devices * 2 * most, width)

    my_owner = lax.dynamic_index_in_dim(owner, device, 0, keepdims=False)
    slot_range = jnp.arange(capacity, dtype=jnp.int32)
    same_owner = (my_owner[:, None] == my_owner[None, :]) & (
        slot_range[:, None] > slot_range[None, :]
    )
    ranking = jnp.sum(same_owner.astype(jnp.int32), axis=1)
    position = my_owner * (2 * most) + ranking
    spots = jnp.arange(devices * 2 * most, dtype=jnp.int32)
    place_in = (position[:, None] == spots[None, :]).astype(BF16)
    place_grad = ((position + most)[:, None] == spots[None, :]).astype(BF16)

    rows_in = dot(place_in, arrived).astype(BF16)
    rows_grad = dot(place_grad, arrived).astype(BF16)
    gate_w, up_w, down_w = w_gate[0], w_up[0], w_down[0]
    gate_pre = dot(rows_in, gate_w)
    up_pre = dot(rows_in, up_w)
    sig = jax.nn.sigmoid(gate_pre)
    silu = gate_pre * sig
    hidden = (silu * up_pre).astype(BF16)
    scaled = (rows_grad.astype(F32) * gate_scale[0][:, None]).astype(BF16)
    back_hidden = dot(scaled, down_w, LAST)
    back_gate = (back_hidden * up_pre * sig * (1.0 + gate_pre * (1.0 - sig))).astype(BF16)
    back_up = (back_hidden * silu).astype(BF16)

    halves = []
    for h in range(2):
        cols = slice(h * half, (h + 1) * half)
        part = dot(back_gate, gate_w[cols], LAST) + dot(back_up, up_w[cols], LAST)
        halves.append(part.astype(BF16))
    stacked = jnp.concatenate(halves, 0)
    half_of = jnp.arange(2 * capacity, dtype=jnp.int32) // capacity
    spot_of = jnp.tile(position, 2) + half_of * most
    unplace = (spots[:, None] == spot_of[None, :]).astype(BF16)
    placed = dot(unplace, stacked).astype(BF16).reshape(devices, 2 * most, half)
    returned = lax.all_to_all(placed, both, split_axis=0, concat_axis=0, tiled=True)

    grad_down = dot(hidden, scaled, ROWS).astype(BF16)
    grad_gate = dot(rows_in, back_gate, ROWS).astype(BF16)
    grad_up = dot(rows_in, back_up, ROWS).astype(BF16)
    returned, grad_down, grad_gate, grad_up = lax.optimization_barrier(
        (returned, grad_down, grad_gate, grad_up)
    )
    returned = returned.reshape(devices * 2 * most, half)

    none = jnp.full_like(token_table, -1)
    totals = []
    for h in range(2):
        pair = [none, none]
        pair[h] = token_table
        table = jnp.concatenate(pair, 1).reshape(-1)
        adder = (table[:, None] == token_ids[None, :tok_rows]).astype(BF16)
        own = out_grad[:, h * half : (h + 1) * half].astype(F32)
        totals.append((own + dot(adder, returned, ROWS)).astype(BF16))

    first_a, first_b = join(
        [totals[0], *ring_gather(totals[0], False)], [totals[1], *ring_gather(totals[1], True)]
    )
    arrays_a = [first_a, *ring_gather(first_a, True)]
    arrays_b = [first_b, *ring_gather(first_b, False)]

    steps = jnp.arange(SIDE, dtype=jnp.int32)
    block_ids = ((inner // SIDE + steps) % SIDE)[:, None] * SIDE + (inner + steps) % SIDE
    block_ids = block_ids.reshape(-1)
    blocks = proj(block_ids, context, arrays_a, arrays_b, groups)
    shares = lax.all_to_all(blocks, "grp", split_axis=0, concat_axis=0, tiled=True)
    grad_ctx = ctx_grad(block_ids, w_out, arrays_a, arrays_b)
    proj_share = shares.astype(F32).sum(axis=0).astype(BF16)
    return (grad_gate[None], grad_up[None], grad_down[None], grad_ctx, proj_share)


def solution(mesh):
    rows = P(("grp", "inner"), None)
    expert = P(("grp", "inner"), None, None)
    return jax.shard_map(
        body,
        mesh=mesh,
        in_specs=(
            rows,
            rows,
            P("grp", "inner"),
            rows,
            P(),
            expert,
            expert,
            expert,
            P("inner", None),
        ),
        out_specs=(expert, expert, expert, P("grp", "inner"), P("inner", "grp")),
        check_vma=False,
    )
```

```python
import jax
import jax.numpy as jnp
from jax import lax
from jax.experimental import pallas as pl
from jax.experimental.pallas import tpu as pltpu
from jax.sharding import PartitionSpec as P

F32 = jnp.float32
BF16 = jnp.bfloat16
ROWS = (((0,), (0,)), ((), ()))
LAST = (((1,), (1,)), ((), ()))
SIDE = 4


def dot(left, right, dims=(((1,), (0,)), ((), ()))):
    return lax.dot_general(left, right, dims, preferred_element_type=F32)


def ring_pairs(step, along_z):
    pairs = []
    for z in range(SIDE):
        for y in range(SIDE):
            to = ((z + step) % SIDE) * SIDE + y if along_z else z * SIDE + (y + step) % SIDE
            pairs.append((z * SIDE + y, to))
    return pairs


def ahead(block, step, along_z):
    return lax.ppermute(block, "inner", ring_pairs(-step, along_z))


def cost(flops, moved):
    return pl.CostEstimate(flops=flops, bytes_accessed=moved, transcendentals=0)


def sum_kernel(table, back, own_a, own_b, out_a, out_b, add_a, add_b):
    @pl.when(pl.program_id(0) == 0)
    def _():
        shape = add_a.shape
        token = lax.broadcasted_iota(jnp.int32, shape, 0)
        row = lax.broadcasted_iota(jnp.int32, shape, 1)
        hit = token == table[...]
        low = (row // 4) % 2 == 0
        add_a[...] = jnp.where(hit & low, 1.0, 0.0).astype(BF16)
        add_b[...] = jnp.where(hit & ~low, 1.0, 0.0).astype(BF16)

    out_a[...] = (own_a[...].astype(F32) + dot(add_a[...], back[...])).astype(BF16)
    out_b[...] = (own_b[...].astype(F32) + dot(add_b[...], back[...])).astype(BF16)


def sum_back(table, back, own):
    rows, cols = back.shape
    tokens = own.shape[0]
    wide = 256
    steps = cols // wide
    out = jax.ShapeDtypeStruct((tokens, cols), BF16)
    out_spec = pl.BlockSpec((tokens, wide), lambda c: (0, c))
    return pl.pallas_call(
        sum_kernel,
        out_shape=(out, out),
        grid=(steps,),
        in_specs=[
            pl.BlockSpec((1, rows), lambda c: (0, 0)),
            pl.BlockSpec((rows, wide), lambda c: (0, c)),
            out_spec,
            pl.BlockSpec((tokens, wide), lambda c: (0, c + steps)),
        ],
        out_specs=(out_spec, out_spec),
        scratch_shapes=[pltpu.VMEM((tokens, rows), BF16)] * 2,
        cost_estimate=cost(4 * tokens * rows * cols, 2 * rows * cols),
    )(table, back, own, own)


def join_kernel(a0, a1, b0, b1, a, b):
    rows = a0.shape[0]
    a[:rows, :] = a0[...]
    a[rows:, :] = a1[...]
    b[:rows, :] = b0[...]
    b[rows:, :] = b1[...]


def join(a0, a1, b0, b1):
    rows, cols = a0.shape
    out = jax.ShapeDtypeStruct((2 * rows, cols), BF16)
    return pl.pallas_call(
        join_kernel, out_shape=(out, out), cost_estimate=cost(0, 16 * rows * cols)
    )(a0, a1, b0, b1)


def turn_kernel(table, block, out_a, out_b):
    turned = block[...].T
    out_a[...] = turned
    out_b[...] = turned


def turned_context(table, context):
    tokens, heads = context.shape
    rows = tokens // 16
    out = jax.ShapeDtypeStruct((heads, tokens), BF16)
    return pl.pallas_call(
        turn_kernel,
        out_shape=(out, out),
        grid_spec=pltpu.PrefetchScalarGridSpec(
            num_scalar_prefetch=1,
            grid=(16,),
            in_specs=[pl.BlockSpec((rows, heads), lambda j, t: (t[j], 0))],
            out_specs=(
                pl.BlockSpec((heads, rows), lambda j, t: (0, j)),
                pl.BlockSpec((heads, rows), lambda j, t: (0, (j % SIDE) * SIDE + j // SIDE)),
            ),
        ),
        cost_estimate=cost(0, 6 * tokens * heads),
    )(table, context)


def ctx_rows(path, spot, rows):
    off, top = spot // 2, 2 * (spot % 2)
    if path == 0:
        return [slice((off * SIDE + top) * rows, (off * SIDE + top + 2) * rows)]
    return [slice(((top + k) * SIDE + off) * rows, ((top + k) * SIDE + off + 1) * rows) for k in range(2)]


EARLY = (0, 1, 2, 3, 6, 7)
LATE = (4, 5)


def early_kernel(ctx_a, ctx_b, w_t, *refs):
    count = len(EARLY)
    arrays, proj, ctx = refs[: 2 * count], refs[2 * count], refs[2 * count + 1]
    depth = arrays[0].shape[0]
    rows = depth // 2
    block = pl.program_id(0)
    half = pl.num_programs(0) // 2

    @pl.when(block == 0)
    def _():
        ctx[...] = jnp.zeros_like(ctx)

    def work(path, turned):
        total = None
        for k, spot in enumerate(EARLY):
            piece = arrays[path * count + k][...]
            term = dot(turned[:, spot * depth : (spot + 1) * depth], piece)
            total = term if total is None else total + term
            part = dot(piece, w_t[...])
            at = 0
            for span in ctx_rows(path, spot, rows):
                size = span.stop - span.start
                ctx[span, :] += part[at : at + size]
                at += size
        proj[0] = total

    @pl.when(block < half)
    def _():
        work(0, ctx_a)

    @pl.when(block >= half)
    def _():
        work(1, ctx_b)


def late_kernel(ctx_a, ctx_b, before, *refs):
    count = len(LATE)
    arrays, proj = refs[: 2 * count], refs[2 * count]
    depth = arrays[0].shape[0]
    block = pl.program_id(0)
    half = pl.num_programs(0) // 2

    def work(path, turned):
        total = before[0]
        for k, spot in enumerate(LATE):
            total += dot(turned[:, spot * depth : (spot + 1) * depth], arrays[path * count + k][...])
        proj[0] = total.astype(BF16)

    @pl.when(block < half)
    def _():
        work(0, ctx_a)

    @pl.when(block >= half)
    def _():
        work(1, ctx_b)


def column_specs(count, depth, groups, wide):
    half = groups // 2
    a_spec = pl.BlockSpec((depth, wide), lambda g: (0, jnp.minimum(g, half - 1)))
    b_spec = pl.BlockSpec((depth, wide), lambda g: (0, jnp.maximum(g - half, 0)))
    return [a_spec] * count + [b_spec] * count


def early_proj(turned, w_t, arrays_a, arrays_b, groups):
    heads, tokens = turned[0].shape
    depth, cols = arrays_a[0].shape
    wide = 2 * cols // groups
    count = len(arrays_a)
    whole = pl.BlockSpec((heads, tokens), lambda g: (0, 0))
    return pl.pallas_call(
        early_kernel,
        out_shape=(
            jax.ShapeDtypeStruct((groups, heads, wide), F32),
            jax.ShapeDtypeStruct((tokens, heads), F32),
        ),
        grid=(groups,),
        in_specs=[whole, whole, pl.BlockSpec((wide, heads), lambda g: (g, 0))]
        + column_specs(count, depth, groups, wide),
        out_specs=(
            pl.BlockSpec((1, heads, wide), lambda g: (g, 0, 0)),
            pl.BlockSpec((tokens, heads), lambda g: (0, 0)),
        ),
        cost_estimate=cost(8 * count * depth * heads * cols, 4 * count * depth * cols),
    )(*turned, w_t, *arrays_a, *arrays_b)


def late_proj(turned, before, arrays_a, arrays_b):
    heads, tokens = turned[0].shape
    depth, cols = arrays_a[0].shape
    groups, unused, wide = before.shape
    count = len(arrays_a)
    whole = pl.BlockSpec((heads, tokens), lambda g: (0, 0))
    slab = pl.BlockSpec((1, heads, wide), lambda g: (g, 0, 0))
    return pl.pallas_call(
        late_kernel,
        out_shape=jax.ShapeDtypeStruct((groups, heads, wide), BF16),
        grid=(groups,),
        in_specs=[whole, whole, slab] + column_specs(count, depth, groups, wide),
        out_specs=slab,
        cost_estimate=cost(4 * count * depth * heads * cols, 4 * count * depth * cols),
    )(*turned, before, *arrays_a, *arrays_b)


def ctx_kernel(table, before, w_t, *refs):
    count = len(LATE)
    arrays, out = refs[: 2 * count], refs[2 * count]
    depth, cols = arrays[0].shape
    rows = depth // 2
    parts = {}
    for path in range(2):
        weights = w_t[path * cols : (path + 1) * cols, :]
        for k, spot in enumerate(LATE):
            part = dot(arrays[path * count + k][...], weights)
            at = 0
            for span in ctx_rows(path, spot, rows):
                for start in range(span.start, span.stop, rows):
                    parts.setdefault(start // rows, []).append(part[at : at + rows])
                    at += rows
    for block in range(SIDE * SIDE):
        total = before[block * rows : (block + 1) * rows, :]
        for part in parts.get(block, []):
            total = total + part
        at = pl.multiple_of(table[block] * rows, rows)
        out[pl.ds(at, rows), :] = total.astype(BF16)


def late_ctx(table, before, w_t, arrays_a, arrays_b):
    tokens, heads = before.shape
    depth, cols = arrays_a[0].shape
    vmem = pl.BlockSpec(memory_space=pltpu.VMEM)
    return pl.pallas_call(
        ctx_kernel,
        out_shape=jax.ShapeDtypeStruct((tokens, heads), BF16),
        in_specs=[pl.BlockSpec(memory_space=pltpu.SMEM)] + [vmem] * 6,
        out_specs=vmem,
        cost_estimate=cost(8 * depth * heads * cols, 8 * tokens * heads),
    )(table, before, w_t, *arrays_a, *arrays_b)


def body(moe_input, out_grad, context, gate_scale, selected, w_gate, w_up, w_down, w_out):
    groups = lax.axis_size("grp")
    inner_count = lax.axis_size("inner")
    devices = groups * inner_count
    tok_rows, width = moe_input.shape
    capacity = selected.shape[1]
    most = 4
    half = width // 2
    inner = lax.axis_index("inner")
    device = lax.axis_index("grp") * inner_count + inner
    both = ("grp", "inner")

    owner = selected // tok_rows
    mine = owner == device
    ordinal = jnp.cumsum(mine.astype(jnp.int32), axis=1) - 1
    slot_ids = jnp.arange(most, dtype=jnp.int32)
    match_slot = mine[:, :, None] & (ordinal[:, :, None] == slot_ids[None, None, :])
    local_token = selected - device * tok_rows
    token_table = jnp.sum(jnp.where(match_slot, local_token[:, :, None] + 1, 0), axis=1) - 1
    table8 = jnp.concatenate(
        [token_table, jnp.where(token_table >= 0, token_table + tok_rows, -1)], 1
    ).reshape(-1)
    token_ids = jnp.arange(2 * tok_rows, dtype=jnp.int32)
    picker = (table8[:, None] == token_ids[None, :]).astype(BF16)
    both_rows = jnp.concatenate([moe_input, out_grad], 0)
    sent = dot(picker, both_rows).astype(BF16).reshape(devices, 2 * most, width)
    arrived = lax.all_to_all(sent, both, split_axis=0, concat_axis=0, tiled=True)
    arrived = arrived.reshape(devices * 2 * most, width)

    my_owner = lax.dynamic_index_in_dim(owner, device, 0, keepdims=False)
    slot_range = jnp.arange(capacity, dtype=jnp.int32)
    same_owner = (my_owner[:, None] == my_owner[None, :]) & (
        slot_range[:, None] > slot_range[None, :]
    )
    ranking = jnp.sum(same_owner.astype(jnp.int32), axis=1)
    position = my_owner * (2 * most) + ranking
    spots = jnp.arange(devices * 2 * most, dtype=jnp.int32)
    place_in = (position[:, None] == spots[None, :]).astype(BF16)
    place_grad = ((position + most)[:, None] == spots[None, :]).astype(BF16)

    rows_in = dot(place_in, arrived).astype(BF16)
    rows_grad = dot(place_grad, arrived).astype(BF16)
    gate_w, up_w, down_w = w_gate[0], w_up[0], w_down[0]
    gate_pre = dot(rows_in, gate_w)
    up_pre = dot(rows_in, up_w)
    sig = jax.nn.sigmoid(gate_pre)
    silu = gate_pre * sig
    hidden = (silu * up_pre).astype(BF16)
    scaled = (rows_grad.astype(F32) * gate_scale[0][:, None]).astype(BF16)
    back_hidden = dot(scaled, down_w, LAST)
    back_gate = (back_hidden * up_pre * sig * (1.0 + gate_pre * (1.0 - sig))).astype(BF16)
    back_up = (back_hidden * silu).astype(BF16)

    halves = []
    for h in range(2):
        cols = slice(h * half, (h + 1) * half)
        part = dot(back_gate, gate_w[cols], LAST) + dot(back_up, up_w[cols], LAST)
        halves.append(part.astype(BF16))
    stacked = jnp.concatenate(halves, 0)
    half_of = jnp.arange(2 * capacity, dtype=jnp.int32) // capacity
    spot_of = jnp.tile(position, 2) + half_of * most
    unplace = (spots[:, None] == spot_of[None, :]).astype(BF16)
    placed = dot(unplace, stacked).astype(BF16).reshape(devices, 2 * most, half)
    returned = lax.all_to_all(placed, both, split_axis=0, concat_axis=0, tiled=True)

    grad_down = dot(hidden, scaled, ROWS).astype(BF16)
    grad_gate = dot(rows_in, back_gate, ROWS).astype(BF16)
    grad_up = dot(rows_in, back_up, ROWS).astype(BF16)
    steps = jnp.arange(SIDE, dtype=jnp.int32)
    block_ids = ((inner // SIDE + steps) % SIDE)[:, None] * SIDE + (inner + steps) % SIDE
    block_ids = block_ids.reshape(-1)
    turned = turned_context(block_ids, context)
    w_t = w_out.T
    back_table = jnp.concatenate([token_table, token_table], 1).reshape(1, -1)
    returned, grad_down, grad_gate, grad_up, turned, w_t, back_table = lax.optimization_barrier(
        (returned, grad_down, grad_gate, grad_up, turned, w_t, back_table)
    )
    returned = returned.reshape(devices * 2 * most, half)

    own = sum_back(back_table, returned, out_grad)

    near = [ahead(own[p], 1, p == 1) for p in range(2)]
    last = [ahead(own[p], 3, p == 1) for p in range(2)]
    far = [ahead(own[p], 2, p == 1) for p in range(2)]
    top = join(own[0], near[0], own[1], near[1])
    top_1 = [ahead(top[p], 1, p == 0) for p in range(2)]
    top_3 = [ahead(top[p], 3, p == 0) for p in range(2)]
    low = join(far[0], last[0], far[1], last[1])
    low_1 = [ahead(low[p], 1, p == 0) for p in range(2)]
    low_3 = [ahead(low[p], 3, p == 0) for p in range(2)]
    top_2 = [ahead(top_3[p], 3, p == 0) for p in range(2)]
    low_2 = [ahead(low_1[p], 1, p == 0) for p in range(2)]
    early = [[top[p], low[p], top_1[p], low_1[p], top_3[p], low_3[p]] for p in range(2)]
    proj_sum, ctx_sum = early_proj(turned, w_t, *early, groups)
    late = [[top_2[p], low_2[p]] for p in range(2)]
    late, proj_sum, ctx_sum = lax.optimization_barrier((late, proj_sum, ctx_sum))
    blocks = late_proj(turned, proj_sum, *late)
    shares = lax.all_to_all(blocks, "grp", split_axis=0, concat_axis=0, tiled=True)
    grad_ctx = late_ctx(block_ids, ctx_sum, w_t, *late)
    proj_share = shares.astype(F32).sum(axis=0).astype(BF16)
    return (grad_gate[None], grad_up[None], grad_down[None], grad_ctx, proj_share)


def solution(mesh):
    rows = P(("grp", "inner"), None)
    expert = P(("grp", "inner"), None, None)
    return jax.shard_map(
        body,
        mesh=mesh,
        in_specs=(
            rows,
            rows,
            P("grp", "inner"),
            rows,
            P(),
            expert,
            expert,
            expert,
            P("inner", None),
        ),
        out_specs=(expert, expert, expert, P("grp", "inner"), P("inner", "grp")),
        check_vma=False,
    )
```

```python
import jax
import jax.numpy as jnp
from jax import lax
from jax.experimental import pallas as pl
from jax.experimental.pallas import tpu as pltpu
from jax.sharding import PartitionSpec as P

F32 = jnp.float32
BF16 = jnp.bfloat16
ROWS = (((0,), (0,)), ((), ()))
LAST = (((1,), (1,)), ((), ()))
SIDE = 4


def dot(left, right, dims=(((1,), (0,)), ((), ()))):
    return lax.dot_general(left, right, dims, preferred_element_type=F32)


def ring_pairs(step, along_z):
    pairs = []
    for z in range(SIDE):
        for y in range(SIDE):
            to = ((z + step) % SIDE) * SIDE + y if along_z else z * SIDE + (y + step) % SIDE
            pairs.append((z * SIDE + y, to))
    return pairs


def ahead(block, step, along_z):
    return lax.ppermute(block, "inner", ring_pairs(-step, along_z))


def cost(flops, moved):
    return pl.CostEstimate(flops=flops, bytes_accessed=moved, transcendentals=0)


def sum_kernel(table, back, own_a, own_b, out_a, out_b, add_a, add_b):
    @pl.when(pl.program_id(0) == 0)
    def _():
        shape = add_a.shape
        token = lax.broadcasted_iota(jnp.int32, shape, 0)
        row = lax.broadcasted_iota(jnp.int32, shape, 1)
        hit = token == table[...]
        low = (row // 4) % 2 == 0
        add_a[...] = jnp.where(hit & low, 1.0, 0.0).astype(BF16)
        add_b[...] = jnp.where(hit & ~low, 1.0, 0.0).astype(BF16)

    out_a[...] = (own_a[...].astype(F32) + dot(add_a[...], back[...])).astype(BF16)
    out_b[...] = (own_b[...].astype(F32) + dot(add_b[...], back[...])).astype(BF16)


def sum_back(table, back, own):
    rows, cols = back.shape
    tokens = own.shape[0]
    wide = 256
    steps = cols // wide
    out = jax.ShapeDtypeStruct((tokens, cols), BF16)
    out_spec = pl.BlockSpec((tokens, wide), lambda c: (0, c))
    return pl.pallas_call(
        sum_kernel,
        out_shape=(out, out),
        grid=(steps,),
        in_specs=[
            pl.BlockSpec((1, rows), lambda c: (0, 0)),
            pl.BlockSpec((rows, wide), lambda c: (0, c)),
            out_spec,
            pl.BlockSpec((tokens, wide), lambda c: (0, c + steps)),
        ],
        out_specs=(out_spec, out_spec),
        scratch_shapes=[pltpu.VMEM((tokens, rows), BF16)] * 2,
        compiler_params=small(16),
        cost_estimate=cost(4 * tokens * rows * cols, 2 * rows * cols),
    )(table, back, own, own)


def join_kernel(a0, a1, b0, b1, a, b):
    rows = a0.shape[0]
    a[:rows, :] = a0[...]
    a[rows:, :] = a1[...]
    b[:rows, :] = b0[...]
    b[rows:, :] = b1[...]


def join(a0, a1, b0, b1):
    rows, cols = a0.shape
    out = jax.ShapeDtypeStruct((2 * rows, cols), BF16)
    return pl.pallas_call(
        join_kernel,
        out_shape=(out, out),
        compiler_params=small(16),
        cost_estimate=cost(0, 16 * rows * cols),
    )(a0, a1, b0, b1)


def turn_kernel(table, block, out_a, out_b):
    turned = block[...].T
    out_a[...] = turned
    out_b[...] = turned


def turned_context(table, context):
    tokens, heads = context.shape
    rows = tokens // 16
    out = jax.ShapeDtypeStruct((heads, tokens), BF16)
    return pl.pallas_call(
        turn_kernel,
        out_shape=(out, out),
        grid_spec=pltpu.PrefetchScalarGridSpec(
            num_scalar_prefetch=1,
            grid=(16,),
            in_specs=[pl.BlockSpec((rows, heads), lambda j, t: (t[j], 0))],
            out_specs=(
                pl.BlockSpec((heads, rows), lambda j, t: (0, j)),
                pl.BlockSpec((heads, rows), lambda j, t: (0, (j % SIDE) * SIDE + j // SIDE)),
            ),
        ),
        compiler_params=small(16),
        cost_estimate=cost(0, 6 * tokens * heads),
    )(table, context)


def ctx_rows(path, spot, rows):
    off, top = spot // 2, 2 * (spot % 2)
    if path == 0:
        return [slice((off * SIDE + top) * rows, (off * SIDE + top + 2) * rows)]
    return [slice(((top + k) * SIDE + off) * rows, ((top + k) * SIDE + off + 1) * rows) for k in range(2)]


EARLY = (0, 1, 3, 6)
MID = (2, 7)
LATE = (4, 5)


def small(limit):
    return pltpu.CompilerParams(vmem_limit_bytes=limit * 1024 * 1024)


def proj_kernel(spots, with_ctx, has_before, *refs):
    count = len(spots)
    refs = list(refs)
    turned = [[refs.pop(0) for k in range(count)] for p in range(2)]
    arrays = [[refs.pop(0) for k in range(count)] for p in range(2)]
    before = refs.pop(0) if has_before else None
    weights = [refs.pop(0), refs.pop(0)] if with_ctx else None
    proj = refs.pop(0)
    ctx = refs.pop(0) if with_ctx else None
    rows = arrays[0][0].shape[0] // 2

    if with_ctx:

        @pl.when(pl.program_id(0) == 0)
        def _():
            ctx[...] = jnp.zeros_like(ctx)

    for path in range(2):
        total = before[path, 0] if has_before else None
        for k, spot in enumerate(spots):
            piece = arrays[path][k][...]
            term = dot(turned[path][k][...], piece)
            total = term if total is None else total + term
            if with_ctx:
                part = dot(piece, weights[path][...])
                at = 0
                for span in ctx_rows(path, spot, rows):
                    size = span.stop - span.start
                    ctx[span, :] += part[at : at + size]
                    at += size
        proj[path, 0] = total.astype(proj.dtype)


def projected(spots, turned, arrays, out_type, before=None, w_t=None):
    heads, tokens = turned[0].shape
    depth, cols = arrays[0][0].shape
    count = len(spots)
    wide = 256
    steps = cols // wide
    slab = pl.BlockSpec((2, 1, heads, wide), lambda c: (0, c, 0, 0))
    in_specs = [pl.BlockSpec((heads, depth), lambda c, s=spot: (0, s)) for spot in spots] * 2
    in_specs += [pl.BlockSpec((depth, wide), lambda c: (0, c))] * (2 * count)
    operands = [turned[0]] * count + [turned[1]] * count + arrays[0] + arrays[1]
    out_shape = [jax.ShapeDtypeStruct((2, steps, heads, wide), out_type)]
    out_specs = [slab]
    if before is not None:
        in_specs.append(slab)
        operands.append(before)
    if w_t is not None:
        in_specs.append(pl.BlockSpec((wide, heads), lambda c: (c, 0)))
        in_specs.append(pl.BlockSpec((wide, heads), lambda c: (c + steps, 0)))
        operands += [w_t, w_t]
        out_shape.append(jax.ShapeDtypeStruct((tokens, heads), F32))
        out_specs.append(pl.BlockSpec((tokens, heads), lambda c: (0, 0)))
    flops = 4 * count * depth * heads * cols * (1 if w_t is None else 2)
    return pl.pallas_call(
        lambda *refs: proj_kernel(spots, w_t is not None, before is not None, *refs),
        out_shape=out_shape,
        grid=(steps,),
        in_specs=in_specs,
        out_specs=out_specs,
        compiler_params=small(20),
        cost_estimate=cost(flops, 4 * count * depth * cols + 8 * heads * cols),
    )(*operands)


def ctx_kernel(spots, table, before, w_t, *refs):
    count = len(spots)
    arrays, out = refs[: 2 * count], refs[2 * count]
    depth, cols = arrays[0].shape
    rows = depth // 2
    parts = {}
    for path in range(2):
        weights = w_t[path * cols : (path + 1) * cols, :]
        for k, spot in enumerate(spots):
            part = dot(arrays[path * count + k][...], weights)
            at = 0
            for span in ctx_rows(path, spot, rows):
                for start in range(span.start, span.stop, rows):
                    parts.setdefault(start // rows, []).append(part[at : at + rows])
                    at += rows
    for block in range(SIDE * SIDE):
        total = before[block * rows : (block + 1) * rows, :]
        for part in parts.get(block, []):
            total = total + part
        at = pl.multiple_of(table[block] * rows, rows)
        out[pl.ds(at, rows), :] = total.astype(BF16)


def ctx_rest(spots, table, before, w_t, arrays):
    tokens, heads = before.shape
    depth, cols = arrays[0][0].shape
    count = len(spots)
    vmem = pl.BlockSpec(memory_space=pltpu.VMEM)
    return pl.pallas_call(
        lambda *refs: ctx_kernel(spots, *refs),
        out_shape=jax.ShapeDtypeStruct((tokens, heads), BF16),
        in_specs=[pl.BlockSpec(memory_space=pltpu.SMEM)] + [vmem] * (2 + 2 * count),
        out_specs=vmem,
        compiler_params=small(20),
        cost_estimate=cost(4 * count * depth * heads * cols, 8 * tokens * heads),
    )(table, before, w_t, *arrays[0], *arrays[1])


def body(moe_input, out_grad, context, gate_scale, selected, w_gate, w_up, w_down, w_out):
    groups = lax.axis_size("grp")
    inner_count = lax.axis_size("inner")
    devices = groups * inner_count
    tok_rows, width = moe_input.shape
    capacity = selected.shape[1]
    most = 4
    half = width // 2
    inner = lax.axis_index("inner")
    device = lax.axis_index("grp") * inner_count + inner
    both = ("grp", "inner")

    owner = selected // tok_rows
    mine = owner == device
    ordinal = jnp.cumsum(mine.astype(jnp.int32), axis=1) - 1
    slot_ids = jnp.arange(most, dtype=jnp.int32)
    match_slot = mine[:, :, None] & (ordinal[:, :, None] == slot_ids[None, None, :])
    local_token = selected - device * tok_rows
    token_table = jnp.sum(jnp.where(match_slot, local_token[:, :, None] + 1, 0), axis=1) - 1
    table8 = jnp.concatenate(
        [token_table, jnp.where(token_table >= 0, token_table + tok_rows, -1)], 1
    ).reshape(-1)
    token_ids = jnp.arange(2 * tok_rows, dtype=jnp.int32)
    picker = (table8[:, None] == token_ids[None, :]).astype(BF16)
    both_rows = jnp.concatenate([moe_input, out_grad], 0)
    sent = dot(picker, both_rows).astype(BF16).reshape(devices, 2 * most, width)
    arrived = lax.all_to_all(sent, both, split_axis=0, concat_axis=0, tiled=True)
    arrived = arrived.reshape(devices * 2 * most, width)

    my_owner = lax.dynamic_index_in_dim(owner, device, 0, keepdims=False)
    slot_range = jnp.arange(capacity, dtype=jnp.int32)
    same_owner = (my_owner[:, None] == my_owner[None, :]) & (
        slot_range[:, None] > slot_range[None, :]
    )
    ranking = jnp.sum(same_owner.astype(jnp.int32), axis=1)
    position = my_owner * (2 * most) + ranking
    spots = jnp.arange(devices * 2 * most, dtype=jnp.int32)
    place_in = (position[:, None] == spots[None, :]).astype(BF16)
    place_grad = ((position + most)[:, None] == spots[None, :]).astype(BF16)

    rows_in = dot(place_in, arrived).astype(BF16)
    rows_grad = dot(place_grad, arrived).astype(BF16)
    gate_w, up_w, down_w = w_gate[0], w_up[0], w_down[0]
    gate_pre = dot(rows_in, gate_w)
    up_pre = dot(rows_in, up_w)
    sig = jax.nn.sigmoid(gate_pre)
    silu = gate_pre * sig
    hidden = (silu * up_pre).astype(BF16)
    scaled = (rows_grad.astype(F32) * gate_scale[0][:, None]).astype(BF16)
    back_hidden = dot(scaled, down_w, LAST)
    back_gate = (back_hidden * up_pre * sig * (1.0 + gate_pre * (1.0 - sig))).astype(BF16)
    back_up = (back_hidden * silu).astype(BF16)

    halves = []
    for h in range(2):
        cols = slice(h * half, (h + 1) * half)
        part = dot(back_gate, gate_w[cols], LAST) + dot(back_up, up_w[cols], LAST)
        halves.append(part.astype(BF16))
    stacked = jnp.concatenate(halves, 0)
    half_of = jnp.arange(2 * capacity, dtype=jnp.int32) // capacity
    spot_of = jnp.tile(position, 2) + half_of * most
    unplace = (spots[:, None] == spot_of[None, :]).astype(BF16)
    placed = dot(unplace, stacked).astype(BF16).reshape(devices, 2 * most, half)
    returned = lax.all_to_all(placed, both, split_axis=0, concat_axis=0, tiled=True)

    grad_down = dot(hidden, scaled, ROWS).astype(BF16)
    grad_gate = dot(rows_in, back_gate, ROWS).astype(BF16)
    grad_up = dot(rows_in, back_up, ROWS).astype(BF16)
    steps = jnp.arange(SIDE, dtype=jnp.int32)
    block_ids = ((inner // SIDE + steps) % SIDE)[:, None] * SIDE + (inner + steps) % SIDE
    block_ids = block_ids.reshape(-1)
    turned = turned_context(block_ids, context)
    w_t = w_out.T
    back_table = jnp.concatenate([token_table, token_table], 1).reshape(1, -1)
    returned, grad_down, grad_gate, grad_up, turned, w_t, back_table = lax.optimization_barrier(
        (returned, grad_down, grad_gate, grad_up, turned, w_t, back_table)
    )
    returned = returned.reshape(devices * 2 * most, half)

    own = sum_back(back_table, returned, out_grad)

    near = [ahead(own[p], 1, p == 1) for p in range(2)]
    last = [ahead(own[p], 3, p == 1) for p in range(2)]
    far = [ahead(own[p], 2, p == 1) for p in range(2)]
    top = join(own[0], near[0], own[1], near[1])
    top_1 = [ahead(top[p], 1, p == 0) for p in range(2)]
    top_3 = [ahead(top[p], 3, p == 0) for p in range(2)]
    low = join(far[0], last[0], far[1], last[1])
    low_1 = [ahead(low[p], 1, p == 0) for p in range(2)]
    low_3 = [ahead(low[p], 3, p == 0) for p in range(2)]
    top_2 = [ahead(top_3[p], 3, p == 0) for p in range(2)]
    low_2 = [ahead(low_1[p], 1, p == 0) for p in range(2)]
    early = [[top[p], low[p], low_1[p], top_3[p]] for p in range(2)]
    proj_sum, ctx_sum = projected(EARLY, turned, early, F32, w_t=w_t)
    mid = [[top_1[p], low_3[p]] for p in range(2)]
    mid, proj_sum, ctx_sum = lax.optimization_barrier((mid, proj_sum, ctx_sum))
    (proj_sum,) = projected(MID, turned, mid, F32, before=proj_sum)
    late = [[top_2[p], low_2[p]] for p in range(2)]
    late, proj_sum = lax.optimization_barrier((late, proj_sum))
    (blocks,) = projected(LATE, turned, late, BF16, before=proj_sum)
    blocks = blocks.reshape(groups, *blocks.shape[2:])
    shares = lax.all_to_all(blocks, "grp", split_axis=0, concat_axis=0, tiled=True)
    rest = [[mid[p][0], late[p][0], late[p][1], mid[p][1]] for p in range(2)]
    grad_ctx = ctx_rest((2, 4, 5, 7), block_ids, ctx_sum, w_t, rest)
    proj_share = shares.astype(F32).sum(axis=0).astype(BF16)
    return (grad_gate[None], grad_up[None], grad_down[None], grad_ctx, proj_share)


def solution(mesh):
    rows = P(("grp", "inner"), None)
    expert = P(("grp", "inner"), None, None)
    return jax.shard_map(
        body,
        mesh=mesh,
        in_specs=(
            rows,
            rows,
            P("grp", "inner"),
            rows,
            P(),
            expert,
            expert,
            expert,
            P("inner", None),
        ),
        out_specs=(expert, expert, expert, P("grp", "inner"), P("inner", "grp")),
        check_vma=False,
    )
```

```python
import jax
import jax.numpy as jnp
from jax import lax
from jax.experimental import pallas as pl
from jax.experimental.pallas import tpu as pltpu
from jax.sharding import PartitionSpec as P

F32 = jnp.float32
BF16 = jnp.bfloat16
ROWS = (((0,), (0,)), ((), ()))
LAST = (((1,), (1,)), ((), ()))
SIDE = 4


def dot(left, right, dims=(((1,), (0,)), ((), ()))):
    return lax.dot_general(left, right, dims, preferred_element_type=F32)


def ring_pairs(step, along_z):
    pairs = []
    for z in range(SIDE):
        for y in range(SIDE):
            to = ((z + step) % SIDE) * SIDE + y if along_z else z * SIDE + (y + step) % SIDE
            pairs.append((z * SIDE + y, to))
    return pairs


def core_pairs():
    return [(2 * x + core, 2 * x + 1 - core) for x in range(SIDE) for core in range(2)]


def x_pairs(step):
    return [(2 * x + core, 2 * ((x + step) % SIDE) + core) for x in range(SIDE) for core in range(2)]


def ahead(block, step, along_z):
    return lax.ppermute(block, "inner", ring_pairs(-step, along_z))


def cost(flops, moved):
    return pl.CostEstimate(flops=flops, bytes_accessed=moved, transcendentals=0)


def sum_kernel(table, back, own_a, own_b, out_a, out_b, add_a, add_b):
    @pl.when(pl.program_id(0) == 0)
    def _():
        shape = add_a.shape
        token = lax.broadcasted_iota(jnp.int32, shape, 0)
        row = lax.broadcasted_iota(jnp.int32, shape, 1)
        hit = token == table[...]
        low = (row // 4) % 2 == 0
        add_a[...] = jnp.where(hit & low, 1.0, 0.0).astype(BF16)
        add_b[...] = jnp.where(hit & ~low, 1.0, 0.0).astype(BF16)

    out_a[...] = (own_a[...].astype(F32) + dot(add_a[...], back[...])).astype(BF16)
    out_b[...] = (own_b[...].astype(F32) + dot(add_b[...], back[...])).astype(BF16)


def sum_back(table, back, own):
    rows, cols = back.shape
    tokens = own.shape[0]
    wide = 256
    steps = cols // wide
    out = jax.ShapeDtypeStruct((tokens, cols), BF16)
    out_spec = pl.BlockSpec((tokens, wide), lambda c: (0, c))
    return pl.pallas_call(
        sum_kernel,
        out_shape=(out, out),
        grid=(steps,),
        in_specs=[
            pl.BlockSpec((1, rows), lambda c: (0, 0)),
            pl.BlockSpec((rows, wide), lambda c: (0, c)),
            out_spec,
            pl.BlockSpec((tokens, wide), lambda c: (0, c + steps)),
        ],
        out_specs=(out_spec, out_spec),
        scratch_shapes=[pltpu.VMEM((tokens, rows), BF16)] * 2,
        compiler_params=small(16),
        cost_estimate=cost(4 * tokens * rows * cols, 2 * rows * cols),
    )(table, back, own, own)


def join_kernel(a0, a1, b0, b1, a, b):
    rows = a0.shape[0]
    a[:rows, :] = a0[...]
    a[rows:, :] = a1[...]
    b[:rows, :] = b0[...]
    b[rows:, :] = b1[...]


def join(a0, a1, b0, b1):
    rows, cols = a0.shape
    out = jax.ShapeDtypeStruct((2 * rows, cols), BF16)
    return pl.pallas_call(
        join_kernel,
        out_shape=(out, out),
        compiler_params=small(16),
        cost_estimate=cost(0, 16 * rows * cols),
    )(a0, a1, b0, b1)


def turn_kernel(table, block, out_a, out_b):
    turned = block[...].T
    out_a[...] = turned
    out_b[...] = turned


def turned_context(table, context):
    tokens, heads = context.shape
    rows = tokens // 16
    out = jax.ShapeDtypeStruct((heads, tokens), BF16)
    return pl.pallas_call(
        turn_kernel,
        out_shape=(out, out),
        grid_spec=pltpu.PrefetchScalarGridSpec(
            num_scalar_prefetch=1,
            grid=(16,),
            in_specs=[pl.BlockSpec((rows, heads), lambda j, t: (t[j], 0))],
            out_specs=(
                pl.BlockSpec((heads, rows), lambda j, t: (0, j)),
                pl.BlockSpec((heads, rows), lambda j, t: (0, (j % SIDE) * SIDE + j // SIDE)),
            ),
        ),
        compiler_params=small(16),
        cost_estimate=cost(0, 6 * tokens * heads),
    )(table, context)


def ctx_rows(path, spot, rows):
    off, top = spot // 2, 2 * (spot % 2)
    if path == 0:
        return [slice((off * SIDE + top) * rows, (off * SIDE + top + 2) * rows)]
    return [slice(((top + k) * SIDE + off) * rows, ((top + k) * SIDE + off + 1) * rows) for k in range(2)]


EARLY = (0, 1, 3, 6)
MID = (2, 7)
LATE = (4, 5)


def small(limit):
    return pltpu.CompilerParams(vmem_limit_bytes=limit * 1024 * 1024)


def proj_kernel(spots, with_ctx, has_before, *refs):
    count = len(spots)
    refs = list(refs)
    turned = [[refs.pop(0) for k in range(count)] for p in range(2)]
    arrays = [[refs.pop(0) for k in range(count)] for p in range(2)]
    before = refs.pop(0) if has_before else None
    weights = [refs.pop(0), refs.pop(0)] if with_ctx else None
    proj = refs.pop(0)
    ctx = refs.pop(0) if with_ctx else None
    rows = arrays[0][0].shape[0] // 2

    if with_ctx:

        @pl.when(pl.program_id(0) == 0)
        def _():
            ctx[...] = jnp.zeros_like(ctx)

    for path in range(2):
        total = before[path, 0] if has_before else None
        for k, spot in enumerate(spots):
            piece = arrays[path][k][...]
            term = dot(turned[path][k][...], piece)
            total = term if total is None else total + term
            if with_ctx:
                part = dot(piece, weights[path][...])
                at = 0
                for span in ctx_rows(path, spot, rows):
                    size = span.stop - span.start
                    ctx[span, :] += part[at : at + size]
                    at += size
        proj[path, 0] = total.astype(proj.dtype)


def projected(spots, turned, arrays, out_type, before=None, w_t=None):
    heads, tokens = turned[0].shape
    depth, cols = arrays[0][0].shape
    count = len(spots)
    wide = 256
    steps = cols // wide
    slab = pl.BlockSpec((2, 1, heads, wide), lambda c: (0, c, 0, 0))
    in_specs = [pl.BlockSpec((heads, depth), lambda c, s=spot: (0, s)) for spot in spots] * 2
    in_specs += [pl.BlockSpec((depth, wide), lambda c: (0, c))] * (2 * count)
    operands = [turned[0]] * count + [turned[1]] * count + arrays[0] + arrays[1]
    out_shape = [jax.ShapeDtypeStruct((2, steps, heads, wide), out_type)]
    out_specs = [slab]
    if before is not None:
        in_specs.append(slab)
        operands.append(before)
    if w_t is not None:
        in_specs.append(pl.BlockSpec((wide, heads), lambda c: (c, 0)))
        in_specs.append(pl.BlockSpec((wide, heads), lambda c: (c + steps, 0)))
        operands += [w_t, w_t]
        out_shape.append(jax.ShapeDtypeStruct((tokens, heads), F32))
        out_specs.append(pl.BlockSpec((tokens, heads), lambda c: (0, 0)))
    flops = 4 * count * depth * heads * cols * (1 if w_t is None else 2)
    return pl.pallas_call(
        lambda *refs: proj_kernel(spots, w_t is not None, before is not None, *refs),
        out_shape=out_shape,
        grid=(steps,),
        in_specs=in_specs,
        out_specs=out_specs,
        compiler_params=small(20),
        cost_estimate=cost(flops, 4 * count * depth * cols + 8 * heads * cols),
    )(*operands)


def late_kernel(spots, core, *refs):
    count = len(spots)
    turned, arrays = refs[: 2 * count], refs[2 * count : 4 * count]
    before, send, keep = refs[4 * count :]
    step = pl.program_id(0)
    for path in range(2):
        total = before[path, 0]
        for k in range(count):
            total += dot(turned[path * count + k][...], arrays[path * count + k][...])

        @pl.when(step % 2 != core[0])
        def _():
            send[path, step // 2] = total.astype(BF16)

        @pl.when(step % 2 == core[0])
        def _():
            keep[path, step // 2] = total


def late_projected(spots, core, turned, arrays, before):
    heads, tokens = turned[0].shape
    depth, cols = arrays[0][0].shape
    count = len(spots)
    wide = 256
    in_specs = [pl.BlockSpec(memory_space=pltpu.SMEM)]
    in_specs += [pl.BlockSpec((heads, depth), lambda c, s=spot: (0, s)) for spot in spots] * 2
    in_specs += [pl.BlockSpec((depth, wide), lambda c: (0, c))] * (2 * count)
    in_specs.append(pl.BlockSpec((2, 1, heads, wide), lambda c: (0, c, 0, 0)))
    whole = (2, 2, heads, wide)
    return pl.pallas_call(
        lambda *refs: late_kernel(spots, *refs),
        out_shape=(jax.ShapeDtypeStruct(whole, BF16), jax.ShapeDtypeStruct(whole, F32)),
        grid=(4,),
        in_specs=in_specs,
        out_specs=[pl.BlockSpec(whole, lambda c: (0, 0, 0, 0))] * 2,
        compiler_params=small(20),
        cost_estimate=cost(4 * count * depth * heads * cols, 4 * count * depth * cols),
    )(
        core.reshape(1),
        *([turned[0]] * count + [turned[1]] * count),
        *arrays[0],
        *arrays[1],
        before,
    )


def pair_kernel(place, keep, got, own, *sent):
    x = place[0]
    for step in range(SIDE):
        at = (x + step) % SIDE
        total = keep[at] + got[at].astype(F32)
        if step == 0:
            own[...] = total
        else:
            sent[step - 1][...] = total.astype(BF16)


def pair_sum(x, keep, got):
    unused, heads, wide = keep.shape
    sent = jax.ShapeDtypeStruct((heads, wide), BF16)
    whole = pl.BlockSpec((SIDE, heads, wide), lambda: (0, 0, 0))
    return pl.pallas_call(
        pair_kernel,
        out_shape=(jax.ShapeDtypeStruct((heads, wide), F32), sent, sent, sent),
        in_specs=[pl.BlockSpec(memory_space=pltpu.SMEM), whole, whole],
        compiler_params=small(16),
        cost_estimate=cost(0, 10 * SIDE * heads * wide),
    )(x.reshape(1), keep, got)


def ctx_kernel(spots, table, before, w_t, *refs):
    count = len(spots)
    arrays, out = refs[: 2 * count], refs[2 * count]
    depth, cols = arrays[0].shape
    rows = depth // 2
    parts = {}
    for path in range(2):
        weights = w_t[path * cols : (path + 1) * cols, :]
        for k, spot in enumerate(spots):
            part = dot(arrays[path * count + k][...], weights)
            at = 0
            for span in ctx_rows(path, spot, rows):
                for start in range(span.start, span.stop, rows):
                    parts.setdefault(start // rows, []).append(part[at : at + rows])
                    at += rows
    for block in range(SIDE * SIDE):
        total = before[block * rows : (block + 1) * rows, :]
        for part in parts.get(block, []):
            total = total + part
        at = pl.multiple_of(table[block] * rows, rows)
        out[pl.ds(at, rows), :] = total.astype(BF16)


def ctx_rest(spots, table, before, w_t, arrays):
    tokens, heads = before.shape
    depth, cols = arrays[0][0].shape
    count = len(spots)
    operands = [before, w_t, *arrays[0], *arrays[1]]
    return pl.pallas_call(
        lambda *refs: ctx_kernel(spots, *refs),
        out_shape=jax.ShapeDtypeStruct((tokens, heads), BF16),
        in_specs=[pl.BlockSpec(memory_space=pltpu.SMEM)]
        + [pl.BlockSpec(a.shape, lambda: (0, 0)) for a in operands],
        compiler_params=small(20),
        cost_estimate=cost(4 * count * depth * heads * cols, 8 * tokens * heads),
    )(table, *operands)


def body(moe_input, out_grad, context, gate_scale, selected, w_gate, w_up, w_down, w_out):
    groups = lax.axis_size("grp")
    inner_count = lax.axis_size("inner")
    devices = groups * inner_count
    tok_rows, width = moe_input.shape
    capacity = selected.shape[1]
    most = 4
    half = width // 2
    inner = lax.axis_index("inner")
    grp = lax.axis_index("grp")
    x, core = grp // 2, grp % 2
    device = grp * inner_count + inner
    both = ("grp", "inner")

    owner = selected // tok_rows
    mine = owner == device
    ordinal = jnp.cumsum(mine.astype(jnp.int32), axis=1) - 1
    slot_ids = jnp.arange(most, dtype=jnp.int32)
    match_slot = mine[:, :, None] & (ordinal[:, :, None] == slot_ids[None, None, :])
    local_token = selected - device * tok_rows
    token_table = jnp.sum(jnp.where(match_slot, local_token[:, :, None] + 1, 0), axis=1) - 1
    table8 = jnp.concatenate(
        [token_table, jnp.where(token_table >= 0, token_table + tok_rows, -1)], 1
    ).reshape(-1)
    token_ids = jnp.arange(2 * tok_rows, dtype=jnp.int32)
    picker = (table8[:, None] == token_ids[None, :]).astype(BF16)
    both_rows = jnp.concatenate([moe_input, out_grad], 0)
    sent = dot(picker, both_rows).astype(BF16).reshape(devices, 2 * most, width)
    arrived = lax.all_to_all(sent, both, split_axis=0, concat_axis=0, tiled=True)
    arrived = arrived.reshape(devices * 2 * most, width)

    my_owner = lax.dynamic_index_in_dim(owner, device, 0, keepdims=False)
    slot_range = jnp.arange(capacity, dtype=jnp.int32)
    same_owner = (my_owner[:, None] == my_owner[None, :]) & (
        slot_range[:, None] > slot_range[None, :]
    )
    ranking = jnp.sum(same_owner.astype(jnp.int32), axis=1)
    position = my_owner * (2 * most) + ranking
    spots = jnp.arange(devices * 2 * most, dtype=jnp.int32)
    place_in = (position[:, None] == spots[None, :]).astype(BF16)
    place_grad = ((position + most)[:, None] == spots[None, :]).astype(BF16)

    rows_in = dot(place_in, arrived).astype(BF16)
    rows_grad = dot(place_grad, arrived).astype(BF16)
    gate_w, up_w, down_w = w_gate[0], w_up[0], w_down[0]
    gate_pre = dot(rows_in, gate_w)
    up_pre = dot(rows_in, up_w)
    sig = jax.nn.sigmoid(gate_pre)
    silu = gate_pre * sig
    hidden = (silu * up_pre).astype(BF16)
    scaled = (rows_grad.astype(F32) * gate_scale[0][:, None]).astype(BF16)
    back_hidden = dot(scaled, down_w, LAST)
    back_gate = (back_hidden * up_pre * sig * (1.0 + gate_pre * (1.0 - sig))).astype(BF16)
    back_up = (back_hidden * silu).astype(BF16)

    halves = []
    for h in range(2):
        cols = slice(h * half, (h + 1) * half)
        part = dot(back_gate, gate_w[cols], LAST) + dot(back_up, up_w[cols], LAST)
        halves.append(part.astype(BF16))
    stacked = jnp.concatenate(halves, 0)
    half_of = jnp.arange(2 * capacity, dtype=jnp.int32) // capacity
    spot_of = jnp.tile(position, 2) + half_of * most
    unplace = (spots[:, None] == spot_of[None, :]).astype(BF16)
    placed = dot(unplace, stacked).astype(BF16).reshape(devices, 2 * most, half)
    returned = lax.all_to_all(placed, both, split_axis=0, concat_axis=0, tiled=True)

    grad_down = dot(hidden, scaled, ROWS).astype(BF16)
    grad_gate = dot(rows_in, back_gate, ROWS).astype(BF16)
    grad_up = dot(rows_in, back_up, ROWS).astype(BF16)
    steps = jnp.arange(SIDE, dtype=jnp.int32)
    block_ids = ((inner // SIDE + steps) % SIDE)[:, None] * SIDE + (inner + steps) % SIDE
    block_ids = block_ids.reshape(-1)
    turned = turned_context(block_ids, context)
    w_t = w_out.T
    back_table = jnp.concatenate([token_table, token_table], 1).reshape(1, -1)
    returned, grad_down, grad_gate, grad_up, turned, w_t, back_table = lax.optimization_barrier(
        (returned, grad_down, grad_gate, grad_up, turned, w_t, back_table)
    )
    returned = returned.reshape(devices * 2 * most, half)

    own = sum_back(back_table, returned, out_grad)

    near = [ahead(own[p], 1, p == 1) for p in range(2)]
    last = [ahead(own[p], 3, p == 1) for p in range(2)]
    far = [ahead(own[p], 2, p == 1) for p in range(2)]
    top = join(own[0], near[0], own[1], near[1])
    top_1 = [ahead(top[p], 1, p == 0) for p in range(2)]
    top_3 = [ahead(top[p], 3, p == 0) for p in range(2)]
    low = join(far[0], last[0], far[1], last[1])
    low_1 = [ahead(low[p], 1, p == 0) for p in range(2)]
    low_3 = [ahead(low[p], 3, p == 0) for p in range(2)]
    top_2 = [ahead(top_3[p], 3, p == 0) for p in range(2)]
    low_2 = [ahead(low_1[p], 1, p == 0) for p in range(2)]
    early = [[top[p], low[p], low_1[p], top_3[p]] for p in range(2)]
    proj_sum, ctx_sum = projected(EARLY, turned, early, F32, w_t=w_t)
    mid = [[top_1[p], low_3[p]] for p in range(2)]
    mid, proj_sum, ctx_sum = lax.optimization_barrier((mid, proj_sum, ctx_sum))
    (proj_sum,) = projected(MID, turned, mid, F32, before=proj_sum)
    late = [[top_2[p], low_2[p]] for p in range(2)]
    late, proj_sum = lax.optimization_barrier((late, proj_sum))
    send, keep = late_projected(LATE, core, turned, late, proj_sum)
    heads = context.shape[1]
    got = lax.ppermute(send.reshape(SIDE, heads, -1), "grp", core_pairs())
    own_share, *ahead_shares = pair_sum(x, keep.reshape(SIDE, heads, -1), got)
    shares = [lax.ppermute(ahead_shares[k], "grp", x_pairs(k + 1)) for k in range(3)]
    rest = [[mid[p][0], late[p][0], late[p][1], mid[p][1]] for p in range(2)]
    grad_ctx = ctx_rest((2, 4, 5, 7), block_ids, ctx_sum, w_t, rest)
    proj_share = (own_share + sum(share.astype(F32) for share in shares)).astype(BF16)
    return (grad_gate[None], grad_up[None], grad_down[None], grad_ctx, proj_share)


def solution(mesh):
    rows = P(("grp", "inner"), None)
    expert = P(("grp", "inner"), None, None)
    return jax.shard_map(
        body,
        mesh=mesh,
        in_specs=(
            rows,
            rows,
            P("grp", "inner"),
            rows,
            P(),
            expert,
            expert,
            expert,
            P("inner", None),
        ),
        out_specs=(expert, expert, expert, P("grp", "inner"), P("inner", "grp")),
        check_vma=False,
    )
```

```python
import jax
import jax.numpy as jnp
from jax import lax
from jax.experimental import pallas as pl
from jax.experimental.pallas import tpu as pltpu
from jax.sharding import PartitionSpec as P

F32 = jnp.float32
BF16 = jnp.bfloat16
ROWS = (((0,), (0,)), ((), ()))
LAST = (((1,), (1,)), ((), ()))
SIDE = 4


def dot(left, right, dims=(((1,), (0,)), ((), ()))):
    return lax.dot_general(left, right, dims, preferred_element_type=F32)


def ring_pairs(step, along_z):
    pairs = []
    for z in range(SIDE):
        for y in range(SIDE):
            to = ((z + step) % SIDE) * SIDE + y if along_z else z * SIDE + (y + step) % SIDE
            pairs.append((z * SIDE + y, to))
    return pairs


def core_pairs():
    return [(2 * x + core, 2 * x + 1 - core) for x in range(SIDE) for core in range(2)]


def x_pairs(step):
    return [(2 * x + core, 2 * ((x + step) % SIDE) + core) for x in range(SIDE) for core in range(2)]


def ahead(block, step, along_z):
    return lax.ppermute(block, "inner", ring_pairs(-step, along_z))


def cost(flops, moved):
    return pl.CostEstimate(flops=flops, bytes_accessed=moved, transcendentals=0)


def small(limit):
    return pltpu.CompilerParams(vmem_limit_bytes=limit * 1024 * 1024)


def pick_kernel(device, selected, moe_input, out_grad, out, table_out, picker, rows):
    step = pl.program_id(0)
    experts, slots = selected.shape
    tokens, lanes = moe_input.shape[0], table_out.shape[1]

    @pl.when(step == 0)
    def _():
        rel = selected[...] - device[0] * tokens
        mine = (rel >= 0) & (rel < tokens)
        first = lax.broadcasted_iota(jnp.int32, (slots, slots), 0)
        second = lax.broadcasted_iota(jnp.int32, (slots, slots), 1)
        order = dot(
            jnp.where(mine, 1.0, 0.0).astype(BF16),
            jnp.where(first <= second, 1.0, 0.0).astype(BF16),
        )
        lane = lax.broadcasted_iota(jnp.int32, (experts, lanes), 1)
        number = (rel + 1).astype(F32)
        table = jnp.zeros((experts, lanes), F32)
        for k in range(4):
            hit = mine & (order == k + 1.0)
            value = jnp.sum(jnp.where(hit, number, 0.0), axis=1, keepdims=True)
            table = jnp.where(lane == k, value, table)
            table = jnp.where((lane == k + 4) & (value > 0.0), value + tokens, table)
        table_out[...] = table
        row = lax.broadcasted_iota(jnp.int32, (8 * experts, lanes), 0)
        lane = lax.broadcasted_iota(jnp.int32, (8 * experts, lanes), 1)
        spread = dot(jnp.where(row // 8 == lane, 1.0, 0.0).astype(BF16), table.astype(BF16))
        pick = jnp.sum(jnp.where(lane == row % 8, spread, 0.0), axis=1, keepdims=True)
        token = lax.broadcasted_iota(jnp.int32, picker.shape, 1) + 1
        picker[...] = jnp.where(token.astype(F32) == pick, 1.0, 0.0).astype(BF16)
        rows[:tokens, :] = moe_input[...]
        rows[tokens:, :] = out_grad[...]

    size = out.shape[0]
    part = picker[pl.ds(pl.multiple_of(step * size, size), size), :]
    out[...] = dot(part, rows[...]).astype(BF16)


def picked(device, selected, moe_input, out_grad):
    experts, slots = selected.shape
    tokens, width = moe_input.shape
    size = 256
    whole = pl.BlockSpec((tokens, width), lambda c: (0, 0))
    return pl.pallas_call(
        pick_kernel,
        out_shape=(
            jax.ShapeDtypeStruct((8 * experts, width), BF16),
            jax.ShapeDtypeStruct((experts, 128), F32),
        ),
        grid=(8 * experts // size,),
        in_specs=[
            pl.BlockSpec(memory_space=pltpu.SMEM),
            pl.BlockSpec((experts, slots), lambda c: (0, 0)),
            whole,
            whole,
        ],
        out_specs=(
            pl.BlockSpec((size, width), lambda c: (c, 0)),
            pl.BlockSpec((experts, 128), lambda c: (0, 0)),
        ),
        scratch_shapes=[
            pltpu.VMEM((8 * experts, 2 * tokens), BF16),
            pltpu.VMEM((2 * tokens, width), BF16),
        ],
        compiler_params=small(60),
        cost_estimate=cost(32 * experts * tokens * width, 20 * experts * width),
    )(device.reshape(1), selected, moe_input, out_grad)


def expert_kernel(place_in, place_grad, scale, arrived, gate_w, up_w, down_w, *refs):
    rows_in, scaled_out, hidden, back_gate, back_up, gate_sum, up_sum, back_sum = refs
    step = pl.program_id(0)

    @pl.when(step == 0)
    def _():
        for total in (gate_sum, up_sum, back_sum):
            total[...] = jnp.zeros_like(total)

    chunk = arrived[...]
    rows = dot(place_in[...], chunk).astype(BF16)
    scaled = (dot(place_grad[...], chunk) * scale[...]).astype(BF16)
    rows_in[...] = rows
    scaled_out[...] = scaled
    gate_sum[...] += dot(rows, gate_w[...])
    up_sum[...] += dot(rows, up_w[...])
    back_sum[...] += dot(scaled, down_w[...], LAST)

    @pl.when(step == pl.num_programs(0) - 1)
    def _():
        gate_pre, up_pre, back = gate_sum[...], up_sum[...], back_sum[...]
        sig = jax.nn.sigmoid(gate_pre)
        silu = gate_pre * sig
        hidden[...] = (silu * up_pre).astype(BF16)
        back_gate[...] = (back * up_pre * sig * (1.0 + gate_pre * (1.0 - sig))).astype(BF16)
        back_up[...] = (back * silu).astype(BF16)


def expert_front(place_in, place_grad, scale, arrived, gate_w, up_w, down_w):
    slots, spots = place_in.shape
    width, hid = gate_w.shape
    wide = 512
    rows = jax.ShapeDtypeStruct((slots, width), BF16)
    units = jax.ShapeDtypeStruct((slots, hid), BF16)
    place = pl.BlockSpec((slots, spots), lambda c: (0, 0))
    rows_spec = pl.BlockSpec((slots, wide), lambda c: (0, c))
    units_spec = pl.BlockSpec((slots, hid), lambda c: (0, 0))
    weights = pl.BlockSpec((wide, hid), lambda c: (c, 0))
    flops = 4 * slots * spots * width + 6 * slots * width * hid
    return pl.pallas_call(
        expert_kernel,
        out_shape=(rows, rows, units, units, units),
        grid=(width // wide,),
        in_specs=[
            place,
            place,
            pl.BlockSpec((slots, 1), lambda c: (0, 0)),
            pl.BlockSpec((spots, wide), lambda c: (0, c)),
            weights,
            weights,
            pl.BlockSpec((hid, wide), lambda c: (0, c)),
        ],
        out_specs=(rows_spec, rows_spec, units_spec, units_spec, units_spec),
        scratch_shapes=[pltpu.VMEM((slots, hid), F32)] * 3,
        compiler_params=small(60),
        cost_estimate=cost(flops, 2 * spots * width),
    )(place_in, place_grad, scale, arrived, gate_w, up_w, down_w)


def sum_kernel(table, back, own_a, own_b, out_a, out_b, add_a, add_b):
    @pl.when(pl.program_id(0) == 0)
    def _():
        shape = add_a.shape
        token = lax.broadcasted_iota(jnp.int32, shape, 0)
        row = lax.broadcasted_iota(jnp.int32, shape, 1)
        hit = token == table[...]
        low = (row // 4) % 2 == 0
        add_a[...] = jnp.where(hit & low, 1.0, 0.0).astype(BF16)
        add_b[...] = jnp.where(hit & ~low, 1.0, 0.0).astype(BF16)

    out_a[...] = (own_a[...].astype(F32) + dot(add_a[...], back[...])).astype(BF16)
    out_b[...] = (own_b[...].astype(F32) + dot(add_b[...], back[...])).astype(BF16)


def sum_back(table, back, own):
    rows, cols = back.shape
    tokens = own.shape[0]
    wide = 256
    steps = cols // wide
    out = jax.ShapeDtypeStruct((tokens, cols), BF16)
    out_spec = pl.BlockSpec((tokens, wide), lambda c: (0, c))
    return pl.pallas_call(
        sum_kernel,
        out_shape=(out, out),
        grid=(steps,),
        in_specs=[
            pl.BlockSpec((1, rows), lambda c: (0, 0)),
            pl.BlockSpec((rows, wide), lambda c: (0, c)),
            out_spec,
            pl.BlockSpec((tokens, wide), lambda c: (0, c + steps)),
        ],
        out_specs=(out_spec, out_spec),
        scratch_shapes=[pltpu.VMEM((tokens, rows), BF16)] * 2,
        compiler_params=small(16),
        cost_estimate=cost(4 * tokens * rows * cols, 2 * rows * cols),
    )(table, back, own, own)


def join_kernel(a0, a1, b0, b1, a, b):
    rows = a0.shape[0]
    a[:rows, :] = a0[...]
    a[rows:, :] = a1[...]
    b[:rows, :] = b0[...]
    b[rows:, :] = b1[...]


def join(a0, a1, b0, b1):
    rows, cols = a0.shape
    out = jax.ShapeDtypeStruct((2 * rows, cols), BF16)
    return pl.pallas_call(
        join_kernel,
        out_shape=(out, out),
        compiler_params=small(16),
        cost_estimate=cost(0, 16 * rows * cols),
    )(a0, a1, b0, b1)


def turn_kernel(table, block, out_a, out_b):
    turned = block[...].T
    out_a[...] = turned
    out_b[...] = turned


def turned_context(table, context):
    tokens, heads = context.shape
    rows = tokens // 16
    out = jax.ShapeDtypeStruct((heads, tokens), BF16)
    return pl.pallas_call(
        turn_kernel,
        out_shape=(out, out),
        grid_spec=pltpu.PrefetchScalarGridSpec(
            num_scalar_prefetch=1,
            grid=(16,),
            in_specs=[pl.BlockSpec((rows, heads), lambda j, t: (t[j], 0))],
            out_specs=(
                pl.BlockSpec((heads, rows), lambda j, t: (0, j)),
                pl.BlockSpec((heads, rows), lambda j, t: (0, (j % SIDE) * SIDE + j // SIDE)),
            ),
        ),
        compiler_params=small(16),
        cost_estimate=cost(0, 6 * tokens * heads),
    )(table, context)


def ctx_rows(path, spot, rows):
    off, top = spot // 2, 2 * (spot % 2)
    if path == 0:
        return [slice((off * SIDE + top) * rows, (off * SIDE + top + 2) * rows)]
    return [slice(((top + k) * SIDE + off) * rows, ((top + k) * SIDE + off + 1) * rows) for k in range(2)]


EARLY = (0, 1, 3, 6)
MID = (2, 7)
LATE = (4, 5)


def proj_kernel(spots, with_ctx, has_before, *refs):
    count = len(spots)
    refs = list(refs)
    turned = [[refs.pop(0) for k in range(count)] for p in range(2)]
    arrays = [[refs.pop(0) for k in range(count)] for p in range(2)]
    before = refs.pop(0) if has_before else None
    weights = [refs.pop(0), refs.pop(0)] if with_ctx else None
    proj = refs.pop(0)
    ctx = refs.pop(0) if with_ctx else None
    rows = arrays[0][0].shape[0] // 2

    if with_ctx:

        @pl.when(pl.program_id(0) == 0)
        def _():
            ctx[...] = jnp.zeros_like(ctx)

    for path in range(2):
        total = before[path, 0] if has_before else None
        for k, spot in enumerate(spots):
            piece = arrays[path][k][...]
            term = dot(turned[path][k][...], piece)
            total = term if total is None else total + term
            if with_ctx:
                part = dot(piece, weights[path][...])
                at = 0
                for span in ctx_rows(path, spot, rows):
                    size = span.stop - span.start
                    ctx[span, :] += part[at : at + size]
                    at += size
        proj[path, 0] = total.astype(proj.dtype)


def projected(spots, turned, arrays, out_type, before=None, w_t=None):
    heads, tokens = turned[0].shape
    depth, cols = arrays[0][0].shape
    count = len(spots)
    wide = 256
    steps = cols // wide
    slab = pl.BlockSpec((2, 1, heads, wide), lambda c: (0, c, 0, 0))
    in_specs = [pl.BlockSpec((heads, depth), lambda c, s=spot: (0, s)) for spot in spots] * 2
    in_specs += [pl.BlockSpec((depth, wide), lambda c: (0, c))] * (2 * count)
    operands = [turned[0]] * count + [turned[1]] * count + arrays[0] + arrays[1]
    out_shape = [jax.ShapeDtypeStruct((2, steps, heads, wide), out_type)]
    out_specs = [slab]
    if before is not None:
        in_specs.append(slab)
        operands.append(before)
    if w_t is not None:
        in_specs.append(pl.BlockSpec((wide, heads), lambda c: (c, 0)))
        in_specs.append(pl.BlockSpec((wide, heads), lambda c: (c + steps, 0)))
        operands += [w_t, w_t]
        out_shape.append(jax.ShapeDtypeStruct((tokens, heads), F32))
        out_specs.append(pl.BlockSpec((tokens, heads), lambda c: (0, 0)))
    flops = 4 * count * depth * heads * cols * (1 if w_t is None else 2)
    return pl.pallas_call(
        lambda *refs: proj_kernel(spots, w_t is not None, before is not None, *refs),
        out_shape=out_shape,
        grid=(steps,),
        in_specs=in_specs,
        out_specs=out_specs,
        compiler_params=small(20),
        cost_estimate=cost(flops, 4 * count * depth * cols + 8 * heads * cols),
    )(*operands)


def late_kernel(spots, core, *refs):
    count = len(spots)
    turned, arrays = refs[: 2 * count], refs[2 * count : 4 * count]
    before, send, keep = refs[4 * count :]
    step = pl.program_id(0)
    for path in range(2):
        total = before[path, 0]
        for k in range(count):
            total += dot(turned[path * count + k][...], arrays[path * count + k][...])

        @pl.when(step % 2 != core[0])
        def _():
            send[path, step // 2] = total.astype(BF16)

        @pl.when(step % 2 == core[0])
        def _():
            keep[path, step // 2] = total


def late_projected(spots, core, turned, arrays, before):
    heads, tokens = turned[0].shape
    depth, cols = arrays[0][0].shape
    count = len(spots)
    wide = 256
    in_specs = [pl.BlockSpec(memory_space=pltpu.SMEM)]
    in_specs += [pl.BlockSpec((heads, depth), lambda c, s=spot: (0, s)) for spot in spots] * 2
    in_specs += [pl.BlockSpec((depth, wide), lambda c: (0, c))] * (2 * count)
    in_specs.append(pl.BlockSpec((2, 1, heads, wide), lambda c: (0, c, 0, 0)))
    whole = (2, 2, heads, wide)
    return pl.pallas_call(
        lambda *refs: late_kernel(spots, *refs),
        out_shape=(jax.ShapeDtypeStruct(whole, BF16), jax.ShapeDtypeStruct(whole, F32)),
        grid=(4,),
        in_specs=in_specs,
        out_specs=[pl.BlockSpec(whole, lambda c: (0, 0, 0, 0))] * 2,
        compiler_params=small(20),
        cost_estimate=cost(4 * count * depth * heads * cols, 4 * count * depth * cols),
    )(
        core.reshape(1),
        *([turned[0]] * count + [turned[1]] * count),
        *arrays[0],
        *arrays[1],
        before,
    )


def pair_kernel(place, keep, got, own, *sent):
    x = place[0]
    for step in range(SIDE):
        at = (x + step) % SIDE
        total = keep[at] + got[at].astype(F32)
        if step == 0:
            own[...] = total
        else:
            sent[step - 1][...] = total.astype(BF16)


def pair_sum(x, keep, got):
    unused, heads, wide = keep.shape
    sent = jax.ShapeDtypeStruct((heads, wide), BF16)
    whole = pl.BlockSpec((SIDE, heads, wide), lambda: (0, 0, 0))
    return pl.pallas_call(
        pair_kernel,
        out_shape=(jax.ShapeDtypeStruct((heads, wide), F32), sent, sent, sent),
        in_specs=[pl.BlockSpec(memory_space=pltpu.SMEM), whole, whole],
        compiler_params=small(16),
        cost_estimate=cost(0, 10 * SIDE * heads * wide),
    )(x.reshape(1), keep, got)


def ctx_kernel(spots, table, before, w_t, *refs):
    count = len(spots)
    arrays, out = refs[: 2 * count], refs[2 * count]
    depth, cols = arrays[0].shape
    rows = depth // 2
    parts = {}
    for path in range(2):
        weights = w_t[path * cols : (path + 1) * cols, :]
        for k, spot in enumerate(spots):
            part = dot(arrays[path * count + k][...], weights)
            at = 0
            for span in ctx_rows(path, spot, rows):
                for start in range(span.start, span.stop, rows):
                    parts.setdefault(start // rows, []).append(part[at : at + rows])
                    at += rows
    for block in range(SIDE * SIDE):
        total = before[block * rows : (block + 1) * rows, :]
        for part in parts.get(block, []):
            total = total + part
        at = pl.multiple_of(table[block] * rows, rows)
        out[pl.ds(at, rows), :] = total.astype(BF16)


def ctx_rest(spots, table, before, w_t, arrays):
    tokens, heads = before.shape
    depth, cols = arrays[0][0].shape
    count = len(spots)
    operands = [before, w_t, *arrays[0], *arrays[1]]
    return pl.pallas_call(
        lambda *refs: ctx_kernel(spots, *refs),
        out_shape=jax.ShapeDtypeStruct((tokens, heads), BF16),
        in_specs=[pl.BlockSpec(memory_space=pltpu.SMEM)]
        + [pl.BlockSpec(a.shape, lambda: (0, 0)) for a in operands],
        compiler_params=small(20),
        cost_estimate=cost(4 * count * depth * heads * cols, 8 * tokens * heads),
    )(table, *operands)


def body(moe_input, out_grad, context, gate_scale, selected, w_gate, w_up, w_down, w_out):
    groups = lax.axis_size("grp")
    inner_count = lax.axis_size("inner")
    devices = groups * inner_count
    tok_rows, width = moe_input.shape
    capacity = selected.shape[1]
    most = 4
    half = width // 2
    inner = lax.axis_index("inner")
    grp = lax.axis_index("grp")
    x, core = grp // 2, grp % 2
    device = grp * inner_count + inner
    both = ("grp", "inner")

    sent, numbers = picked(device, selected, moe_input, out_grad)
    arrived = lax.all_to_all(
        sent.reshape(devices, 2 * most, width), both, split_axis=0, concat_axis=0, tiled=True
    )
    arrived = arrived.reshape(devices * 2 * most, width)
    token_table = numbers[:, :most].astype(jnp.int32) - 1

    owner = selected // tok_rows
    my_owner = lax.dynamic_index_in_dim(owner, device, 0, keepdims=False)
    slot_range = jnp.arange(capacity, dtype=jnp.int32)
    same_owner = (my_owner[:, None] == my_owner[None, :]) & (
        slot_range[:, None] > slot_range[None, :]
    )
    ranking = jnp.sum(same_owner.astype(jnp.int32), axis=1)
    position = my_owner * (2 * most) + ranking
    spots = jnp.arange(devices * 2 * most, dtype=jnp.int32)
    place_in = (position[:, None] == spots[None, :]).astype(BF16)
    place_grad = ((position + most)[:, None] == spots[None, :]).astype(BF16)

    gate_w, up_w, down_w = w_gate[0], w_up[0], w_down[0]
    rows_in, scaled, hidden, back_gate, back_up = expert_front(
        place_in, place_grad, gate_scale.reshape(-1, 1), arrived, gate_w, up_w, down_w
    )

    halves = []
    for h in range(2):
        cols = slice(h * half, (h + 1) * half)
        part = dot(back_gate, gate_w[cols], LAST) + dot(back_up, up_w[cols], LAST)
        halves.append(part.astype(BF16))
    stacked = jnp.concatenate(halves, 0)
    half_of = jnp.arange(2 * capacity, dtype=jnp.int32) // capacity
    spot_of = jnp.tile(position, 2) + half_of * most
    unplace = (spots[:, None] == spot_of[None, :]).astype(BF16)
    placed = dot(unplace, stacked).astype(BF16).reshape(devices, 2 * most, half)
    returned = lax.all_to_all(placed, both, split_axis=0, concat_axis=0, tiled=True)

    grad_down = dot(hidden, scaled, ROWS).astype(BF16)
    grad_gate = dot(rows_in, back_gate, ROWS).astype(BF16)
    grad_up = dot(rows_in, back_up, ROWS).astype(BF16)
    steps = jnp.arange(SIDE, dtype=jnp.int32)
    block_ids = ((inner // SIDE + steps) % SIDE)[:, None] * SIDE + (inner + steps) % SIDE
    block_ids = block_ids.reshape(-1)
    turned = turned_context(block_ids, context)
    w_t = w_out.T
    back_table = jnp.concatenate([token_table, token_table], 1).reshape(1, -1)
    returned, grad_down, grad_gate, grad_up, turned, w_t, back_table = lax.optimization_barrier(
        (returned, grad_down, grad_gate, grad_up, turned, w_t, back_table)
    )
    returned = returned.reshape(devices * 2 * most, half)

    own = sum_back(back_table, returned, out_grad)

    near = [ahead(own[p], 1, p == 1) for p in range(2)]
    last = [ahead(own[p], 3, p == 1) for p in range(2)]
    far = [ahead(own[p], 2, p == 1) for p in range(2)]
    top = join(own[0], near[0], own[1], near[1])
    top_1 = [ahead(top[p], 1, p == 0) for p in range(2)]
    top_3 = [ahead(top[p], 3, p == 0) for p in range(2)]
    low = join(far[0], last[0], far[1], last[1])
    low_1 = [ahead(low[p], 1, p == 0) for p in range(2)]
    low_3 = [ahead(low[p], 3, p == 0) for p in range(2)]
    top_2 = [ahead(top_3[p], 3, p == 0) for p in range(2)]
    low_2 = [ahead(low_1[p], 1, p == 0) for p in range(2)]
    early = [[top[p], low[p], low_1[p], top_3[p]] for p in range(2)]
    proj_sum, ctx_sum = projected(EARLY, turned, early, F32, w_t=w_t)
    mid = [[top_1[p], low_3[p]] for p in range(2)]
    mid, proj_sum, ctx_sum = lax.optimization_barrier((mid, proj_sum, ctx_sum))
    (proj_sum,) = projected(MID, turned, mid, F32, before=proj_sum)
    late = [[top_2[p], low_2[p]] for p in range(2)]
    late, proj_sum = lax.optimization_barrier((late, proj_sum))
    send, keep = late_projected(LATE, core, turned, late, proj_sum)
    heads = context.shape[1]
    got = lax.ppermute(send.reshape(SIDE, heads, -1), "grp", core_pairs())
    own_share, *ahead_shares = pair_sum(x, keep.reshape(SIDE, heads, -1), got)
    shares = [lax.ppermute(ahead_shares[k], "grp", x_pairs(k + 1)) for k in range(3)]
    rest = [[mid[p][0], late[p][0], late[p][1], mid[p][1]] for p in range(2)]
    grad_ctx = ctx_rest((2, 4, 5, 7), block_ids, ctx_sum, w_t, rest)
    proj_share = (own_share + sum(share.astype(F32) for share in shares)).astype(BF16)
    return (grad_gate[None], grad_up[None], grad_down[None], grad_ctx, proj_share)


def solution(mesh):
    rows = P(("grp", "inner"), None)
    expert = P(("grp", "inner"), None, None)
    return jax.shard_map(
        body,
        mesh=mesh,
        in_specs=(
            rows,
            rows,
            P("grp", "inner"),
            rows,
            P(),
            expert,
            expert,
            expert,
            P("inner", None),
        ),
        out_specs=(expert, expert, expert, P("grp", "inner"), P("inner", "grp")),
        check_vma=False,
    )
```

```python
import jax
import jax.numpy as jnp
from jax import lax
from jax.experimental import pallas as pl
from jax.experimental.pallas import tpu as pltpu
from jax.sharding import PartitionSpec as P

F32 = jnp.float32
BF16 = jnp.bfloat16
ROWS = (((0,), (0,)), ((), ()))
LAST = (((1,), (1,)), ((), ()))
SIDE = 4


def dot(left, right, dims=(((1,), (0,)), ((), ()))):
    return lax.dot_general(left, right, dims, preferred_element_type=F32)


def ring_pairs(step, along_z):
    pairs = []
    for z in range(SIDE):
        for y in range(SIDE):
            to = ((z + step) % SIDE) * SIDE + y if along_z else z * SIDE + (y + step) % SIDE
            pairs.append((z * SIDE + y, to))
    return pairs


def core_pairs():
    return [(2 * x + core, 2 * x + 1 - core) for x in range(SIDE) for core in range(2)]


def x_pairs(step):
    return [(2 * x + core, 2 * ((x + step) % SIDE) + core) for x in range(SIDE) for core in range(2)]


def ahead(block, step, along_z):
    return lax.ppermute(block, "inner", ring_pairs(-step, along_z))


def cost(flops, moved):
    return pl.CostEstimate(flops=flops, bytes_accessed=moved, transcendentals=0)


def small(limit):
    return pltpu.CompilerParams(vmem_limit_bytes=limit * 1024 * 1024)


def pick_kernel(device, selected, moe_input, out_grad, out, table_out, picker, rows):
    step = pl.program_id(0)
    experts, slots = selected.shape
    tokens, lanes = moe_input.shape[0], table_out.shape[1]

    @pl.when(step == 0)
    def _():
        rel = selected[...] - device[0] * tokens
        mine = (rel >= 0) & (rel < tokens)
        first = lax.broadcasted_iota(jnp.int32, (slots, slots), 0)
        second = lax.broadcasted_iota(jnp.int32, (slots, slots), 1)
        order = dot(
            jnp.where(mine, 1.0, 0.0).astype(BF16),
            jnp.where(first <= second, 1.0, 0.0).astype(BF16),
        )
        lane = lax.broadcasted_iota(jnp.int32, (experts, lanes), 1)
        number = (rel + 1).astype(F32)
        table = jnp.zeros((experts, lanes), F32)
        for k in range(4):
            hit = mine & (order == k + 1.0)
            value = jnp.sum(jnp.where(hit, number, 0.0), axis=1, keepdims=True)
            table = jnp.where(lane == k, value, table)
            table = jnp.where((lane == k + 4) & (value > 0.0), value + tokens, table)
        table_out[...] = table
        row = lax.broadcasted_iota(jnp.int32, (8 * experts, lanes), 0)
        lane = lax.broadcasted_iota(jnp.int32, (8 * experts, lanes), 1)
        spread = dot(jnp.where(row // 8 == lane, 1.0, 0.0).astype(BF16), table.astype(BF16))
        pick = jnp.sum(jnp.where(lane == row % 8, spread, 0.0), axis=1, keepdims=True)
        token = lax.broadcasted_iota(jnp.int32, picker.shape, 1) + 1
        picker[...] = jnp.where(token.astype(F32) == pick, 1.0, 0.0).astype(BF16)
        rows[:tokens, :] = moe_input[...]
        rows[tokens:, :] = out_grad[...]

    size = out.shape[0]
    part = picker[pl.ds(pl.multiple_of(step * size, size), size), :]
    out[...] = dot(part, rows[...]).astype(BF16)


def picked(device, selected, moe_input, out_grad):
    experts, slots = selected.shape
    tokens, width = moe_input.shape
    size = 256
    whole = pl.BlockSpec((tokens, width), lambda c: (0, 0))
    return pl.pallas_call(
        pick_kernel,
        out_shape=(
            jax.ShapeDtypeStruct((8 * experts, width), BF16),
            jax.ShapeDtypeStruct((experts, 128), F32),
        ),
        grid=(8 * experts // size,),
        in_specs=[
            pl.BlockSpec(memory_space=pltpu.SMEM),
            pl.BlockSpec((experts, slots), lambda c: (0, 0)),
            whole,
            whole,
        ],
        out_specs=(
            pl.BlockSpec((size, width), lambda c: (c, 0)),
            pl.BlockSpec((experts, 128), lambda c: (0, 0)),
        ),
        scratch_shapes=[
            pltpu.VMEM((8 * experts, 2 * tokens), BF16),
            pltpu.VMEM((2 * tokens, width), BF16),
        ],
        compiler_params=small(60),
        cost_estimate=cost(32 * experts * tokens * width, 20 * experts * width),
    )(device.reshape(1), selected, moe_input, out_grad)


def expert_kernel(position, scale, spots, gate_hbm, up_hbm, down_hbm, arrived, *refs):
    results, refs = refs[:6], refs[6:]
    chunks, gate_w, up_w, down_w, gate_sum, up_sum, back_sum, stacked = refs[:8]
    rows_in, scaled_in, hidden, back_gate, back_up, out, in_sem, out_sem = refs[8:]
    count, depth, wide = chunks.shape
    slots = position.shape[0]

    def fetches(k):
        cols = slice(k * wide, (k + 1) * wide)
        pairs = (
            (arrived.at[:, cols], chunks.at[k]),
            (gate_hbm.at[cols, :], gate_w.at[cols, :]),
            (up_hbm.at[cols, :], up_w.at[cols, :]),
            (down_hbm.at[:, cols], down_w.at[:, cols]),
        )
        return [pltpu.make_async_copy(a, b, in_sem.at[k, n]) for n, (a, b) in enumerate(pairs)]

    def store(n, source):
        return pltpu.make_async_copy(source, results[n], out_sem.at[n])

    for k in range(count):
        for copy in fetches(k):
            copy.start()
    spot = lax.broadcasted_iota(jnp.int32, (slots, depth), 1)
    place_in = jnp.where(spot == position[...], 1.0, 0.0).astype(BF16)
    place_grad = jnp.where(spot == position[...] + 4, 1.0, 0.0).astype(BF16)
    for k in range(count):
        cols = slice(k * wide, (k + 1) * wide)
        waits = fetches(k)
        waits[0].wait()
        chunk = chunks[k]
        rows = dot(place_in, chunk).astype(BF16)
        scaled = (dot(place_grad, chunk) * scale[...]).astype(BF16)
        rows_in[:, cols] = rows
        scaled_in[:, cols] = scaled
        for copy in waits[1:]:
            copy.wait()
        terms = (
            (gate_sum, dot(rows, gate_w[cols, :])),
            (up_sum, dot(rows, up_w[cols, :])),
            (back_sum, dot(scaled, down_w[:, cols], LAST)),
        )
        for total, term in terms:
            total[...] = term if k == 0 else total[...] + term
    store(0, rows_in).start()
    store(1, scaled_in).start()
    gate_pre, up_pre, back = gate_sum[...], up_sum[...], back_sum[...]
    sig = jax.nn.sigmoid(gate_pre)
    silu = gate_pre * sig
    back_gate[...] = (back * up_pre * sig * (1.0 + gate_pre * (1.0 - sig))).astype(BF16)
    back_up[...] = (back * silu).astype(BF16)
    hidden[...] = (silu * up_pre).astype(BF16)
    for n, source in ((2, hidden), (3, back_gate), (4, back_up)):
        store(n, source).start()
    half = stacked.shape[1]
    for h in range(2):
        cols = slice(h * half, (h + 1) * half)
        part = dot(back_gate[...], gate_w[cols, :], LAST) + dot(back_up[...], up_w[cols, :], LAST)
        stacked[h * slots : (h + 1) * slots, :] = part.astype(BF16)
    size = out.shape[1]

    def send(k):
        return pltpu.make_async_copy(
            out.at[k], results[5].at[k * size : (k + 1) * size, :], out_sem.at[5 + k]
        )

    for k in range(out.shape[0]):
        row = lax.broadcasted_iota(jnp.int32, (size, spots.shape[1]), 0) + k * size
        unplace = jnp.where(row == spots[...], 1.0, 0.0).astype(BF16)
        out[k] = dot(unplace, stacked[...]).astype(BF16)
        send(k).start()
    for n, source in enumerate((rows_in, scaled_in, hidden, back_gate, back_up)):
        store(n, source).wait()
    for k in range(out.shape[0]):
        send(k).wait()


def expert(position, scale, spots, gate_w, up_w, down_w, arrived):
    slots = position.shape[0]
    depth, width = arrived.shape
    hid = gate_w.shape[1]
    chunks, half = 4, width // 2
    rows, units = (slots, width), (slots, hid)
    shapes = (rows, rows, units, units, units, (depth, half))
    flops = 4 * slots * depth * width + 10 * slots * width * hid + 4 * slots * depth * half
    hbm = pl.BlockSpec(memory_space=pl.ANY)
    return pl.pallas_call(
        expert_kernel,
        out_shape=[jax.ShapeDtypeStruct(shape, BF16) for shape in shapes],
        in_specs=[pl.BlockSpec(a.shape, lambda: (0, 0)) for a in (position, scale, spots)]
        + [hbm] * 4,
        out_specs=[hbm] * 6,
        scratch_shapes=[
            pltpu.VMEM((chunks, depth, width // chunks), BF16),
            pltpu.VMEM((width, hid), BF16),
            pltpu.VMEM((width, hid), BF16),
            pltpu.VMEM((hid, width), BF16),
            pltpu.VMEM(units, F32),
            pltpu.VMEM(units, F32),
            pltpu.VMEM(units, F32),
            pltpu.VMEM((2 * slots, half), BF16),
            pltpu.VMEM(rows, BF16),
            pltpu.VMEM(rows, BF16),
            pltpu.VMEM(units, BF16),
            pltpu.VMEM(units, BF16),
            pltpu.VMEM(units, BF16),
            pltpu.VMEM((4, depth // 4, half), BF16),
            pltpu.SemaphoreType.DMA((chunks, 4)),
            pltpu.SemaphoreType.DMA((9,)),
        ],
        compiler_params=small(60),
        cost_estimate=cost(flops, 2 * depth * width + 6 * width * hid),
    )(position, scale, spots, gate_w, up_w, down_w, arrived)


def sum_kernel(table, back, own_a, own_b, out_a, out_b, add_a, add_b):
    @pl.when(pl.program_id(0) == 0)
    def _():
        shape = add_a.shape
        token = lax.broadcasted_iota(jnp.int32, shape, 0)
        row = lax.broadcasted_iota(jnp.int32, shape, 1)
        hit = token == table[...]
        low = (row // 4) % 2 == 0
        add_a[...] = jnp.where(hit & low, 1.0, 0.0).astype(BF16)
        add_b[...] = jnp.where(hit & ~low, 1.0, 0.0).astype(BF16)

    out_a[...] = (own_a[...].astype(F32) + dot(add_a[...], back[...])).astype(BF16)
    out_b[...] = (own_b[...].astype(F32) + dot(add_b[...], back[...])).astype(BF16)


def sum_back(table, back, own):
    rows, cols = back.shape
    tokens = own.shape[0]
    wide = 256
    steps = cols // wide
    out = jax.ShapeDtypeStruct((tokens, cols), BF16)
    out_spec = pl.BlockSpec((tokens, wide), lambda c: (0, c))
    return pl.pallas_call(
        sum_kernel,
        out_shape=(out, out),
        grid=(steps,),
        in_specs=[
            pl.BlockSpec((1, rows), lambda c: (0, 0)),
            pl.BlockSpec((rows, wide), lambda c: (0, c)),
            out_spec,
            pl.BlockSpec((tokens, wide), lambda c: (0, c + steps)),
        ],
        out_specs=(out_spec, out_spec),
        scratch_shapes=[pltpu.VMEM((tokens, rows), BF16)] * 2,
        compiler_params=small(16),
        cost_estimate=cost(4 * tokens * rows * cols, 2 * rows * cols),
    )(table, back, own, own)


def join_kernel(a0, a1, b0, b1, a, b):
    rows = a0.shape[0]
    a[:rows, :] = a0[...]
    a[rows:, :] = a1[...]
    b[:rows, :] = b0[...]
    b[rows:, :] = b1[...]


def join(a0, a1, b0, b1):
    rows, cols = a0.shape
    out = jax.ShapeDtypeStruct((2 * rows, cols), BF16)
    return pl.pallas_call(
        join_kernel,
        out_shape=(out, out),
        compiler_params=small(16),
        cost_estimate=cost(0, 16 * rows * cols),
    )(a0, a1, b0, b1)


def turn_kernel(table, block, out_a, out_b):
    turned = block[...].T
    out_a[...] = turned
    out_b[...] = turned


def turned_context(table, context):
    tokens, heads = context.shape
    rows = tokens // 16
    out = jax.ShapeDtypeStruct((heads, tokens), BF16)
    return pl.pallas_call(
        turn_kernel,
        out_shape=(out, out),
        grid_spec=pltpu.PrefetchScalarGridSpec(
            num_scalar_prefetch=1,
            grid=(16,),
            in_specs=[pl.BlockSpec((rows, heads), lambda j, t: (t[j], 0))],
            out_specs=(
                pl.BlockSpec((heads, rows), lambda j, t: (0, j)),
                pl.BlockSpec((heads, rows), lambda j, t: (0, (j % SIDE) * SIDE + j // SIDE)),
            ),
        ),
        compiler_params=small(16),
        cost_estimate=cost(0, 6 * tokens * heads),
    )(table, context)


def ctx_rows(path, spot, rows):
    off, top = spot // 2, 2 * (spot % 2)
    if path == 0:
        return [slice((off * SIDE + top) * rows, (off * SIDE + top + 2) * rows)]
    return [slice(((top + k) * SIDE + off) * rows, ((top + k) * SIDE + off + 1) * rows) for k in range(2)]


EARLY = (0, 1, 3, 6)
MID = (2, 7)
LATE = (4, 5)


def proj_kernel(spots, with_ctx, has_before, *refs):
    count = len(spots)
    refs = list(refs)
    turned = [[refs.pop(0) for k in range(count)] for p in range(2)]
    arrays = [[refs.pop(0) for k in range(count)] for p in range(2)]
    before = refs.pop(0) if has_before else None
    weights = [refs.pop(0), refs.pop(0)] if with_ctx else None
    proj = refs.pop(0)
    ctx = refs.pop(0) if with_ctx else None
    rows = arrays[0][0].shape[0] // 2

    if with_ctx:

        @pl.when(pl.program_id(0) == 0)
        def _():
            ctx[...] = jnp.zeros_like(ctx)

    for path in range(2):
        total = before[path, 0] if has_before else None
        for k, spot in enumerate(spots):
            piece = arrays[path][k][...]
            term = dot(turned[path][k][...], piece)
            total = term if total is None else total + term
            if with_ctx:
                part = dot(piece, weights[path][...])
                at = 0
                for span in ctx_rows(path, spot, rows):
                    size = span.stop - span.start
                    ctx[span, :] += part[at : at + size]
                    at += size
        proj[path, 0] = total.astype(proj.dtype)


def projected(spots, turned, arrays, out_type, before=None, w_t=None):
    heads, tokens = turned[0].shape
    depth, cols = arrays[0][0].shape
    count = len(spots)
    wide = 256
    steps = cols // wide
    slab = pl.BlockSpec((2, 1, heads, wide), lambda c: (0, c, 0, 0))
    in_specs = [pl.BlockSpec((heads, depth), lambda c, s=spot: (0, s)) for spot in spots] * 2
    in_specs += [pl.BlockSpec((depth, wide), lambda c: (0, c))] * (2 * count)
    operands = [turned[0]] * count + [turned[1]] * count + arrays[0] + arrays[1]
    out_shape = [jax.ShapeDtypeStruct((2, steps, heads, wide), out_type)]
    out_specs = [slab]
    if before is not None:
        in_specs.append(slab)
        operands.append(before)
    if w_t is not None:
        in_specs.append(pl.BlockSpec((wide, heads), lambda c: (c, 0)))
        in_specs.append(pl.BlockSpec((wide, heads), lambda c: (c + steps, 0)))
        operands += [w_t, w_t]
        out_shape.append(jax.ShapeDtypeStruct((tokens, heads), F32))
        out_specs.append(pl.BlockSpec((tokens, heads), lambda c: (0, 0)))
    flops = 4 * count * depth * heads * cols * (1 if w_t is None else 2)
    return pl.pallas_call(
        lambda *refs: proj_kernel(spots, w_t is not None, before is not None, *refs),
        out_shape=out_shape,
        grid=(steps,),
        in_specs=in_specs,
        out_specs=out_specs,
        compiler_params=small(20),
        cost_estimate=cost(flops, 4 * count * depth * cols + 8 * heads * cols),
    )(*operands)


def late_kernel(spots, core, *refs):
    count = len(spots)
    turned, arrays = refs[: 2 * count], refs[2 * count : 4 * count]
    before, send, keep = refs[4 * count :]
    step = pl.program_id(0)
    for path in range(2):
        total = before[path, 0]
        for k in range(count):
            total += dot(turned[path * count + k][...], arrays[path * count + k][...])

        @pl.when(step % 2 != core[0])
        def _():
            send[path, step // 2] = total.astype(BF16)

        @pl.when(step % 2 == core[0])
        def _():
            keep[path, step // 2] = total


def late_projected(spots, core, turned, arrays, before):
    heads, tokens = turned[0].shape
    depth, cols = arrays[0][0].shape
    count = len(spots)
    wide = 256
    in_specs = [pl.BlockSpec(memory_space=pltpu.SMEM)]
    in_specs += [pl.BlockSpec((heads, depth), lambda c, s=spot: (0, s)) for spot in spots] * 2
    in_specs += [pl.BlockSpec((depth, wide), lambda c: (0, c))] * (2 * count)
    in_specs.append(pl.BlockSpec((2, 1, heads, wide), lambda c: (0, c, 0, 0)))
    whole = (2, 2, heads, wide)
    return pl.pallas_call(
        lambda *refs: late_kernel(spots, *refs),
        out_shape=(jax.ShapeDtypeStruct(whole, BF16), jax.ShapeDtypeStruct(whole, F32)),
        grid=(4,),
        in_specs=in_specs,
        out_specs=[pl.BlockSpec(whole, lambda c: (0, 0, 0, 0))] * 2,
        compiler_params=small(20),
        cost_estimate=cost(4 * count * depth * heads * cols, 4 * count * depth * cols),
    )(
        core.reshape(1),
        *([turned[0]] * count + [turned[1]] * count),
        *arrays[0],
        *arrays[1],
        before,
    )


def pair_kernel(place, keep, got, own, *sent):
    x = place[0]
    for step in range(SIDE):
        at = (x + step) % SIDE
        total = keep[at] + got[at].astype(F32)
        if step == 0:
            own[...] = total
        else:
            sent[step - 1][...] = total.astype(BF16)


def pair_sum(x, keep, got):
    unused, heads, wide = keep.shape
    sent = jax.ShapeDtypeStruct((heads, wide), BF16)
    whole = pl.BlockSpec((SIDE, heads, wide), lambda: (0, 0, 0))
    return pl.pallas_call(
        pair_kernel,
        out_shape=(jax.ShapeDtypeStruct((heads, wide), F32), sent, sent, sent),
        in_specs=[pl.BlockSpec(memory_space=pltpu.SMEM), whole, whole],
        compiler_params=small(16),
        cost_estimate=cost(0, 10 * SIDE * heads * wide),
    )(x.reshape(1), keep, got)


def ctx_kernel(spots, table, before, w_t, *refs):
    count = len(spots)
    arrays, out = refs[: 2 * count], refs[2 * count]
    depth, cols = arrays[0].shape
    rows = depth // 2
    parts = {}
    for path in range(2):
        weights = w_t[path * cols : (path + 1) * cols, :]
        for k, spot in enumerate(spots):
            part = dot(arrays[path * count + k][...], weights)
            at = 0
            for span in ctx_rows(path, spot, rows):
                for start in range(span.start, span.stop, rows):
                    parts.setdefault(start // rows, []).append(part[at : at + rows])
                    at += rows
    for block in range(SIDE * SIDE):
        total = before[block * rows : (block + 1) * rows, :]
        for part in parts.get(block, []):
            total = total + part
        at = pl.multiple_of(table[block] * rows, rows)
        out[pl.ds(at, rows), :] = total.astype(BF16)


def ctx_rest(spots, table, before, w_t, arrays):
    tokens, heads = before.shape
    depth, cols = arrays[0][0].shape
    count = len(spots)
    operands = [before, w_t, *arrays[0], *arrays[1]]
    return pl.pallas_call(
        lambda *refs: ctx_kernel(spots, *refs),
        out_shape=jax.ShapeDtypeStruct((tokens, heads), BF16),
        in_specs=[pl.BlockSpec(memory_space=pltpu.SMEM)]
        + [pl.BlockSpec(a.shape, lambda: (0, 0)) for a in operands],
        compiler_params=small(20),
        cost_estimate=cost(4 * count * depth * heads * cols, 8 * tokens * heads),
    )(table, *operands)


def body(moe_input, out_grad, context, gate_scale, selected, w_gate, w_up, w_down, w_out):
    groups = lax.axis_size("grp")
    inner_count = lax.axis_size("inner")
    devices = groups * inner_count
    tok_rows, width = moe_input.shape
    capacity = selected.shape[1]
    most = 4
    half = width // 2
    inner = lax.axis_index("inner")
    grp = lax.axis_index("grp")
    x, core = grp // 2, grp % 2
    device = grp * inner_count + inner
    both = ("grp", "inner")

    sent, numbers = picked(device, selected, moe_input, out_grad)
    arrived = lax.all_to_all(
        sent.reshape(devices, 2 * most, width), both, split_axis=0, concat_axis=0, tiled=True
    )
    token_table = numbers[:, :most].astype(jnp.int32) - 1

    owner = selected // tok_rows
    my_owner = lax.dynamic_index_in_dim(owner, device, 0, keepdims=False)
    slot_range = jnp.arange(capacity, dtype=jnp.int32)
    same_owner = (my_owner[:, None] == my_owner[None, :]) & (
        slot_range[:, None] > slot_range[None, :]
    )
    ranking = jnp.sum(same_owner.astype(jnp.int32), axis=1)
    position = my_owner * (2 * most) + ranking
    half_of = jnp.arange(2 * capacity, dtype=jnp.int32) // capacity
    spot_of = jnp.tile(position, 2) + half_of * most
    rows_in, scaled, hidden, back_gate, back_up, placed = expert(
        position.reshape(-1, 1),
        gate_scale.reshape(-1, 1),
        spot_of.reshape(1, -1),
        w_gate[0],
        w_up[0],
        w_down[0],
        arrived.reshape(devices * 2 * most, width),
    )
    placed = placed.reshape(devices, 2 * most, half)
    returned = lax.all_to_all(placed, both, split_axis=0, concat_axis=0, tiled=True)

    grad_down = dot(hidden, scaled, ROWS).astype(BF16)
    grad_gate = dot(rows_in, back_gate, ROWS).astype(BF16)
    grad_up = dot(rows_in, back_up, ROWS).astype(BF16)
    steps = jnp.arange(SIDE, dtype=jnp.int32)
    block_ids = ((inner // SIDE + steps) % SIDE)[:, None] * SIDE + (inner + steps) % SIDE
    block_ids = block_ids.reshape(-1)
    turned = turned_context(block_ids, context)
    w_t = w_out.T
    back_table = jnp.concatenate([token_table, token_table], 1).reshape(1, -1)
    returned, grad_down, grad_gate, grad_up, turned, w_t, back_table = lax.optimization_barrier(
        (returned, grad_down, grad_gate, grad_up, turned, w_t, back_table)
    )
    returned = returned.reshape(devices * 2 * most, half)

    own = sum_back(back_table, returned, out_grad)

    near = [ahead(own[p], 1, p == 1) for p in range(2)]
    last = [ahead(own[p], 3, p == 1) for p in range(2)]
    far = [ahead(own[p], 2, p == 1) for p in range(2)]
    top = join(own[0], near[0], own[1], near[1])
    top_1 = [ahead(top[p], 1, p == 0) for p in range(2)]
    top_3 = [ahead(top[p], 3, p == 0) for p in range(2)]
    low = join(far[0], last[0], far[1], last[1])
    low_1 = [ahead(low[p], 1, p == 0) for p in range(2)]
    low_3 = [ahead(low[p], 3, p == 0) for p in range(2)]
    top_2 = [ahead(top_3[p], 3, p == 0) for p in range(2)]
    low_2 = [ahead(low_1[p], 1, p == 0) for p in range(2)]
    early = [[top[p], low[p], low_1[p], top_3[p]] for p in range(2)]
    proj_sum, ctx_sum = projected(EARLY, turned, early, F32, w_t=w_t)
    mid = [[top_1[p], low_3[p]] for p in range(2)]
    mid, proj_sum, ctx_sum = lax.optimization_barrier((mid, proj_sum, ctx_sum))
    (proj_sum,) = projected(MID, turned, mid, F32, before=proj_sum)
    late = [[top_2[p], low_2[p]] for p in range(2)]
    late, proj_sum = lax.optimization_barrier((late, proj_sum))
    send, keep = late_projected(LATE, core, turned, late, proj_sum)
    heads = context.shape[1]
    got = lax.ppermute(send.reshape(SIDE, heads, -1), "grp", core_pairs())
    own_share, *ahead_shares = pair_sum(x, keep.reshape(SIDE, heads, -1), got)
    shares = [lax.ppermute(ahead_shares[k], "grp", x_pairs(k + 1)) for k in range(3)]
    rest = [[mid[p][0], late[p][0], late[p][1], mid[p][1]] for p in range(2)]
    grad_ctx = ctx_rest((2, 4, 5, 7), block_ids, ctx_sum, w_t, rest)
    proj_share = (own_share + sum(share.astype(F32) for share in shares)).astype(BF16)
    return (grad_gate[None], grad_up[None], grad_down[None], grad_ctx, proj_share)


def solution(mesh):
    rows = P(("grp", "inner"), None)
    expert = P(("grp", "inner"), None, None)
    return jax.shard_map(
        body,
        mesh=mesh,
        in_specs=(
            rows,
            rows,
            P("grp", "inner"),
            rows,
            P(),
            expert,
            expert,
            expert,
            P("inner", None),
        ),
        out_specs=(expert, expert, expert, P("grp", "inner"), P("inner", "grp")),
        check_vma=False,
    )
```

```python
import jax
import jax.numpy as jnp
from jax import lax
from jax.experimental import pallas as pl
from jax.experimental.pallas import tpu as pltpu
from jax.sharding import PartitionSpec as P

F32 = jnp.float32
BF16 = jnp.bfloat16
ROWS = (((0,), (0,)), ((), ()))
LAST = (((1,), (1,)), ((), ()))
SIDE = 4


def dot(left, right, dims=(((1,), (0,)), ((), ()))):
    return lax.dot_general(left, right, dims, preferred_element_type=F32)


def ring_pairs(step, along_z):
    pairs = []
    for z in range(SIDE):
        for y in range(SIDE):
            to = ((z + step) % SIDE) * SIDE + y if along_z else z * SIDE + (y + step) % SIDE
            pairs.append((z * SIDE + y, to))
    return pairs


def core_pairs():
    return [(2 * x + core, 2 * x + 1 - core) for x in range(SIDE) for core in range(2)]


def x_pairs(step):
    return [(2 * x + core, 2 * ((x + step) % SIDE) + core) for x in range(SIDE) for core in range(2)]


def ahead(block, step, along_z):
    return lax.ppermute(block, "inner", ring_pairs(-step, along_z))


def cost(flops, moved):
    return pl.CostEstimate(flops=flops, bytes_accessed=moved, transcendentals=0)


def small(limit):
    return pltpu.CompilerParams(vmem_limit_bytes=limit * 1024 * 1024)


def pick_kernel(device, selected, moe_input, out_grad, out, table_out, picker, rows):
    step = pl.program_id(0)
    experts, slots = selected.shape
    tokens, lanes = moe_input.shape[0], table_out.shape[1]

    @pl.when(step == 0)
    def _():
        rel = selected[...] - device[0] * tokens
        mine = (rel >= 0) & (rel < tokens)
        first = lax.broadcasted_iota(jnp.int32, (slots, slots), 0)
        second = lax.broadcasted_iota(jnp.int32, (slots, slots), 1)
        order = dot(
            jnp.where(mine, 1.0, 0.0).astype(BF16),
            jnp.where(first <= second, 1.0, 0.0).astype(BF16),
        )
        lane = lax.broadcasted_iota(jnp.int32, (experts, lanes), 1)
        number = (rel + 1).astype(F32)
        table = jnp.zeros((experts, lanes), F32)
        for k in range(4):
            hit = mine & (order == k + 1.0)
            value = jnp.sum(jnp.where(hit, number, 0.0), axis=1, keepdims=True)
            table = jnp.where(lane == k, value, table)
            table = jnp.where((lane == k + 4) & (value > 0.0), value + tokens, table)
        table_out[...] = table
        row = lax.broadcasted_iota(jnp.int32, (8 * experts, lanes), 0)
        lane = lax.broadcasted_iota(jnp.int32, (8 * experts, lanes), 1)
        spread = dot(jnp.where(row // 8 == lane, 1.0, 0.0).astype(BF16), table.astype(BF16))
        pick = jnp.sum(jnp.where(lane == row % 8, spread, 0.0), axis=1, keepdims=True)
        token = lax.broadcasted_iota(jnp.int32, picker.shape, 1) + 1
        picker[...] = jnp.where(token.astype(F32) == pick, 1.0, 0.0).astype(BF16)
        rows[:tokens, :] = moe_input[...]
        rows[tokens:, :] = out_grad[...]

    size = out.shape[0]
    part = picker[pl.ds(pl.multiple_of(step * size, size), size), :]
    out[...] = dot(part, rows[...]).astype(BF16)


def picked(device, selected, moe_input, out_grad):
    experts, slots = selected.shape
    tokens, width = moe_input.shape
    size = 256
    whole = pl.BlockSpec((tokens, width), lambda c: (0, 0))
    return pl.pallas_call(
        pick_kernel,
        out_shape=(
            jax.ShapeDtypeStruct((8 * experts, width), BF16),
            jax.ShapeDtypeStruct((experts, 128), F32),
        ),
        grid=(8 * experts // size,),
        in_specs=[
            pl.BlockSpec(memory_space=pltpu.SMEM),
            pl.BlockSpec((experts, slots), lambda c: (0, 0)),
            whole,
            whole,
        ],
        out_specs=(
            pl.BlockSpec((size, width), lambda c: (c, 0)),
            pl.BlockSpec((experts, 128), lambda c: (0, 0)),
        ),
        scratch_shapes=[
            pltpu.VMEM((8 * experts, 2 * tokens), BF16),
            pltpu.VMEM((2 * tokens, width), BF16),
        ],
        compiler_params=small(60),
        cost_estimate=cost(32 * experts * tokens * width, 20 * experts * width),
    )(device.reshape(1), selected, moe_input, out_grad)


def expert_kernel(position, scale, spots, gate_hbm, up_hbm, down_hbm, arrived, *refs):
    results, refs = refs[:6], refs[6:]
    chunks, gate_w, up_w, down_w, gate_sum, up_sum, back_sum, stacked = refs[:8]
    rows_in, scaled_in, hidden, back_gate, back_up, out, in_sem, out_sem = refs[8:]
    count, depth, wide = chunks.shape
    slots = position.shape[0]

    def fetches(k):
        cols = slice(k * wide, (k + 1) * wide)
        pairs = (
            (arrived.at[:, cols], chunks.at[k]),
            (gate_hbm.at[cols, :], gate_w.at[cols, :]),
            (up_hbm.at[cols, :], up_w.at[cols, :]),
            (down_hbm.at[:, cols], down_w.at[:, cols]),
        )
        return [pltpu.make_async_copy(a, b, in_sem.at[k, n]) for n, (a, b) in enumerate(pairs)]

    def store(n, source):
        return pltpu.make_async_copy(source, results[n], out_sem.at[n])

    for k in range(count):
        for copy in fetches(k):
            copy.start()
    spot = lax.broadcasted_iota(jnp.int32, (slots, depth), 1)
    place_in = jnp.where(spot == position[...], 1.0, 0.0).astype(BF16)
    place_grad = jnp.where(spot == position[...] + 4, 1.0, 0.0).astype(BF16)
    for k in range(count):
        cols = slice(k * wide, (k + 1) * wide)
        waits = fetches(k)
        waits[0].wait()
        chunk = chunks[k]
        rows = dot(place_in, chunk).astype(BF16)
        scaled = (dot(place_grad, chunk) * scale[...]).astype(BF16)
        rows_in[:, cols] = rows
        scaled_in[:, cols] = scaled
        for copy in waits[1:]:
            copy.wait()
        terms = (
            (gate_sum, dot(rows, gate_w[cols, :])),
            (up_sum, dot(rows, up_w[cols, :])),
            (back_sum, dot(scaled, down_w[:, cols], LAST)),
        )
        for total, term in terms:
            total[...] = term if k == 0 else total[...] + term
    store(0, rows_in).start()
    store(1, scaled_in).start()
    gate_pre, up_pre, back = gate_sum[...], up_sum[...], back_sum[...]
    sig = jax.nn.sigmoid(gate_pre)
    silu = gate_pre * sig
    back_gate[...] = (back * up_pre * sig * (1.0 + gate_pre * (1.0 - sig))).astype(BF16)
    back_up[...] = (back * silu).astype(BF16)
    hidden[...] = (silu * up_pre).astype(BF16)
    for n, source in ((2, hidden), (3, back_gate), (4, back_up)):
        store(n, source).start()
    half = stacked.shape[1]
    for h in range(2):
        cols = slice(h * half, (h + 1) * half)
        part = dot(back_gate[...], gate_w[cols, :], LAST) + dot(back_up[...], up_w[cols, :], LAST)
        stacked[h * slots : (h + 1) * slots, :] = part.astype(BF16)
    size = out.shape[1]

    def send(k):
        return pltpu.make_async_copy(
            out.at[k], results[5].at[k * size : (k + 1) * size, :], out_sem.at[5 + k]
        )

    for k in range(out.shape[0]):
        row = lax.broadcasted_iota(jnp.int32, (size, spots.shape[1]), 0) + k * size
        unplace = jnp.where(row == spots[...], 1.0, 0.0).astype(BF16)
        out[k] = dot(unplace, stacked[...]).astype(BF16)
        send(k).start()
    for n, source in enumerate((rows_in, scaled_in, hidden, back_gate, back_up)):
        store(n, source).wait()
    for k in range(out.shape[0]):
        send(k).wait()


def expert(position, scale, spots, gate_w, up_w, down_w, arrived):
    slots = position.shape[0]
    depth, width = arrived.shape
    hid = gate_w.shape[1]
    chunks, half = 4, width // 2
    rows, units = (slots, width), (slots, hid)
    shapes = (rows, rows, units, units, units, (depth, half))
    flops = 4 * slots * depth * width + 10 * slots * width * hid + 4 * slots * depth * half
    hbm = pl.BlockSpec(memory_space=pl.ANY)
    return pl.pallas_call(
        expert_kernel,
        out_shape=[jax.ShapeDtypeStruct(shape, BF16) for shape in shapes],
        in_specs=[pl.BlockSpec(a.shape, lambda: (0, 0)) for a in (position, scale, spots)]
        + [hbm] * 4,
        out_specs=[hbm] * 6,
        scratch_shapes=[
            pltpu.VMEM((chunks, depth, width // chunks), BF16),
            pltpu.VMEM((width, hid), BF16),
            pltpu.VMEM((width, hid), BF16),
            pltpu.VMEM((hid, width), BF16),
            pltpu.VMEM(units, F32),
            pltpu.VMEM(units, F32),
            pltpu.VMEM(units, F32),
            pltpu.VMEM((2 * slots, half), BF16),
            pltpu.VMEM(rows, BF16),
            pltpu.VMEM(rows, BF16),
            pltpu.VMEM(units, BF16),
            pltpu.VMEM(units, BF16),
            pltpu.VMEM(units, BF16),
            pltpu.VMEM((4, depth // 4, half), BF16),
            pltpu.SemaphoreType.DMA((chunks, 4)),
            pltpu.SemaphoreType.DMA((9,)),
        ],
        compiler_params=small(60),
        cost_estimate=cost(flops, 2 * depth * width + 6 * width * hid),
    )(position, scale, spots, gate_w, up_w, down_w, arrived)


def sum_kernel(table, back, own, out_a, out_b, chunks, mine, sems):
    count, rows, wide = chunks.shape
    tokens = mine.shape[0]

    def fetch(k):
        return pltpu.make_async_copy(
            back.at[:, k * wide : (k + 1) * wide], chunks.at[k], sems.at[k]
        )

    for k in range(count):
        fetch(k).start()
    first = pltpu.make_async_copy(own, mine, sems.at[count])
    first.start()
    token = lax.broadcasted_iota(jnp.int32, (tokens, rows), 0)
    row = lax.broadcasted_iota(jnp.int32, (tokens, rows), 1)
    hit = token == table[...]
    low = (row // 4) % 2 == 0
    add_a = jnp.where(hit & low, 1.0, 0.0).astype(BF16)
    add_b = jnp.where(hit & ~low, 1.0, 0.0).astype(BF16)
    first.wait()
    for k in range(count):
        fetch(k).wait()
        cols = slice(k * wide, (k + 1) * wide)
        after = slice((count + k) * wide, (count + k + 1) * wide)
        chunk = chunks[k]
        out_a[:, cols] = (mine[:, cols].astype(F32) + dot(add_a, chunk)).astype(BF16)
        out_b[:, cols] = (mine[:, after].astype(F32) + dot(add_b, chunk)).astype(BF16)


def sum_back(table, back, own):
    rows, cols = back.shape
    tokens = own.shape[0]
    count = 4
    out = jax.ShapeDtypeStruct((tokens, cols), BF16)
    hbm = pl.BlockSpec(memory_space=pltpu.HBM)
    return pl.pallas_call(
        sum_kernel,
        out_shape=(out, out),
        in_specs=[pl.BlockSpec((1, rows), lambda: (0, 0)), hbm, hbm],
        scratch_shapes=[
            pltpu.VMEM((count, rows, cols // count), BF16),
            pltpu.VMEM(own.shape, BF16),
            pltpu.SemaphoreType.DMA((count + 1,)),
        ],
        compiler_params=small(16),
        cost_estimate=cost(4 * tokens * rows * cols, 2 * rows * cols),
    )(table, back, own)


def join_kernel(a0, a1, b0, b1, a, b):
    rows = a0.shape[0]
    a[:rows, :] = a0[...]
    a[rows:, :] = a1[...]
    b[:rows, :] = b0[...]
    b[rows:, :] = b1[...]


def join(a0, a1, b0, b1):
    rows, cols = a0.shape
    out = jax.ShapeDtypeStruct((2 * rows, cols), BF16)
    return pl.pallas_call(
        join_kernel,
        out_shape=(out, out),
        compiler_params=small(16),
        cost_estimate=cost(0, 16 * rows * cols),
    )(a0, a1, b0, b1)


def turn_kernel(table, block, out_a, out_b):
    turned = block[...].T
    out_a[...] = turned
    out_b[...] = turned


def turned_context(table, context):
    tokens, heads = context.shape
    rows = tokens // 16
    out = jax.ShapeDtypeStruct((heads, tokens), BF16)
    return pl.pallas_call(
        turn_kernel,
        out_shape=(out, out),
        grid_spec=pltpu.PrefetchScalarGridSpec(
            num_scalar_prefetch=1,
            grid=(16,),
            in_specs=[pl.BlockSpec((rows, heads), lambda j, t: (t[j], 0))],
            out_specs=(
                pl.BlockSpec((heads, rows), lambda j, t: (0, j)),
                pl.BlockSpec((heads, rows), lambda j, t: (0, (j % SIDE) * SIDE + j // SIDE)),
            ),
        ),
        compiler_params=small(16),
        cost_estimate=cost(0, 6 * tokens * heads),
    )(table, context)


def ctx_rows(path, spot, rows):
    off, top = spot // 2, 2 * (spot % 2)
    if path == 0:
        return [slice((off * SIDE + top) * rows, (off * SIDE + top + 2) * rows)]
    return [slice(((top + k) * SIDE + off) * rows, ((top + k) * SIDE + off + 1) * rows) for k in range(2)]


EARLY = (0, 1, 3, 6)
MID = (2, 7)
LATE = (4, 5)


def proj_kernel(spots, with_ctx, has_before, twin, *refs):
    count = len(spots)
    refs = list(refs)
    turned = [[refs.pop(0) for k in range(count)] for p in range(2)]
    arrays = [[refs.pop(0) for k in range(count)] for p in range(2)]
    before = refs.pop(0) if has_before else None
    weights = [refs.pop(0), refs.pop(0)] if with_ctx else None
    proj = refs.pop(0)
    ctx = refs.pop(0) if with_ctx else None
    narrow = refs.pop(0) if twin else None
    rows = arrays[0][0].shape[0] // 2

    if with_ctx:

        @pl.when(pl.program_id(0) == 0)
        def _():
            ctx[...] = jnp.zeros_like(ctx)

    for path in range(2):
        total = before[path, 0] if has_before else None
        for k, spot in enumerate(spots):
            piece = arrays[path][k][...]
            term = dot(turned[path][k][...], piece)
            total = term if total is None else total + term
            if with_ctx:
                part = dot(piece, weights[path][...])
                at = 0
                for span in ctx_rows(path, spot, rows):
                    size = span.stop - span.start
                    ctx[span, :] += part[at : at + size]
                    at += size
        proj[path, 0] = total
        if twin:
            narrow[path, 0] = total.astype(BF16)


def projected(spots, turned, arrays, before=None, w_t=None, twin=False):
    heads, tokens = turned[0].shape
    depth, cols = arrays[0][0].shape
    count = len(spots)
    wide = 256
    steps = cols // wide
    slab = pl.BlockSpec((2, 1, heads, wide), lambda c: (0, c, 0, 0))
    in_specs = [pl.BlockSpec((heads, depth), lambda c, s=spot: (0, s)) for spot in spots] * 2
    in_specs += [pl.BlockSpec((depth, wide), lambda c: (0, c))] * (2 * count)
    operands = [turned[0]] * count + [turned[1]] * count + arrays[0] + arrays[1]
    out_shape = [jax.ShapeDtypeStruct((2, steps, heads, wide), F32)]
    out_specs = [slab]
    if before is not None:
        in_specs.append(slab)
        operands.append(before)
    if w_t is not None:
        in_specs.append(pl.BlockSpec((wide, heads), lambda c: (c, 0)))
        in_specs.append(pl.BlockSpec((wide, heads), lambda c: (c + steps, 0)))
        operands += [w_t, w_t]
        out_shape.append(jax.ShapeDtypeStruct((tokens, heads), F32))
        out_specs.append(pl.BlockSpec((tokens, heads), lambda c: (0, 0)))
    if twin:
        out_shape.append(jax.ShapeDtypeStruct((2, steps, heads, wide), BF16))
        out_specs.append(slab)
    flops = 4 * count * depth * heads * cols * (1 if w_t is None else 2)
    return pl.pallas_call(
        lambda *refs: proj_kernel(spots, w_t is not None, before is not None, twin, *refs),
        out_shape=out_shape,
        grid=(steps,),
        in_specs=in_specs,
        out_specs=out_specs,
        compiler_params=small(20),
        cost_estimate=cost(flops, 4 * count * depth * cols + 8 * heads * cols),
    )(*operands)


def pair_kernel(place, keep, got, own, *sent):
    x, core = place[0], place[1]
    for step in range(SIDE):
        at = (x + step) % SIDE
        path, column = at // 2, 2 * (at % 2) + core
        total = keep[path, column] + got[path, column].astype(F32)
        if step == 0:
            own[...] = total
        else:
            sent[step - 1][...] = total.astype(BF16)


def pair_sum(place, keep, got):
    heads, wide = keep.shape[2:]
    sent = jax.ShapeDtypeStruct((heads, wide), BF16)
    whole = pl.BlockSpec(keep.shape, lambda: (0, 0, 0, 0))
    return pl.pallas_call(
        pair_kernel,
        out_shape=(jax.ShapeDtypeStruct((heads, wide), F32), sent, sent, sent),
        in_specs=[pl.BlockSpec(memory_space=pltpu.SMEM), whole, whole],
        compiler_params=small(16),
        cost_estimate=cost(0, 10 * SIDE * heads * wide),
    )(place, keep, got)


def ctx_kernel(spots, table, before, w_t, *refs):
    count = len(spots)
    arrays, out = refs[: 2 * count], refs[2 * count]
    depth, cols = arrays[0].shape
    rows = depth // 2
    parts = {}
    for path in range(2):
        weights = w_t[path * cols : (path + 1) * cols, :]
        for k, spot in enumerate(spots):
            part = dot(arrays[path * count + k][...], weights)
            at = 0
            for span in ctx_rows(path, spot, rows):
                for start in range(span.start, span.stop, rows):
                    parts.setdefault(start // rows, []).append(part[at : at + rows])
                    at += rows
    for block in range(SIDE * SIDE):
        total = before[block * rows : (block + 1) * rows, :]
        for part in parts.get(block, []):
            total = total + part
        at = pl.multiple_of(table[block] * rows, rows)
        out[pl.ds(at, rows), :] = total.astype(BF16)


def ctx_rest(spots, table, before, w_t, arrays):
    tokens, heads = before.shape
    depth, cols = arrays[0][0].shape
    count = len(spots)
    operands = [before, w_t, *arrays[0], *arrays[1]]
    return pl.pallas_call(
        lambda *refs: ctx_kernel(spots, *refs),
        out_shape=jax.ShapeDtypeStruct((tokens, heads), BF16),
        in_specs=[pl.BlockSpec(memory_space=pltpu.SMEM)]
        + [pl.BlockSpec(a.shape, lambda: (0, 0)) for a in operands],
        compiler_params=small(20),
        cost_estimate=cost(4 * count * depth * heads * cols, 8 * tokens * heads),
    )(table, *operands)


def body(moe_input, out_grad, context, gate_scale, selected, w_gate, w_up, w_down, w_out):
    groups = lax.axis_size("grp")
    inner_count = lax.axis_size("inner")
    devices = groups * inner_count
    tok_rows, width = moe_input.shape
    capacity = selected.shape[1]
    most = 4
    half = width // 2
    inner = lax.axis_index("inner")
    grp = lax.axis_index("grp")
    x, core = grp // 2, grp % 2
    device = grp * inner_count + inner
    both = ("grp", "inner")

    sent, numbers = picked(device, selected, moe_input, out_grad)
    arrived = lax.all_to_all(
        sent.reshape(devices, 2 * most, width), both, split_axis=0, concat_axis=0, tiled=True
    )
    token_table = numbers[:, :most].astype(jnp.int32) - 1

    owner = selected // tok_rows
    my_owner = lax.dynamic_index_in_dim(owner, device, 0, keepdims=False)
    slot_range = jnp.arange(capacity, dtype=jnp.int32)
    same_owner = (my_owner[:, None] == my_owner[None, :]) & (
        slot_range[:, None] > slot_range[None, :]
    )
    ranking = jnp.sum(same_owner.astype(jnp.int32), axis=1)
    position = my_owner * (2 * most) + ranking
    half_of = jnp.arange(2 * capacity, dtype=jnp.int32) // capacity
    spot_of = jnp.tile(position, 2) + half_of * most
    rows_in, scaled, hidden, back_gate, back_up, placed = expert(
        position.reshape(-1, 1),
        gate_scale.reshape(-1, 1),
        spot_of.reshape(1, -1),
        w_gate[0],
        w_up[0],
        w_down[0],
        arrived.reshape(devices * 2 * most, width),
    )
    placed = placed.reshape(devices, 2 * most, half)
    returned = lax.all_to_all(placed, both, split_axis=0, concat_axis=0, tiled=True)

    grad_down = dot(hidden, scaled, ROWS).astype(BF16)
    grad_gate = dot(rows_in, back_gate, ROWS).astype(BF16)
    grad_up = dot(rows_in, back_up, ROWS).astype(BF16)
    steps = jnp.arange(SIDE, dtype=jnp.int32)
    block_ids = ((inner // SIDE + steps) % SIDE)[:, None] * SIDE + (inner + steps) % SIDE
    block_ids = block_ids.reshape(-1)
    turned = turned_context(block_ids, context)
    w_t = w_out.T
    back_table = jnp.concatenate([token_table, token_table], 1).reshape(1, -1)
    place = jnp.stack([x, core])
    returned, grad_down, grad_gate, grad_up, turned, w_t, back_table, place = (
        lax.optimization_barrier(
            (returned, grad_down, grad_gate, grad_up, turned, w_t, back_table, place)
        )
    )
    returned = returned.reshape(devices * 2 * most, half)

    own = sum_back(back_table, returned, out_grad)

    near = [ahead(own[p], 1, p == 1) for p in range(2)]
    last = [ahead(own[p], 3, p == 1) for p in range(2)]
    far = [ahead(own[p], 2, p == 1) for p in range(2)]
    top = join(own[0], near[0], own[1], near[1])
    top_1 = [ahead(top[p], 1, p == 0) for p in range(2)]
    top_3 = [ahead(top[p], 3, p == 0) for p in range(2)]
    low = join(far[0], last[0], far[1], last[1])
    low_1 = [ahead(low[p], 1, p == 0) for p in range(2)]
    low_3 = [ahead(low[p], 3, p == 0) for p in range(2)]
    top_2 = [ahead(top_3[p], 3, p == 0) for p in range(2)]
    low_2 = [ahead(low_1[p], 1, p == 0) for p in range(2)]
    early = [[top[p], low[p], low_1[p], top_3[p]] for p in range(2)]
    proj_sum, ctx_sum = projected(EARLY, turned, early, w_t=w_t)
    mid = [[top_1[p], low_3[p]] for p in range(2)]
    mid, proj_sum, ctx_sum = lax.optimization_barrier((mid, proj_sum, ctx_sum))
    (proj_sum,) = projected(MID, turned, mid, before=proj_sum)
    late = [[top_2[p], low_2[p]] for p in range(2)]
    late, proj_sum = lax.optimization_barrier((late, proj_sum))
    keep, send = projected(LATE, turned, late, before=proj_sum, twin=True)
    got = lax.ppermute(send, "grp", core_pairs())
    own_share, *ahead_shares = pair_sum(place, keep, got)
    shares = [lax.ppermute(ahead_shares[k], "grp", x_pairs(k + 1)) for k in range(3)]
    rest = [[mid[p][0], late[p][0], late[p][1], mid[p][1]] for p in range(2)]
    grad_ctx = ctx_rest((2, 4, 5, 7), block_ids, ctx_sum, w_t, rest)
    proj_share = (own_share + sum(share.astype(F32) for share in shares)).astype(BF16)
    return (grad_gate[None], grad_up[None], grad_down[None], grad_ctx, proj_share)


def solution(mesh):
    rows = P(("grp", "inner"), None)
    expert = P(("grp", "inner"), None, None)
    return jax.shard_map(
        body,
        mesh=mesh,
        in_specs=(
            rows,
            rows,
            P("grp", "inner"),
            rows,
            P(),
            expert,
            expert,
            expert,
            P("inner", None),
        ),
        out_specs=(expert, expert, expert, P("grp", "inner"), P("inner", "grp")),
        check_vma=False,
    )
```

```python
import jax
import jax.numpy as jnp
from jax import lax
from jax.experimental import pallas as pl
from jax.experimental.pallas import tpu as pltpu
from jax.sharding import PartitionSpec as P


F32 = jnp.float32
BF16 = jnp.bfloat16
ROWS = (((0,), (0,)), ((), ()))
LAST = (((1,), (1,)), ((), ()))
SIDE = 4


def dot(left, right, dims=(((1,), (0,)), ((), ()))):
    return lax.dot_general(left, right, dims, preferred_element_type=F32)


def ring_pairs(step, along_z):
    pairs = []
    for z in range(SIDE):
        for y in range(SIDE):
            to = ((z + step) % SIDE) * SIDE + y if along_z else z * SIDE + (y + step) % SIDE
            pairs.append((z * SIDE + y, to))
    return pairs


def core_pairs():
    return [(2 * x + core, 2 * x + 1 - core) for x in range(SIDE) for core in range(2)]


def x_pairs(step):
    return [(2 * x + core, 2 * ((x + step) % SIDE) + core) for x in range(SIDE) for core in range(2)]


def ahead(block, step, along_z):
    return lax.ppermute(block, "inner", ring_pairs(-step, along_z))


def cost(flops, moved):
    return pl.CostEstimate(flops=flops, bytes_accessed=moved, transcendentals=0)


def small(limit):
    return pltpu.CompilerParams(vmem_limit_bytes=limit * 1024 * 1024)


def pick_kernel(device, selected, moe_input, out_grad, out, table_out, rows, parts, sems):
    experts, slots = selected.shape
    tokens, lanes = moe_input.shape[0], table_out.shape[1]
    count, size = parts.shape[:2]
    fetches = [
        pltpu.make_async_copy(source, rows.at[k * tokens : (k + 1) * tokens, :], sems.at[k])
        for k, source in enumerate((moe_input, out_grad))
    ]
    for copy in fetches:
        copy.start()
    rel = selected[...] - device[0] * tokens
    mine = (rel >= 0) & (rel < tokens)
    first = lax.broadcasted_iota(jnp.int32, (slots, slots), 0)
    second = lax.broadcasted_iota(jnp.int32, (slots, slots), 1)
    order = dot(
        jnp.where(mine, 1.0, 0.0).astype(BF16),
        jnp.where(first <= second, 1.0, 0.0).astype(BF16),
    )
    lane = lax.broadcasted_iota(jnp.int32, (experts, lanes), 1)
    number = (rel + 1).astype(F32)
    table = jnp.zeros((experts, lanes), F32)
    for k in range(4):
        hit = mine & (order == k + 1.0)
        value = jnp.sum(jnp.where(hit, number, 0.0), axis=1, keepdims=True)
        table = jnp.where(lane == k, value, table)
        table = jnp.where((lane == k + 4) & (value > 0.0), value + tokens, table)
    table_out[...] = table
    narrow = table.astype(BF16)
    for copy in fetches:
        copy.wait()

    def store(k):
        return pltpu.make_async_copy(
            parts.at[k], out.at[k * size : (k + 1) * size, :], sems.at[2 + k]
        )

    row = lax.broadcasted_iota(jnp.int32, (size, lanes), 0)
    lane = lax.broadcasted_iota(jnp.int32, (size, lanes), 1)
    token = (lax.broadcasted_iota(jnp.int32, (size, 2 * tokens), 1) + 1).astype(F32)
    for k in range(count):
        spread = dot(jnp.where((row + k * size) // 8 == lane, 1.0, 0.0).astype(BF16), narrow)
        pick = jnp.sum(jnp.where(lane == row % 8, spread, 0.0), axis=1, keepdims=True)
        picker = jnp.where(token == pick, 1.0, 0.0).astype(BF16)
        parts[k] = dot(picker, rows[...]).astype(BF16)
        store(k).start()
    for k in range(count):
        store(k).wait()


def picked(device, selected, moe_input, out_grad):
    experts, slots = selected.shape
    tokens, width = moe_input.shape
    count = 4
    hbm = pl.BlockSpec(memory_space=pl.ANY)
    return pl.pallas_call(
        pick_kernel,
        out_shape=(
            jax.ShapeDtypeStruct((8 * experts, width), BF16),
            jax.ShapeDtypeStruct((experts, 128), F32),
        ),
        in_specs=[
            pl.BlockSpec(memory_space=pltpu.SMEM),
            pl.BlockSpec((experts, slots), lambda: (0, 0)),
            hbm,
            hbm,
        ],
        out_specs=(hbm, pl.BlockSpec((experts, 128), lambda: (0, 0))),
        scratch_shapes=[
            pltpu.VMEM((2 * tokens, width), BF16),
            pltpu.VMEM((count, 8 * experts // count, width), BF16),
            pltpu.SemaphoreType.DMA((2 + count,)),
        ],
        compiler_params=small(60),
        cost_estimate=cost(32 * experts * tokens * width, 20 * experts * width),
    )(device.reshape(1), selected, moe_input, out_grad)


def expert_kernel(position, scale, spots, gate_hbm, up_hbm, down_hbm, arrived, *refs):
    results, refs = refs[:6], refs[6:]
    chunks, gate_w, up_w, down_w, gate_sum, up_sum, back_sum, stacked = refs[:8]
    rows_in, scaled_in, hidden, back_gate, back_up, out, in_sem, out_sem = refs[8:]
    count, depth, wide = chunks.shape
    slots = position.shape[0]

    def fetches(k):
        cols = slice(k * wide, (k + 1) * wide)
        pairs = (
            (arrived.at[:, cols], chunks.at[k]),
            (gate_hbm.at[cols, :], gate_w.at[cols, :]),
            (up_hbm.at[cols, :], up_w.at[cols, :]),
            (down_hbm.at[:, cols], down_w.at[:, cols]),
        )
        return [pltpu.make_async_copy(a, b, in_sem.at[k, n]) for n, (a, b) in enumerate(pairs)]

    def store(n, source):
        return pltpu.make_async_copy(source, results[n], out_sem.at[n])

    for k in range(count):
        for copy in fetches(k):
            copy.start()
    spot = lax.broadcasted_iota(jnp.int32, (slots, depth), 1)
    place_in = jnp.where(spot == position[...], 1.0, 0.0).astype(BF16)
    place_grad = jnp.where(spot == position[...] + 4, 1.0, 0.0).astype(BF16)
    place = jnp.concatenate([place_in, place_grad], 0)
    for k in range(count):
        cols = slice(k * wide, (k + 1) * wide)
        waits = fetches(k)
        waits[0].wait()
        chunk = chunks[k]
        found = dot(place, chunk)
        rows = found[:slots].astype(BF16)
        scaled = (found[slots:] * scale[...]).astype(BF16)
        rows_in[:, cols] = rows
        scaled_in[:, cols] = scaled
        for copy in waits[1:]:
            copy.wait()
        terms = (
            (gate_sum, dot(rows, gate_w[cols, :])),
            (up_sum, dot(rows, up_w[cols, :])),
            (back_sum, dot(scaled, down_w[:, cols], LAST)),
        )
        for total, term in terms:
            total[...] = term if k == 0 else total[...] + term
    store(0, rows_in).start()
    store(1, scaled_in).start()
    gate_pre, up_pre, back = gate_sum[...], up_sum[...], back_sum[...]
    sig = jax.nn.sigmoid(gate_pre)
    silu = gate_pre * sig
    back_gate[...] = (back * up_pre * sig * (1.0 + gate_pre * (1.0 - sig))).astype(BF16)
    back_up[...] = (back * silu).astype(BF16)
    hidden[...] = (silu * up_pre).astype(BF16)
    for n, source in ((2, hidden), (3, back_gate), (4, back_up)):
        store(n, source).start()
    half = stacked.shape[1]
    for h in range(2):
        cols = slice(h * half, (h + 1) * half)
        part = dot(back_gate[...], gate_w[cols, :], LAST) + dot(back_up[...], up_w[cols, :], LAST)
        stacked[h * slots : (h + 1) * slots, :] = part.astype(BF16)
    size = out.shape[1]

    def send(k):
        return pltpu.make_async_copy(
            out.at[k], results[5].at[k * size : (k + 1) * size, :], out_sem.at[5 + k]
        )

    for k in range(out.shape[0]):
        row = lax.broadcasted_iota(jnp.int32, (size, spots.shape[1]), 0) + k * size
        unplace = jnp.where(row == spots[...], 1.0, 0.0).astype(BF16)
        out[k] = dot(unplace, stacked[...]).astype(BF16)
        send(k).start()
    for n, source in enumerate((rows_in, scaled_in, hidden, back_gate, back_up)):
        store(n, source).wait()
    for k in range(out.shape[0]):
        send(k).wait()


def expert(position, scale, spots, gate_w, up_w, down_w, arrived):
    slots = position.shape[0]
    depth, width = arrived.shape
    hid = gate_w.shape[1]
    chunks, half = 4, width // 2
    rows, units = (slots, width), (slots, hid)
    shapes = (rows, rows, units, units, units, (depth, half))
    flops = 4 * slots * depth * width + 10 * slots * width * hid + 4 * slots * depth * half
    hbm = pl.BlockSpec(memory_space=pl.ANY)
    return pl.pallas_call(
        expert_kernel,
        out_shape=[jax.ShapeDtypeStruct(shape, BF16) for shape in shapes],
        in_specs=[pl.BlockSpec(a.shape, lambda: (0, 0)) for a in (position, scale, spots)]
        + [hbm] * 4,
        out_specs=[hbm] * 6,
        scratch_shapes=[
            pltpu.VMEM((chunks, depth, width // chunks), BF16),
            pltpu.VMEM((width, hid), BF16),
            pltpu.VMEM((width, hid), BF16),
            pltpu.VMEM((hid, width), BF16),
            pltpu.VMEM(units, F32),
            pltpu.VMEM(units, F32),
            pltpu.VMEM(units, F32),
            pltpu.VMEM((2 * slots, half), BF16),
            pltpu.VMEM(rows, BF16),
            pltpu.VMEM(rows, BF16),
            pltpu.VMEM(units, BF16),
            pltpu.VMEM(units, BF16),
            pltpu.VMEM(units, BF16),
            pltpu.VMEM((4, depth // 4, half), BF16),
            pltpu.SemaphoreType.DMA((chunks, 4)),
            pltpu.SemaphoreType.DMA((9,)),
        ],
        compiler_params=small(60),
        cost_estimate=cost(flops, 2 * depth * width + 6 * width * hid),
    )(position, scale, spots, gate_w, up_w, down_w, arrived)


def sum_kernel(table, back, own, out_a, out_b, chunks, mine, sems):
    count, rows, wide = chunks.shape
    tokens = mine.shape[0]

    def fetch(k):
        return pltpu.make_async_copy(
            back.at[:, k * wide : (k + 1) * wide], chunks.at[k], sems.at[k]
        )

    for k in range(count):
        fetch(k).start()
    first = pltpu.make_async_copy(own, mine, sems.at[count])
    first.start()
    token = lax.broadcasted_iota(jnp.int32, (tokens, rows), 0)
    row = lax.broadcasted_iota(jnp.int32, (tokens, rows), 1)
    hit = token == table[...]
    low = (row // 4) % 2 == 0
    add_a = jnp.where(hit & low, 1.0, 0.0).astype(BF16)
    add_b = jnp.where(hit & ~low, 1.0, 0.0).astype(BF16)
    first.wait()
    for k in range(count):
        fetch(k).wait()
        cols = slice(k * wide, (k + 1) * wide)
        after = slice((count + k) * wide, (count + k + 1) * wide)
        chunk = chunks[k]
        out_a[:, cols] = (mine[:, cols].astype(F32) + dot(add_a, chunk)).astype(BF16)
        out_b[:, cols] = (mine[:, after].astype(F32) + dot(add_b, chunk)).astype(BF16)


def sum_back(table, back, own):
    rows, cols = back.shape
    tokens = own.shape[0]
    count = 4
    out = jax.ShapeDtypeStruct((tokens, cols), BF16)
    hbm = pl.BlockSpec(memory_space=pltpu.HBM)
    return pl.pallas_call(
        sum_kernel,
        out_shape=(out, out),
        in_specs=[pl.BlockSpec((1, rows), lambda: (0, 0)), hbm, hbm],
        scratch_shapes=[
            pltpu.VMEM((count, rows, cols // count), BF16),
            pltpu.VMEM(own.shape, BF16),
            pltpu.SemaphoreType.DMA((count + 1,)),
        ],
        compiler_params=small(16),
        cost_estimate=cost(4 * tokens * rows * cols, 2 * rows * cols),
    )(table, back, own)


def join_kernel(a0, a1, b0, b1, a, b):
    rows = a0.shape[0]
    a[:rows, :] = a0[...]
    a[rows:, :] = a1[...]
    b[:rows, :] = b0[...]
    b[rows:, :] = b1[...]


def join(a0, a1, b0, b1):
    rows, cols = a0.shape
    out = jax.ShapeDtypeStruct((2 * rows, cols), BF16)
    return pl.pallas_call(
        join_kernel,
        out_shape=(out, out),
        compiler_params=small(16),
        cost_estimate=cost(0, 16 * rows * cols),
    )(a0, a1, b0, b1)


def turn_kernel(table, block, out_a, out_b):
    turned = block[...].T
    out_a[...] = turned
    out_b[...] = turned


def turned_context(table, context):
    tokens, heads = context.shape
    rows = tokens // 16
    out = jax.ShapeDtypeStruct((heads, tokens), BF16)
    return pl.pallas_call(
        turn_kernel,
        out_shape=(out, out),
        grid_spec=pltpu.PrefetchScalarGridSpec(
            num_scalar_prefetch=1,
            grid=(16,),
            in_specs=[pl.BlockSpec((rows, heads), lambda j, t: (t[j], 0))],
            out_specs=(
                pl.BlockSpec((heads, rows), lambda j, t: (0, j)),
                pl.BlockSpec((heads, rows), lambda j, t: (0, (j % SIDE) * SIDE + j // SIDE)),
            ),
        ),
        compiler_params=small(16),
        cost_estimate=cost(0, 6 * tokens * heads),
    )(table, context)


def ctx_rows(path, spot, rows):
    off, top = spot // 2, 2 * (spot % 2)
    if path == 0:
        return [slice((off * SIDE + top) * rows, (off * SIDE + top + 2) * rows)]
    return [slice(((top + k) * SIDE + off) * rows, ((top + k) * SIDE + off + 1) * rows) for k in range(2)]


EARLY = (0, 1, 2, 6)
MID = (3, 7)
LATE = (4, 5)


def proj_kernel(spots, with_ctx, has_before, twin, *refs):
    count = len(spots)
    refs = list(refs)
    turned = [[refs.pop(0) for _ in range(count)] for _ in range(2)]
    arrays = [[refs.pop(0) for _ in range(count)] for _ in range(2)]
    before = refs.pop(0) if has_before else None
    weights = [refs.pop(0), refs.pop(0)] if with_ctx else None
    proj = refs.pop(0)
    ctx = refs.pop(0) if with_ctx else None
    narrow = refs.pop(0) if twin else None
    rows = arrays[0][0].shape[0] // 2

    if with_ctx:

        @pl.when(pl.program_id(0) == 0)
        def _():
            ctx[...] = jnp.zeros_like(ctx)

    for path in range(2):
        total = before[path, 0] if has_before else None
        for k, spot in enumerate(spots):
            piece = arrays[path][k][...]
            term = dot(turned[path][k][...], piece)
            total = term if total is None else total + term
            if with_ctx:
                part = dot(piece, weights[path][...])
                at = 0
                for span in ctx_rows(path, spot, rows):
                    size = span.stop - span.start
                    ctx[span, :] += part[at : at + size]
                    at += size
        proj[path, 0] = total
        if twin:
            narrow[path, 0] = total.astype(BF16)


def projected(spots, turned, arrays, before=None, w_t=None, twin=False):
    heads, tokens = turned[0].shape
    depth, cols = arrays[0][0].shape
    count = len(spots)
    wide = 256
    steps = cols // wide
    slab = pl.BlockSpec((2, 1, heads, wide), lambda c: (0, c, 0, 0))
    in_specs = [pl.BlockSpec((heads, depth), lambda c, s=spot: (0, s)) for spot in spots] * 2
    in_specs += [pl.BlockSpec((depth, wide), lambda c: (0, c))] * (2 * count)
    operands = [turned[0]] * count + [turned[1]] * count + arrays[0] + arrays[1]
    out_shape = [jax.ShapeDtypeStruct((2, steps, heads, wide), F32)]
    out_specs = [slab]
    if before is not None:
        in_specs.append(slab)
        operands.append(before)
    if w_t is not None:
        in_specs.append(pl.BlockSpec((wide, heads), lambda c: (c, 0)))
        in_specs.append(pl.BlockSpec((wide, heads), lambda c: (c + steps, 0)))
        operands += [w_t, w_t]
        out_shape.append(jax.ShapeDtypeStruct((tokens, heads), F32))
        out_specs.append(pl.BlockSpec((tokens, heads), lambda c: (0, 0)))
    if twin:
        out_shape.append(jax.ShapeDtypeStruct((2, steps, heads, wide), BF16))
        out_specs.append(slab)
    flops = 4 * count * depth * heads * cols * (1 if w_t is None else 2)
    return pl.pallas_call(
        lambda *refs: proj_kernel(spots, w_t is not None, before is not None, twin, *refs),
        out_shape=out_shape,
        grid=(steps,),
        in_specs=in_specs,
        out_specs=out_specs,
        compiler_params=small(20),
        cost_estimate=cost(flops, 4 * count * depth * cols + 8 * heads * cols),
    )(*operands)


def pair_kernel(place, keep, got, own, *sent):
    x, core = place[0], place[1]
    for step in range(SIDE):
        at = (x + step) % SIDE
        path, column = at // 2, 2 * (at % 2) + core
        total = keep[path, column] + got[path, column].astype(F32)
        if step == 0:
            own[...] = total
        else:
            sent[step - 1][...] = total.astype(BF16)


def pair_sum(place, keep, got):
    heads, wide = keep.shape[2:]
    sent = jax.ShapeDtypeStruct((heads, wide), BF16)
    whole = pl.BlockSpec(keep.shape, lambda: (0, 0, 0, 0))
    return pl.pallas_call(
        pair_kernel,
        out_shape=(jax.ShapeDtypeStruct((heads, wide), F32), sent, sent, sent),
        in_specs=[pl.BlockSpec(memory_space=pltpu.SMEM), whole, whole],
        compiler_params=small(16),
        cost_estimate=cost(0, 10 * SIDE * heads * wide),
    )(place, keep, got)


def ctx_kernel(spots, table, before, w_t, *refs):
    count = len(spots)
    arrays, out = refs[: 2 * count], refs[2 * count]
    depth, cols = arrays[0].shape
    rows = depth // 2
    parts = {}
    for path in range(2):
        weights = w_t[path * cols : (path + 1) * cols, :]
        for k, spot in enumerate(spots):
            part = dot(arrays[path * count + k][...], weights)
            at = 0
            for span in ctx_rows(path, spot, rows):
                for start in range(span.start, span.stop, rows):
                    parts.setdefault(start // rows, []).append(part[at : at + rows])
                    at += rows
    for block in range(SIDE * SIDE):
        total = before[block * rows : (block + 1) * rows, :]
        for part in parts.get(block, []):
            total = total + part
        at = pl.multiple_of(table[block] * rows, rows)
        out[pl.ds(at, rows), :] = total.astype(BF16)


def ctx_rest(spots, table, before, w_t, arrays):
    tokens, heads = before.shape
    depth, cols = arrays[0][0].shape
    count = len(spots)
    operands = [before, w_t, *arrays[0], *arrays[1]]
    return pl.pallas_call(
        lambda *refs: ctx_kernel(spots, *refs),
        out_shape=jax.ShapeDtypeStruct((tokens, heads), BF16),
        in_specs=[pl.BlockSpec(memory_space=pltpu.SMEM)]
        + [pl.BlockSpec(a.shape, lambda: (0, 0)) for a in operands],
        compiler_params=small(20),
        cost_estimate=cost(4 * count * depth * heads * cols, 8 * tokens * heads),
    )(table, *operands)


def body(moe_input, out_grad, context, gate_scale, selected, w_gate, w_up, w_down, w_out):
    groups = lax.axis_size("grp")
    inner_count = lax.axis_size("inner")
    devices = groups * inner_count
    tok_rows, width = moe_input.shape
    capacity = selected.shape[1]
    most = 4
    half = width // 2
    inner = lax.axis_index("inner")
    grp = lax.axis_index("grp")
    x, core = grp // 2, grp % 2
    device = grp * inner_count + inner
    both = ("grp", "inner")

    sent, numbers = picked(device, selected, moe_input, out_grad)
    arrived = lax.all_to_all(
        sent.reshape(devices, 2 * most, width), both, split_axis=0, concat_axis=0, tiled=True
    )
    token_table = numbers[:, :most].astype(jnp.int32) - 1

    owner = selected // tok_rows
    my_owner = lax.dynamic_index_in_dim(owner, device, 0, keepdims=False)
    slot_range = jnp.arange(capacity, dtype=jnp.int32)
    same_owner = (my_owner[:, None] == my_owner[None, :]) & (
        slot_range[:, None] > slot_range[None, :]
    )
    ranking = jnp.sum(same_owner.astype(jnp.int32), axis=1)
    position = my_owner * (2 * most) + ranking
    half_of = jnp.arange(2 * capacity, dtype=jnp.int32) // capacity
    spot_of = jnp.tile(position, 2) + half_of * most
    rows_in, scaled, hidden, back_gate, back_up, placed = expert(
        position.reshape(-1, 1),
        gate_scale.reshape(-1, 1),
        spot_of.reshape(1, -1),
        w_gate[0],
        w_up[0],
        w_down[0],
        arrived.reshape(devices * 2 * most, width),
    )
    placed = placed.reshape(devices, 2 * most, half)
    returned = lax.all_to_all(placed, both, split_axis=0, concat_axis=0, tiled=True)

    grad_down = dot(hidden, scaled, ROWS).astype(BF16)
    grad_gate = dot(rows_in, back_gate, ROWS).astype(BF16)
    grad_up = dot(rows_in, back_up, ROWS).astype(BF16)
    steps = jnp.arange(SIDE, dtype=jnp.int32)
    block_ids = ((inner // SIDE + steps) % SIDE)[:, None] * SIDE + (inner + steps) % SIDE
    block_ids = block_ids.reshape(-1)
    turned = turned_context(block_ids, context)
    w_t = w_out.T
    back_table = jnp.concatenate([token_table, token_table], 1).reshape(1, -1)
    place = jnp.stack([x, core])
    returned, grad_down, grad_gate, grad_up, turned, w_t, back_table, place = (
        lax.optimization_barrier(
            (returned, grad_down, grad_gate, grad_up, turned, w_t, back_table, place)
        )
    )
    returned = returned.reshape(devices * 2 * most, half)

    own = sum_back(back_table, returned, out_grad)

    def step(blocks, count, z_path):
        out = []
        for p in range(2):
            out.append(ahead(blocks[p], count, p == z_path))
        return out

    near = step(own, 1, 1)
    last = step(own, 3, 1)
    far = step(own, 2, 1)
    top = join(own[0], near[0], own[1], near[1])
    top_3 = step(top, 3, 0)
    top_1 = step(top, 1, 0)
    low = join(far[0], last[0], far[1], last[1])
    low_1 = step(low, 1, 0)
    low_3 = step(low, 3, 0)
    top_2 = step(top_3, 3, 0)
    low_2 = step(low_1, 1, 0)
    early = [[top[p], low[p], top_1[p], top_3[p]] for p in range(2)]
    proj_sum, ctx_sum = projected(EARLY, turned, early, w_t=w_t)
    mid = [[low_1[p], low_3[p]] for p in range(2)]
    mid, proj_sum, ctx_sum = lax.optimization_barrier((mid, proj_sum, ctx_sum))
    (proj_sum,) = projected(MID, turned, mid, before=proj_sum)
    late = [[top_2[p], low_2[p]] for p in range(2)]
    late, proj_sum = lax.optimization_barrier((late, proj_sum))
    keep, send = projected(LATE, turned, late, before=proj_sum, twin=True)
    got = lax.ppermute(send, "grp", core_pairs())
    own_share, *ahead_shares = pair_sum(place, keep, got)
    shares = [lax.ppermute(ahead_shares[k], "grp", x_pairs(k + 1)) for k in range(3)]
    rest = [[mid[p][0], late[p][0], late[p][1], mid[p][1]] for p in range(2)]
    grad_ctx = ctx_rest((3, 4, 5, 7), block_ids, ctx_sum, w_t, rest)
    proj_share = (own_share + sum(share.astype(F32) for share in shares)).astype(BF16)
    return (grad_gate[None], grad_up[None], grad_down[None], grad_ctx, proj_share)


def solution(mesh):
    rows = P(("grp", "inner"), None)
    expert = P(("grp", "inner"), None, None)
    return jax.shard_map(
        body,
        mesh=mesh,
        in_specs=(
            rows,
            rows,
            P("grp", "inner"),
            rows,
            P(),
            expert,
            expert,
            expert,
            P("inner", None),
        ),
        out_specs=(expert, expert, expert, P("grp", "inner"), P("inner", "grp")),
        check_vma=False,
    )
```

```python
import jax
import jax.numpy as jnp
from jax import lax
from jax.experimental import pallas as pl
from jax.experimental.pallas import tpu as pltpu
from jax.sharding import PartitionSpec as P


F32 = jnp.float32
BF16 = jnp.bfloat16
ROWS = (((0,), (0,)), ((), ()))
LAST = (((1,), (1,)), ((), ()))
SIDE = 4


def dot(left, right, dims=(((1,), (0,)), ((), ()))):
    return lax.dot_general(left, right, dims, preferred_element_type=F32)


def ring_pairs(step, along_z):
    pairs = []
    for z in range(SIDE):
        for y in range(SIDE):
            to = ((z + step) % SIDE) * SIDE + y if along_z else z * SIDE + (y + step) % SIDE
            pairs.append((z * SIDE + y, to))
    return pairs


def core_pairs():
    return [(2 * x + core, 2 * x + 1 - core) for x in range(SIDE) for core in range(2)]


def x_pairs(step):
    return [(2 * x + core, 2 * ((x + step) % SIDE) + core) for x in range(SIDE) for core in range(2)]


def ahead(block, step, along_z):
    return lax.ppermute(block, "inner", ring_pairs(-step, along_z))


def cost(flops, moved):
    return pl.CostEstimate(flops=flops, bytes_accessed=moved, transcendentals=0)


def small(limit):
    return pltpu.CompilerParams(vmem_limit_bytes=limit * 1024 * 1024)


def pick_kernel(device, selected, moe_input, out_grad, out, table_out, picker, rows):
    step = pl.program_id(0)
    experts, slots = selected.shape
    tokens, lanes = moe_input.shape[0], table_out.shape[1]

    @pl.when(step == 0)
    def _():
        rel = selected[...] - device[0] * tokens
        mine = (rel >= 0) & (rel < tokens)
        first = lax.broadcasted_iota(jnp.int32, (slots, slots), 0)
        second = lax.broadcasted_iota(jnp.int32, (slots, slots), 1)
        order = dot(
            jnp.where(mine, 1.0, 0.0).astype(BF16),
            jnp.where(first <= second, 1.0, 0.0).astype(BF16),
        )
        lane = lax.broadcasted_iota(jnp.int32, (experts, lanes), 1)
        number = (rel + 1).astype(F32)
        table = jnp.zeros((experts, lanes), F32)
        for k in range(4):
            hit = mine & (order == k + 1.0)
            value = jnp.sum(jnp.where(hit, number, 0.0), axis=1, keepdims=True)
            table = jnp.where(lane == k, value, table)
            table = jnp.where((lane == k + 4) & (value > 0.0), value + tokens, table)
        table_out[...] = table
        row = lax.broadcasted_iota(jnp.int32, (8 * experts, lanes), 0)
        lane = lax.broadcasted_iota(jnp.int32, (8 * experts, lanes), 1)
        spread = dot(jnp.where(row // 8 == lane, 1.0, 0.0).astype(BF16), table.astype(BF16))
        pick = jnp.sum(jnp.where(lane == row % 8, spread, 0.0), axis=1, keepdims=True)
        token = lax.broadcasted_iota(jnp.int32, picker.shape, 1) + 1
        picker[...] = jnp.where(token.astype(F32) == pick, 1.0, 0.0).astype(BF16)
        rows[:tokens, :] = moe_input[...]
        rows[tokens:, :] = out_grad[...]

    size = out.shape[0]
    part = picker[pl.ds(pl.multiple_of(step * size, size), size), :]
    out[...] = dot(part, rows[...]).astype(BF16)


def picked(device, selected, moe_input, out_grad):
    experts, slots = selected.shape
    tokens, width = moe_input.shape
    size = 256
    whole = pl.BlockSpec((tokens, width), lambda c: (0, 0))
    return pl.pallas_call(
        pick_kernel,
        out_shape=(
            jax.ShapeDtypeStruct((8 * experts, width), BF16),
            jax.ShapeDtypeStruct((experts, 128), F32),
        ),
        grid=(8 * experts // size,),
        in_specs=[
            pl.BlockSpec(memory_space=pltpu.SMEM),
            pl.BlockSpec((experts, slots), lambda c: (0, 0)),
            whole,
            whole,
        ],
        out_specs=(
            pl.BlockSpec((size, width), lambda c: (c, 0)),
            pl.BlockSpec((experts, 128), lambda c: (0, 0)),
        ),
        scratch_shapes=[
            pltpu.VMEM((8 * experts, 2 * tokens), BF16),
            pltpu.VMEM((2 * tokens, width), BF16),
        ],
        compiler_params=small(60),
        cost_estimate=cost(32 * experts * tokens * width, 20 * experts * width),
    )(device.reshape(1), selected, moe_input, out_grad)


def expert_kernel(position, scale, spots, gate_hbm, up_hbm, down_hbm, arrived, *refs):
    results, refs = refs[:6], refs[6:]
    chunks, gate_w, up_w, down_w, gate_sum, up_sum, back_sum, stacked = refs[:8]
    rows_in, scaled_in, hidden, back_gate, back_up, out, in_sem, out_sem = refs[8:]
    count, depth, wide = chunks.shape
    slots = position.shape[0]

    def fetches(k):
        cols = slice(k * wide, (k + 1) * wide)
        pairs = (
            (arrived.at[:, cols], chunks.at[k]),
            (gate_hbm.at[cols, :], gate_w.at[cols, :]),
            (up_hbm.at[cols, :], up_w.at[cols, :]),
            (down_hbm.at[:, cols], down_w.at[:, cols]),
        )
        return [pltpu.make_async_copy(a, b, in_sem.at[k, n]) for n, (a, b) in enumerate(pairs)]

    def store(n, source):
        return pltpu.make_async_copy(source, results[n], out_sem.at[n])

    ahead_by = 2
    for k in range(ahead_by):
        for copy in fetches(k):
            copy.start()
    spot = lax.broadcasted_iota(jnp.int32, (slots, depth), 1)
    place_in = jnp.where(spot == position[...], 1.0, 0.0).astype(BF16)
    place_grad = jnp.where(spot == position[...] + 4, 1.0, 0.0).astype(BF16)
    for k in range(count):
        cols = slice(k * wide, (k + 1) * wide)
        waits = fetches(k)
        waits[0].wait()
        chunk = chunks[k]
        rows = dot(place_in, chunk).astype(BF16)
        scaled = (dot(place_grad, chunk) * scale[...]).astype(BF16)
        rows_in[:, cols] = rows
        scaled_in[:, cols] = scaled
        for copy in waits[1:]:
            copy.wait()
        if k + ahead_by < count:
            for copy in fetches(k + ahead_by):
                copy.start()
        terms = (
            (gate_sum, dot(rows, gate_w[cols, :])),
            (up_sum, dot(rows, up_w[cols, :])),
            (back_sum, dot(scaled, down_w[:, cols], LAST)),
        )
        for total, term in terms:
            total[...] = term if k == 0 else total[...] + term
    store(0, rows_in).start()
    store(1, scaled_in).start()
    gate_pre, up_pre, back = gate_sum[...], up_sum[...], back_sum[...]
    sig = jax.nn.sigmoid(gate_pre)
    silu = gate_pre * sig
    back_gate[...] = (back * up_pre * sig * (1.0 + gate_pre * (1.0 - sig))).astype(BF16)
    back_up[...] = (back * silu).astype(BF16)
    hidden[...] = (silu * up_pre).astype(BF16)
    for n, source in ((2, hidden), (3, back_gate), (4, back_up)):
        store(n, source).start()
    half = stacked.shape[1]
    for h in range(2):
        cols = slice(h * half, (h + 1) * half)
        part = dot(back_gate[...], gate_w[cols, :], LAST) + dot(back_up[...], up_w[cols, :], LAST)
        stacked[h * slots : (h + 1) * slots, :] = part.astype(BF16)
    size = out.shape[1]

    def send(k):
        return pltpu.make_async_copy(
            out.at[k], results[5].at[k * size : (k + 1) * size, :], out_sem.at[5 + k]
        )

    for k in range(out.shape[0]):
        row = lax.broadcasted_iota(jnp.int32, (size, spots.shape[1]), 0) + k * size
        unplace = jnp.where(row == spots[...], 1.0, 0.0).astype(BF16)
        out[k] = dot(unplace, stacked[...]).astype(BF16)
        send(k).start()
    for n, source in enumerate((rows_in, scaled_in, hidden, back_gate, back_up)):
        store(n, source).wait()
    for k in range(out.shape[0]):
        send(k).wait()


def expert(position, scale, spots, gate_w, up_w, down_w, arrived):
    slots = position.shape[0]
    depth, width = arrived.shape
    hid = gate_w.shape[1]
    chunks, half = 4, width // 2
    rows, units = (slots, width), (slots, hid)
    shapes = (rows, rows, units, units, units, (depth, half))
    flops = 4 * slots * depth * width + 10 * slots * width * hid + 4 * slots * depth * half
    hbm = pl.BlockSpec(memory_space=pl.ANY)
    return pl.pallas_call(
        expert_kernel,
        out_shape=[jax.ShapeDtypeStruct(shape, BF16) for shape in shapes],
        in_specs=[pl.BlockSpec(a.shape, lambda: (0, 0)) for a in (position, scale, spots)]
        + [hbm] * 4,
        out_specs=[hbm] * 6,
        scratch_shapes=[
            pltpu.VMEM((chunks, depth, width // chunks), BF16),
            pltpu.VMEM((width, hid), BF16),
            pltpu.VMEM((width, hid), BF16),
            pltpu.VMEM((hid, width), BF16),
            pltpu.VMEM(units, F32),
            pltpu.VMEM(units, F32),
            pltpu.VMEM(units, F32),
            pltpu.VMEM((2 * slots, half), BF16),
            pltpu.VMEM(rows, BF16),
            pltpu.VMEM(rows, BF16),
            pltpu.VMEM(units, BF16),
            pltpu.VMEM(units, BF16),
            pltpu.VMEM(units, BF16),
            pltpu.VMEM((4, depth // 4, half), BF16),
            pltpu.SemaphoreType.DMA((chunks, 4)),
            pltpu.SemaphoreType.DMA((9,)),
        ],
        compiler_params=small(60),
        cost_estimate=cost(flops, 2 * depth * width + 6 * width * hid),
    )(position, scale, spots, gate_w, up_w, down_w, arrived)


def sum_kernel(table, back, own, out_a, out_b, chunks, mine, sems):
    count, rows, wide = chunks.shape
    tokens = mine.shape[0]

    def fetch(k):
        return pltpu.make_async_copy(
            back.at[:, k * wide : (k + 1) * wide], chunks.at[k], sems.at[k]
        )

    for k in range(count):
        fetch(k).start()
    first = pltpu.make_async_copy(own, mine, sems.at[count])
    first.start()
    token = lax.broadcasted_iota(jnp.int32, (tokens, rows), 0)
    row = lax.broadcasted_iota(jnp.int32, (tokens, rows), 1)
    hit = token == table[...]
    low = (row // 4) % 2 == 0
    add_a = jnp.where(hit & low, 1.0, 0.0).astype(BF16)
    add_b = jnp.where(hit & ~low, 1.0, 0.0).astype(BF16)
    first.wait()
    for k in range(count):
        fetch(k).wait()
        cols = slice(k * wide, (k + 1) * wide)
        after = slice((count + k) * wide, (count + k + 1) * wide)
        chunk = chunks[k]
        out_a[:, cols] = (mine[:, cols].astype(F32) + dot(add_a, chunk)).astype(BF16)
        out_b[:, cols] = (mine[:, after].astype(F32) + dot(add_b, chunk)).astype(BF16)


def sum_back(table, back, own):
    rows, cols = back.shape
    tokens = own.shape[0]
    count = 4
    out = jax.ShapeDtypeStruct((tokens, cols), BF16)
    hbm = pl.BlockSpec(memory_space=pltpu.HBM)
    return pl.pallas_call(
        sum_kernel,
        out_shape=(out, out),
        in_specs=[pl.BlockSpec((1, rows), lambda: (0, 0)), hbm, hbm],
        scratch_shapes=[
            pltpu.VMEM((count, rows, cols // count), BF16),
            pltpu.VMEM(own.shape, BF16),
            pltpu.SemaphoreType.DMA((count + 1,)),
        ],
        compiler_params=small(16),
        cost_estimate=cost(4 * tokens * rows * cols, 2 * rows * cols),
    )(table, back, own)


def join_kernel(a0, a1, b0, b1, a, b):
    rows = a0.shape[0]
    a[:rows, :] = a0[...]
    a[rows:, :] = a1[...]
    b[:rows, :] = b0[...]
    b[rows:, :] = b1[...]


def join(a0, a1, b0, b1):
    rows, cols = a0.shape
    out = jax.ShapeDtypeStruct((2 * rows, cols), BF16)
    return pl.pallas_call(
        join_kernel,
        out_shape=(out, out),
        compiler_params=small(16),
        cost_estimate=cost(0, 16 * rows * cols),
    )(a0, a1, b0, b1)


def turn_kernel(table, block, out_a, out_b):
    turned = block[...].T
    out_a[...] = turned
    out_b[...] = turned


def turned_context(table, context):
    tokens, heads = context.shape
    rows = tokens // 16
    out = jax.ShapeDtypeStruct((heads, tokens), BF16)
    return pl.pallas_call(
        turn_kernel,
        out_shape=(out, out),
        grid_spec=pltpu.PrefetchScalarGridSpec(
            num_scalar_prefetch=1,
            grid=(16,),
            in_specs=[pl.BlockSpec((rows, heads), lambda j, t: (t[j], 0))],
            out_specs=(
                pl.BlockSpec((heads, rows), lambda j, t: (0, j)),
                pl.BlockSpec((heads, rows), lambda j, t: (0, (j % SIDE) * SIDE + j // SIDE)),
            ),
        ),
        compiler_params=small(16),
        cost_estimate=cost(0, 6 * tokens * heads),
    )(table, context)


def ctx_rows(path, spot, rows):
    off, top = spot // 2, 2 * (spot % 2)
    if path == 0:
        return [slice((off * SIDE + top) * rows, (off * SIDE + top + 2) * rows)]
    return [slice(((top + k) * SIDE + off) * rows, ((top + k) * SIDE + off + 1) * rows) for k in range(2)]


EARLY = (0, 1, 2, 6)
MID = (3, 7)
LATE = (4, 5)


def proj_kernel(spots, with_ctx, has_before, twin, *refs):
    count = len(spots)
    refs = list(refs)
    turned = [[refs.pop(0) for _ in range(count)] for _ in range(2)]
    arrays = [[refs.pop(0) for _ in range(count)] for _ in range(2)]
    before = refs.pop(0) if has_before else None
    weights = [refs.pop(0), refs.pop(0)] if with_ctx else None
    proj = refs.pop(0)
    ctx = refs.pop(0) if with_ctx else None
    narrow = refs.pop(0) if twin else None
    rows = arrays[0][0].shape[0] // 2

    if with_ctx:

        @pl.when(pl.program_id(0) == 0)
        def _():
            ctx[...] = jnp.zeros_like(ctx)

    for path in range(2):
        total = before[path, 0] if has_before else None
        for k, spot in enumerate(spots):
            piece = arrays[path][k][...]
            term = dot(turned[path][k][...], piece)
            total = term if total is None else total + term
            if with_ctx:
                part = dot(piece, weights[path][...])
                at = 0
                for span in ctx_rows(path, spot, rows):
                    size = span.stop - span.start
                    ctx[span, :] += part[at : at + size]
                    at += size
        proj[path, 0] = total
        if twin:
            narrow[path, 0] = total.astype(BF16)


def projected(spots, turned, arrays, before=None, w_t=None, twin=False):
    heads, tokens = turned[0].shape
    depth, cols = arrays[0][0].shape
    count = len(spots)
    wide = 256
    steps = cols // wide
    slab = pl.BlockSpec((2, 1, heads, wide), lambda c: (0, c, 0, 0))
    in_specs = [pl.BlockSpec((heads, depth), lambda c, s=spot: (0, s)) for spot in spots] * 2
    in_specs += [pl.BlockSpec((depth, wide), lambda c: (0, c))] * (2 * count)
    operands = [turned[0]] * count + [turned[1]] * count + arrays[0] + arrays[1]
    out_shape = [jax.ShapeDtypeStruct((2, steps, heads, wide), F32)]
    out_specs = [slab]
    if before is not None:
        in_specs.append(slab)
        operands.append(before)
    if w_t is not None:
        in_specs.append(pl.BlockSpec((wide, heads), lambda c: (c, 0)))
        in_specs.append(pl.BlockSpec((wide, heads), lambda c: (c + steps, 0)))
        operands += [w_t, w_t]
        out_shape.append(jax.ShapeDtypeStruct((tokens, heads), F32))
        out_specs.append(pl.BlockSpec((tokens, heads), lambda c: (0, 0)))
    if twin:
        out_shape.append(jax.ShapeDtypeStruct((2, steps, heads, wide), BF16))
        out_specs.append(slab)
    flops = 4 * count * depth * heads * cols * (1 if w_t is None else 2)
    return pl.pallas_call(
        lambda *refs: proj_kernel(spots, w_t is not None, before is not None, twin, *refs),
        out_shape=out_shape,
        grid=(steps,),
        in_specs=in_specs,
        out_specs=out_specs,
        compiler_params=small(20),
        cost_estimate=cost(flops, 4 * count * depth * cols + 8 * heads * cols),
    )(*operands)


def pair_kernel(place, keep, got, own, *sent):
    x, core = place[0], place[1]
    for step in range(SIDE):
        at = (x + step) % SIDE
        path, column = at // 2, 2 * (at % 2) + core
        total = keep[path, column] + got[path, column].astype(F32)
        if step == 0:
            own[...] = total
        else:
            sent[step - 1][...] = total.astype(BF16)


def pair_sum(place, keep, got):
    heads, wide = keep.shape[2:]
    sent = jax.ShapeDtypeStruct((heads, wide), BF16)
    whole = pl.BlockSpec(keep.shape, lambda: (0, 0, 0, 0))
    return pl.pallas_call(
        pair_kernel,
        out_shape=(jax.ShapeDtypeStruct((heads, wide), F32), sent, sent, sent),
        in_specs=[pl.BlockSpec(memory_space=pltpu.SMEM), whole, whole],
        compiler_params=small(16),
        cost_estimate=cost(0, 10 * SIDE * heads * wide),
    )(place, keep, got)


def ctx_kernel(spots, table, before, w_t, *refs):
    count = len(spots)
    arrays, out = refs[: 2 * count], refs[2 * count]
    depth, cols = arrays[0].shape
    rows = depth // 2
    parts = {}
    for path in range(2):
        weights = w_t[path * cols : (path + 1) * cols, :]
        for k, spot in enumerate(spots):
            part = dot(arrays[path * count + k][...], weights)
            at = 0
            for span in ctx_rows(path, spot, rows):
                for start in range(span.start, span.stop, rows):
                    parts.setdefault(start // rows, []).append(part[at : at + rows])
                    at += rows
    for block in range(SIDE * SIDE):
        total = before[block * rows : (block + 1) * rows, :]
        for part in parts.get(block, []):
            total = total + part
        at = pl.multiple_of(table[block] * rows, rows)
        out[pl.ds(at, rows), :] = total.astype(BF16)


def ctx_rest(spots, table, before, w_t, arrays):
    tokens, heads = before.shape
    depth, cols = arrays[0][0].shape
    count = len(spots)
    operands = [before, w_t, *arrays[0], *arrays[1]]
    return pl.pallas_call(
        lambda *refs: ctx_kernel(spots, *refs),
        out_shape=jax.ShapeDtypeStruct((tokens, heads), BF16),
        in_specs=[pl.BlockSpec(memory_space=pltpu.SMEM)]
        + [pl.BlockSpec(a.shape, lambda: (0, 0)) for a in operands],
        compiler_params=small(20),
        cost_estimate=cost(4 * count * depth * heads * cols, 8 * tokens * heads),
    )(table, *operands)


def body(moe_input, out_grad, context, gate_scale, selected, w_gate, w_up, w_down, w_out):
    groups = lax.axis_size("grp")
    inner_count = lax.axis_size("inner")
    devices = groups * inner_count
    tok_rows, width = moe_input.shape
    capacity = selected.shape[1]
    most = 4
    half = width // 2
    inner = lax.axis_index("inner")
    grp = lax.axis_index("grp")
    x, core = grp // 2, grp % 2
    device = grp * inner_count + inner
    both = ("grp", "inner")

    sent, numbers = picked(device, selected, moe_input, out_grad)
    arrived = lax.all_to_all(
        sent.reshape(devices, 2 * most, width), both, split_axis=0, concat_axis=0, tiled=True
    )
    token_table = numbers[:, :most].astype(jnp.int32) - 1

    owner = selected // tok_rows
    my_owner = lax.dynamic_index_in_dim(owner, device, 0, keepdims=False)
    slot_range = jnp.arange(capacity, dtype=jnp.int32)
    same_owner = (my_owner[:, None] == my_owner[None, :]) & (
        slot_range[:, None] > slot_range[None, :]
    )
    ranking = jnp.sum(same_owner.astype(jnp.int32), axis=1)
    position = my_owner * (2 * most) + ranking
    half_of = jnp.arange(2 * capacity, dtype=jnp.int32) // capacity
    spot_of = jnp.tile(position, 2) + half_of * most
    rows_in, scaled, hidden, back_gate, back_up, placed = expert(
        position.reshape(-1, 1),
        gate_scale.reshape(-1, 1),
        spot_of.reshape(1, -1),
        w_gate[0],
        w_up[0],
        w_down[0],
        arrived.reshape(devices * 2 * most, width),
    )
    placed = placed.reshape(devices, 2 * most, half)
    returned = lax.all_to_all(placed, both, split_axis=0, concat_axis=0, tiled=True)

    grad_down = dot(hidden, scaled, ROWS).astype(BF16)
    grad_gate = dot(rows_in, back_gate, ROWS).astype(BF16)
    grad_up = dot(rows_in, back_up, ROWS).astype(BF16)
    steps = jnp.arange(SIDE, dtype=jnp.int32)
    block_ids = ((inner // SIDE + steps) % SIDE)[:, None] * SIDE + (inner + steps) % SIDE
    block_ids = block_ids.reshape(-1)
    turned = turned_context(block_ids, context)
    w_t = w_out.T
    back_table = jnp.concatenate([token_table, token_table], 1).reshape(1, -1)
    place = jnp.stack([x, core])
    returned, grad_down, grad_gate, grad_up, turned, w_t, back_table, place = (
        lax.optimization_barrier(
            (returned, grad_down, grad_gate, grad_up, turned, w_t, back_table, place)
        )
    )
    returned = returned.reshape(devices * 2 * most, half)

    own = sum_back(back_table, returned, out_grad)

    def step(blocks, count, z_path):
        out = []
        for p in range(2):
            out.append(ahead(blocks[p], count, p == z_path))
        return out

    near = step(own, 1, 1)
    last = step(own, 3, 1)
    far = step(own, 2, 1)
    top = join(own[0], near[0], own[1], near[1])
    top_3 = step(top, 3, 0)
    top_1 = step(top, 1, 0)
    low = join(far[0], last[0], far[1], last[1])
    low_1 = step(low, 1, 0)
    low_3 = step(low, 3, 0)
    top_2 = step(top_3, 3, 0)
    low_2 = step(low_1, 1, 0)
    early = [[top[p], low[p], top_1[p], top_3[p]] for p in range(2)]
    proj_sum, ctx_sum = projected(EARLY, turned, early, w_t=w_t)
    mid = [[low_1[p], low_3[p]] for p in range(2)]
    mid, proj_sum, ctx_sum = lax.optimization_barrier((mid, proj_sum, ctx_sum))
    (proj_sum,) = projected(MID, turned, mid, before=proj_sum)
    late = [[top_2[p], low_2[p]] for p in range(2)]
    late, proj_sum = lax.optimization_barrier((late, proj_sum))
    keep, send = projected(LATE, turned, late, before=proj_sum, twin=True)
    got = lax.ppermute(send, "grp", core_pairs())
    own_share, *ahead_shares = pair_sum(place, keep, got)
    shares = [lax.ppermute(ahead_shares[k], "grp", x_pairs(k + 1)) for k in range(3)]
    rest = [[mid[p][0], late[p][0], late[p][1], mid[p][1]] for p in range(2)]
    grad_ctx = ctx_rest((3, 4, 5, 7), block_ids, ctx_sum, w_t, rest)
    proj_share = (own_share + sum(share.astype(F32) for share in shares)).astype(BF16)
    return (grad_gate[None], grad_up[None], grad_down[None], grad_ctx, proj_share)


def solution(mesh):
    rows = P(("grp", "inner"), None)
    expert = P(("grp", "inner"), None, None)
    return jax.shard_map(
        body,
        mesh=mesh,
        in_specs=(
            rows,
            rows,
            P("grp", "inner"),
            rows,
            P(),
            expert,
            expert,
            expert,
            P("inner", None),
        ),
        out_specs=(expert, expert, expert, P("grp", "inner"), P("inner", "grp")),
        check_vma=False,
    )
```

```python
import jax
import jax.numpy as jnp
from jax import lax
from jax.experimental import pallas as pl
from jax.experimental.pallas import tpu as pltpu
from jax.sharding import PartitionSpec as P


F32 = jnp.float32
BF16 = jnp.bfloat16
ROWS = (((0,), (0,)), ((), ()))
LAST = (((1,), (1,)), ((), ()))
SIDE = 4


def dot(left, right, dims=(((1,), (0,)), ((), ()))):
    return lax.dot_general(left, right, dims, preferred_element_type=F32)


def ring_pairs(step, along_z):
    pairs = []
    for z in range(SIDE):
        for y in range(SIDE):
            to = ((z + step) % SIDE) * SIDE + y if along_z else z * SIDE + (y + step) % SIDE
            pairs.append((z * SIDE + y, to))
    return pairs


def core_pairs():
    return [(2 * x + core, 2 * x + 1 - core) for x in range(SIDE) for core in range(2)]


def x_pairs(step):
    return [(2 * x + core, 2 * ((x + step) % SIDE) + core) for x in range(SIDE) for core in range(2)]


def ahead(block, step, along_z):
    return lax.ppermute(block, "inner", ring_pairs(-step, along_z))


def cost(flops, moved):
    return pl.CostEstimate(flops=flops, bytes_accessed=moved, transcendentals=0)


def small(limit):
    return pltpu.CompilerParams(vmem_limit_bytes=limit * 1024 * 1024)


def pick_kernel(device, selected, moe_input, out_grad, out, table_out, picker, rows):
    step = pl.program_id(0)
    experts, slots = selected.shape
    tokens, lanes = moe_input.shape[0], table_out.shape[1]

    @pl.when(step == 0)
    def _():
        rel = selected[...] - device[0] * tokens
        mine = (rel >= 0) & (rel < tokens)
        first = lax.broadcasted_iota(jnp.int32, (slots, slots), 0)
        second = lax.broadcasted_iota(jnp.int32, (slots, slots), 1)
        order = dot(
            jnp.where(mine, 1.0, 0.0).astype(BF16),
            jnp.where(first <= second, 1.0, 0.0).astype(BF16),
        )
        lane = lax.broadcasted_iota(jnp.int32, (experts, lanes), 1)
        number = (rel + 1).astype(F32)
        table = jnp.zeros((experts, lanes), F32)
        for k in range(4):
            hit = mine & (order == k + 1.0)
            value = jnp.sum(jnp.where(hit, number, 0.0), axis=1, keepdims=True)
            table = jnp.where(lane == k, value, table)
            table = jnp.where((lane == k + 4) & (value > 0.0), value + tokens, table)
        table_out[...] = table
        row = lax.broadcasted_iota(jnp.int32, (8 * experts, lanes), 0)
        lane = lax.broadcasted_iota(jnp.int32, (8 * experts, lanes), 1)
        spread = dot(jnp.where(row // 8 == lane, 1.0, 0.0).astype(BF16), table.astype(BF16))
        pick = jnp.sum(jnp.where(lane == row % 8, spread, 0.0), axis=1, keepdims=True)
        token = lax.broadcasted_iota(jnp.int32, picker.shape, 1) + 1
        picker[...] = jnp.where(token.astype(F32) == pick, 1.0, 0.0).astype(BF16)
        rows[:tokens, :] = moe_input[...]
        rows[tokens:, :] = out_grad[...]

    size = out.shape[0]
    part = picker[pl.ds(pl.multiple_of(step * size, size), size), :]
    out[...] = dot(part, rows[...]).astype(BF16)


def picked(device, selected, moe_input, out_grad):
    experts, slots = selected.shape
    tokens, width = moe_input.shape
    size = 256
    whole = pl.BlockSpec((tokens, width), lambda c: (0, 0))
    return pl.pallas_call(
        pick_kernel,
        out_shape=(
            jax.ShapeDtypeStruct((8 * experts, width), BF16),
            jax.ShapeDtypeStruct((experts, 128), F32),
        ),
        grid=(8 * experts // size,),
        in_specs=[
            pl.BlockSpec(memory_space=pltpu.SMEM),
            pl.BlockSpec((experts, slots), lambda c: (0, 0)),
            whole,
            whole,
        ],
        out_specs=(
            pl.BlockSpec((size, width), lambda c: (c, 0)),
            pl.BlockSpec((experts, 128), lambda c: (0, 0)),
        ),
        scratch_shapes=[
            pltpu.VMEM((8 * experts, 2 * tokens), BF16),
            pltpu.VMEM((2 * tokens, width), BF16),
        ],
        compiler_params=small(60),
        cost_estimate=cost(32 * experts * tokens * width, 20 * experts * width),
    )(device.reshape(1), selected, moe_input, out_grad)


def expert_kernel(position, scale, spots, gate_hbm, up_hbm, down_hbm, arrived, *refs):
    results, refs = refs[:6], refs[6:]
    chunks, gate_w, up_w, down_w, gate_sum, up_sum, back_sum, stacked = refs[:8]
    rows_in, scaled_in, hidden, back_gate, back_up, out, in_sem, out_sem = refs[8:]
    count, depth, wide = chunks.shape
    slots = position.shape[0]

    def fetches(k):
        cols = slice(k * wide, (k + 1) * wide)
        pairs = (
            (arrived.at[:, cols], chunks.at[k]),
            (gate_hbm.at[cols, :], gate_w.at[cols, :]),
            (up_hbm.at[cols, :], up_w.at[cols, :]),
            (down_hbm.at[:, cols], down_w.at[:, cols]),
        )
        return [pltpu.make_async_copy(a, b, in_sem.at[k, n]) for n, (a, b) in enumerate(pairs)]

    def store(n, source):
        return pltpu.make_async_copy(source, results[n], out_sem.at[n])

    for k in range(count):
        for copy in fetches(k):
            copy.start()
    spot = lax.broadcasted_iota(jnp.int32, (slots, depth), 1)
    place_in = jnp.where(spot == position[...], 1.0, 0.0).astype(BF16)
    place_grad = jnp.where(spot == position[...] + 4, 1.0, 0.0).astype(BF16)
    for k in range(count):
        cols = slice(k * wide, (k + 1) * wide)
        waits = fetches(k)
        waits[0].wait()
        chunk = chunks[k]
        rows = dot(place_in, chunk).astype(BF16)
        scaled = (dot(place_grad, chunk) * scale[...]).astype(BF16)
        rows_in[:, cols] = rows
        scaled_in[:, cols] = scaled
        for copy in waits[1:]:
            copy.wait()
        terms = (
            (gate_sum, dot(rows, gate_w[cols, :])),
            (up_sum, dot(rows, up_w[cols, :])),
            (back_sum, dot(scaled, down_w[:, cols], LAST)),
        )
        for total, term in terms:
            total[...] = term if k == 0 else total[...] + term
    store(0, rows_in).start()
    store(1, scaled_in).start()
    gate_pre, up_pre, back = gate_sum[...], up_sum[...], back_sum[...]
    sig = jax.nn.sigmoid(gate_pre)
    silu = gate_pre * sig
    back_gate[...] = (back * up_pre * sig * (1.0 + gate_pre * (1.0 - sig))).astype(BF16)
    back_up[...] = (back * silu).astype(BF16)
    hidden[...] = (silu * up_pre).astype(BF16)
    for n, source in ((2, hidden), (3, back_gate), (4, back_up)):
        store(n, source).start()
    half = stacked.shape[1]
    for h in range(2):
        cols = slice(h * half, (h + 1) * half)
        part = dot(back_gate[...], gate_w[cols, :], LAST) + dot(back_up[...], up_w[cols, :], LAST)
        stacked[h * slots : (h + 1) * slots, :] = part.astype(BF16)
    size = out.shape[1]

    def send(k):
        return pltpu.make_async_copy(
            out.at[k], results[5].at[k * size : (k + 1) * size, :], out_sem.at[5 + k]
        )

    for k in range(out.shape[0]):
        row = lax.broadcasted_iota(jnp.int32, (size, spots.shape[1]), 0) + k * size
        unplace = jnp.where(row == spots[...], 1.0, 0.0).astype(BF16)
        out[k] = dot(unplace, stacked[...]).astype(BF16)
        send(k).start()
    for n, source in enumerate((rows_in, scaled_in, hidden, back_gate, back_up)):
        store(n, source).wait()
    for k in range(out.shape[0]):
        send(k).wait()


def expert(position, scale, spots, gate_w, up_w, down_w, arrived):
    slots = position.shape[0]
    depth, width = arrived.shape
    hid = gate_w.shape[1]
    chunks, half = 4, width // 2
    rows, units = (slots, width), (slots, hid)
    shapes = (rows, rows, units, units, units, (depth, half))
    flops = 4 * slots * depth * width + 10 * slots * width * hid + 4 * slots * depth * half
    hbm = pl.BlockSpec(memory_space=pl.ANY)
    return pl.pallas_call(
        expert_kernel,
        out_shape=[jax.ShapeDtypeStruct(shape, BF16) for shape in shapes],
        in_specs=[pl.BlockSpec(a.shape, lambda: (0, 0)) for a in (position, scale, spots)]
        + [hbm] * 4,
        out_specs=[hbm] * 6,
        scratch_shapes=[
            pltpu.VMEM((chunks, depth, width // chunks), BF16),
            pltpu.VMEM((width, hid), BF16),
            pltpu.VMEM((width, hid), BF16),
            pltpu.VMEM((hid, width), BF16),
            pltpu.VMEM(units, F32),
            pltpu.VMEM(units, F32),
            pltpu.VMEM(units, F32),
            pltpu.VMEM((2 * slots, half), BF16),
            pltpu.VMEM(rows, BF16),
            pltpu.VMEM(rows, BF16),
            pltpu.VMEM(units, BF16),
            pltpu.VMEM(units, BF16),
            pltpu.VMEM(units, BF16),
            pltpu.VMEM((4, depth // 4, half), BF16),
            pltpu.SemaphoreType.DMA((chunks, 4)),
            pltpu.SemaphoreType.DMA((9,)),
        ],
        compiler_params=small(60),
        cost_estimate=cost(flops, 2 * depth * width + 6 * width * hid),
    )(position, scale, spots, gate_w, up_w, down_w, arrived)


def sum_kernel(table, back, own, out_a, out_b, chunks, mine, sems):
    count, rows, wide = chunks.shape
    tokens = mine.shape[0]

    def fetch(k):
        return pltpu.make_async_copy(
            back.at[:, k * wide : (k + 1) * wide], chunks.at[k], sems.at[k]
        )

    for k in range(count):
        fetch(k).start()
    first = pltpu.make_async_copy(own, mine, sems.at[count])
    first.start()
    token = lax.broadcasted_iota(jnp.int32, (tokens, rows), 0)
    row = lax.broadcasted_iota(jnp.int32, (tokens, rows), 1)
    hit = token == table[...]
    low = (row // 4) % 2 == 0
    add_a = jnp.where(hit & low, 1.0, 0.0).astype(BF16)
    add_b = jnp.where(hit & ~low, 1.0, 0.0).astype(BF16)
    first.wait()
    for k in range(count):
        fetch(k).wait()
        cols = slice(k * wide, (k + 1) * wide)
        after = slice((count + k) * wide, (count + k + 1) * wide)
        chunk = chunks[k]
        out_a[:, cols] = (mine[:, cols].astype(F32) + dot(add_a, chunk)).astype(BF16)
        out_b[:, cols] = (mine[:, after].astype(F32) + dot(add_b, chunk)).astype(BF16)


def sum_back(table, back, own):
    rows, cols = back.shape
    tokens = own.shape[0]
    count = 4
    out = jax.ShapeDtypeStruct((tokens, cols), BF16)
    hbm = pl.BlockSpec(memory_space=pltpu.HBM)
    return pl.pallas_call(
        sum_kernel,
        out_shape=(out, out),
        in_specs=[pl.BlockSpec((1, rows), lambda: (0, 0)), hbm, hbm],
        scratch_shapes=[
            pltpu.VMEM((count, rows, cols // count), BF16),
            pltpu.VMEM(own.shape, BF16),
            pltpu.SemaphoreType.DMA((count + 1,)),
        ],
        compiler_params=small(59),
        cost_estimate=cost(4 * tokens * rows * cols, 2 * rows * cols),
    )(table, back, own)


def join_kernel(a0, a1, b0, b1, a, b):
    rows = a0.shape[0]
    a[:rows, :] = a0[...]
    a[rows:, :] = a1[...]
    b[:rows, :] = b0[...]
    b[rows:, :] = b1[...]


def join(a0, a1, b0, b1):
    rows, cols = a0.shape
    out = jax.ShapeDtypeStruct((2 * rows, cols), BF16)
    return pl.pallas_call(
        join_kernel,
        out_shape=(out, out),
        compiler_params=small(16),
        cost_estimate=cost(0, 16 * rows * cols),
    )(a0, a1, b0, b1)


def turn_kernel(table, block, out_a, out_b):
    turned = block[...].T
    out_a[...] = turned
    out_b[...] = turned


def turned_context(table, context):
    tokens, heads = context.shape
    rows = tokens // 16
    out = jax.ShapeDtypeStruct((heads, tokens), BF16)
    return pl.pallas_call(
        turn_kernel,
        out_shape=(out, out),
        grid_spec=pltpu.PrefetchScalarGridSpec(
            num_scalar_prefetch=1,
            grid=(16,),
            in_specs=[pl.BlockSpec((rows, heads), lambda j, t: (t[j], 0))],
            out_specs=(
                pl.BlockSpec((heads, rows), lambda j, t: (0, j)),
                pl.BlockSpec((heads, rows), lambda j, t: (0, (j % SIDE) * SIDE + j // SIDE)),
            ),
        ),
        compiler_params=small(16),
        cost_estimate=cost(0, 6 * tokens * heads),
    )(table, context)


def ctx_rows(path, spot, rows):
    off, top = spot // 2, 2 * (spot % 2)
    if path == 0:
        return [slice((off * SIDE + top) * rows, (off * SIDE + top + 2) * rows)]
    return [slice(((top + k) * SIDE + off) * rows, ((top + k) * SIDE + off + 1) * rows) for k in range(2)]


EARLY = (0, 1, 2, 6)
MID = (3, 7)
LATE = (4, 5)


def proj_kernel(spots, with_ctx, has_before, twin, *refs):
    count = len(spots)
    refs = list(refs)
    turned = [[refs.pop(0) for _ in range(count)] for _ in range(2)]
    arrays = [[refs.pop(0) for _ in range(count)] for _ in range(2)]
    before = refs.pop(0) if has_before else None
    weights = [refs.pop(0), refs.pop(0)] if with_ctx else None
    proj = refs.pop(0)
    ctx = refs.pop(0) if with_ctx else None
    narrow = refs.pop(0) if twin else None
    rows = arrays[0][0].shape[0] // 2

    if with_ctx:

        @pl.when(pl.program_id(0) == 0)
        def _():
            ctx[...] = jnp.zeros_like(ctx)

    for path in range(2):
        total = before[path, 0] if has_before else None
        for k, spot in enumerate(spots):
            piece = arrays[path][k][...]
            term = dot(turned[path][k][...], piece)
            total = term if total is None else total + term
            if with_ctx:
                part = dot(piece, weights[path][...])
                at = 0
                for span in ctx_rows(path, spot, rows):
                    size = span.stop - span.start
                    ctx[span, :] += part[at : at + size]
                    at += size
        proj[path, 0] = total
        if twin:
            narrow[path, 0] = total.astype(BF16)


def projected(spots, turned, arrays, before=None, w_t=None, twin=False):
    heads, tokens = turned[0].shape
    depth, cols = arrays[0][0].shape
    count = len(spots)
    wide = 256
    steps = cols // wide
    slab = pl.BlockSpec((2, 1, heads, wide), lambda c: (0, c, 0, 0))
    in_specs = [pl.BlockSpec((heads, depth), lambda c, s=spot: (0, s)) for spot in spots] * 2
    in_specs += [pl.BlockSpec((depth, wide), lambda c: (0, c))] * (2 * count)
    operands = [turned[0]] * count + [turned[1]] * count + arrays[0] + arrays[1]
    out_shape = [jax.ShapeDtypeStruct((2, steps, heads, wide), F32)]
    out_specs = [slab]
    if before is not None:
        in_specs.append(slab)
        operands.append(before)
    if w_t is not None:
        in_specs.append(pl.BlockSpec((wide, heads), lambda c: (c, 0)))
        in_specs.append(pl.BlockSpec((wide, heads), lambda c: (c + steps, 0)))
        operands += [w_t, w_t]
        out_shape.append(jax.ShapeDtypeStruct((tokens, heads), F32))
        out_specs.append(pl.BlockSpec((tokens, heads), lambda c: (0, 0)))
    if twin:
        out_shape.append(jax.ShapeDtypeStruct((2, steps, heads, wide), BF16))
        out_specs.append(slab)
    flops = 4 * count * depth * heads * cols * (1 if w_t is None else 2)
    return pl.pallas_call(
        lambda *refs: proj_kernel(spots, w_t is not None, before is not None, twin, *refs),
        out_shape=out_shape,
        grid=(steps,),
        in_specs=in_specs,
        out_specs=out_specs,
        compiler_params=small(20),
        cost_estimate=cost(flops, 4 * count * depth * cols + 8 * heads * cols),
    )(*operands)


def pair_kernel(place, keep, got, own, *sent):
    x, core = place[0], place[1]
    for step in range(SIDE):
        at = (x + step) % SIDE
        path, column = at // 2, 2 * (at % 2) + core
        total = keep[path, column] + got[path, column].astype(F32)
        if step == 0:
            own[...] = total
        else:
            sent[step - 1][...] = total.astype(BF16)


def pair_sum(place, keep, got):
    heads, wide = keep.shape[2:]
    sent = jax.ShapeDtypeStruct((heads, wide), BF16)
    whole = pl.BlockSpec(keep.shape, lambda: (0, 0, 0, 0))
    return pl.pallas_call(
        pair_kernel,
        out_shape=(jax.ShapeDtypeStruct((heads, wide), F32), sent, sent, sent),
        in_specs=[pl.BlockSpec(memory_space=pltpu.SMEM), whole, whole],
        compiler_params=small(16),
        cost_estimate=cost(0, 10 * SIDE * heads * wide),
    )(place, keep, got)


def ctx_kernel(spots, table, before, w_t, *refs):
    count = len(spots)
    arrays, out = refs[: 2 * count], refs[2 * count]
    depth, cols = arrays[0].shape
    rows = depth // 2
    parts = {}
    for path in range(2):
        weights = w_t[path * cols : (path + 1) * cols, :]
        for k, spot in enumerate(spots):
            part = dot(arrays[path * count + k][...], weights)
            at = 0
            for span in ctx_rows(path, spot, rows):
                for start in range(span.start, span.stop, rows):
                    parts.setdefault(start // rows, []).append(part[at : at + rows])
                    at += rows
    for block in range(SIDE * SIDE):
        total = before[block * rows : (block + 1) * rows, :]
        for part in parts.get(block, []):
            total = total + part
        at = pl.multiple_of(table[block] * rows, rows)
        out[pl.ds(at, rows), :] = total.astype(BF16)


def ctx_rest(spots, table, before, w_t, arrays):
    tokens, heads = before.shape
    depth, cols = arrays[0][0].shape
    count = len(spots)
    operands = [before, w_t, *arrays[0], *arrays[1]]
    return pl.pallas_call(
        lambda *refs: ctx_kernel(spots, *refs),
        out_shape=jax.ShapeDtypeStruct((tokens, heads), BF16),
        in_specs=[pl.BlockSpec(memory_space=pltpu.SMEM)]
        + [pl.BlockSpec(a.shape, lambda: (0, 0)) for a in operands],
        compiler_params=small(20),
        cost_estimate=cost(4 * count * depth * heads * cols, 8 * tokens * heads),
    )(table, *operands)


def body(moe_input, out_grad, context, gate_scale, selected, w_gate, w_up, w_down, w_out):
    groups = lax.axis_size("grp")
    inner_count = lax.axis_size("inner")
    devices = groups * inner_count
    tok_rows, width = moe_input.shape
    capacity = selected.shape[1]
    most = 4
    half = width // 2
    inner = lax.axis_index("inner")
    grp = lax.axis_index("grp")
    x, core = grp // 2, grp % 2
    device = grp * inner_count + inner
    both = ("grp", "inner")

    sent, numbers = picked(device, selected, moe_input, out_grad)
    arrived = lax.all_to_all(
        sent.reshape(devices, 2 * most, width), both, split_axis=0, concat_axis=0, tiled=True
    )
    token_table = numbers[:, :most].astype(jnp.int32) - 1

    owner = selected // tok_rows
    my_owner = lax.dynamic_index_in_dim(owner, device, 0, keepdims=False)
    slot_range = jnp.arange(capacity, dtype=jnp.int32)
    same_owner = (my_owner[:, None] == my_owner[None, :]) & (
        slot_range[:, None] > slot_range[None, :]
    )
    ranking = jnp.sum(same_owner.astype(jnp.int32), axis=1)
    position = my_owner * (2 * most) + ranking
    half_of = jnp.arange(2 * capacity, dtype=jnp.int32) // capacity
    spot_of = jnp.tile(position, 2) + half_of * most
    rows_in, scaled, hidden, back_gate, back_up, placed = expert(
        position.reshape(-1, 1),
        gate_scale.reshape(-1, 1),
        spot_of.reshape(1, -1),
        w_gate[0],
        w_up[0],
        w_down[0],
        arrived.reshape(devices * 2 * most, width),
    )
    placed = placed.reshape(devices, 2 * most, half)
    returned = lax.all_to_all(placed, both, split_axis=0, concat_axis=0, tiled=True)

    grad_down = dot(hidden, scaled, ROWS).astype(BF16)
    grad_gate = dot(rows_in, back_gate, ROWS).astype(BF16)
    grad_up = dot(rows_in, back_up, ROWS).astype(BF16)
    steps = jnp.arange(SIDE, dtype=jnp.int32)
    block_ids = ((inner // SIDE + steps) % SIDE)[:, None] * SIDE + (inner + steps) % SIDE
    block_ids = block_ids.reshape(-1)
    turned = turned_context(block_ids, context)
    w_t = w_out.T
    back_table = jnp.concatenate([token_table, token_table], 1).reshape(1, -1)
    place = jnp.stack([x, core])
    returned, grad_down, grad_gate, grad_up, turned, w_t, back_table, place = (
        lax.optimization_barrier(
            (returned, grad_down, grad_gate, grad_up, turned, w_t, back_table, place)
        )
    )
    returned = returned.reshape(devices * 2 * most, half)

    own = sum_back(back_table, returned, out_grad)

    def step(blocks, count, z_path):
        out = []
        for p in range(2):
            out.append(ahead(blocks[p], count, p == z_path))
        return out

    near = step(own, 1, 1)
    last = step(own, 3, 1)
    far = step(own, 2, 1)
    top = join(own[0], near[0], own[1], near[1])
    top_3 = step(top, 3, 0)
    top_1 = step(top, 1, 0)
    low = join(far[0], last[0], far[1], last[1])
    low_1 = step(low, 1, 0)
    low_3 = step(low, 3, 0)
    top_2 = step(top_3, 3, 0)
    low_2 = step(low_1, 1, 0)
    early = [[top[p], low[p], top_1[p], top_3[p]] for p in range(2)]
    proj_sum, ctx_sum = projected(EARLY, turned, early, w_t=w_t)
    mid = [[low_1[p], low_3[p]] for p in range(2)]
    mid, proj_sum, ctx_sum = lax.optimization_barrier((mid, proj_sum, ctx_sum))
    (proj_sum,) = projected(MID, turned, mid, before=proj_sum)
    late = [[top_2[p], low_2[p]] for p in range(2)]
    late, proj_sum = lax.optimization_barrier((late, proj_sum))
    keep, send = projected(LATE, turned, late, before=proj_sum, twin=True)
    got = lax.ppermute(send, "grp", core_pairs())
    own_share, *ahead_shares = pair_sum(place, keep, got)
    shares = [lax.ppermute(ahead_shares[k], "grp", x_pairs(k + 1)) for k in range(3)]
    rest = [[mid[p][0], late[p][0], late[p][1], mid[p][1]] for p in range(2)]
    grad_ctx = ctx_rest((3, 4, 5, 7), block_ids, ctx_sum, w_t, rest)
    proj_share = (own_share + sum(share.astype(F32) for share in shares)).astype(BF16)
    return (grad_gate[None], grad_up[None], grad_down[None], grad_ctx, proj_share)


def solution(mesh):
    rows = P(("grp", "inner"), None)
    expert = P(("grp", "inner"), None, None)
    return jax.shard_map(
        body,
        mesh=mesh,
        in_specs=(
            rows,
            rows,
            P("grp", "inner"),
            rows,
            P(),
            expert,
            expert,
            expert,
            P("inner", None),
        ),
        out_specs=(expert, expert, expert, P("grp", "inner"), P("inner", "grp")),
        check_vma=False,
    )
```
